32 devices in a mesh: dp: 8 (over z, y), head: 4 (over x, core).
Axes of the slice: x: 2, y: 2, z: 4, core: 2. Of those that a mesh axis runs over, the one named last changes fastest.
Arguments:
- source: bfloat16 [2, 16384, 512], P(None, ('dp', 'head')), may hold values from -6 to 6
- target: bfloat16 [2, 16384, 512], P(None, ('dp', 'head')), may hold values from -6 to 6
- cotangent: bfloat16 [2, 16384, 512], P(None, ('dp', 'head')), may hold values from -6 to 6
- short_lengths: int32 [2, 64], P(None, 'dp'), may hold values from 128 to 256, as said below
- long_lengths: int32 [2, 16], P(None, 'dp'), may hold values from 512 to 1024, as said below
- attn_weights: bfloat16 [12, 512, 512], replicated, may hold values from -0.375 to 0.375
- up_weights: bfloat16 [2, 512, 2048], replicated, may hold values from -0.25 to 0.25
- down_weights: bfloat16 [2, 2048, 512], replicated, may hold values from -0.125 to 0.125
- norm_gains: float32 [5, 512], replicated, may hold values from 0.25 to 1.75
- norm_shifts: float32 [5, 512], replicated, may hold values from -1 to 1
Outputs:
- decoded: bfloat16 [2, 16384, 512], P(None, ('dp', 'head'))
- grad_source: float32 [2, 16384, 512], P(None, ('dp', 'head'))
- grad_target: float32 [2, 16384, 512], P(None, ('dp', 'head'))
- grad_attn: float32 [12, 512, 512], P(None, ('dp', 'head'))
- grad_up: float32 [2, 512, 2048], P(None, ('dp', 'head'))
- grad_down: float32 [2, 2048, 512], P(None, ('dp', 'head'))
- grad_gains: float32 [5, 512], P(None, ('dp', 'head'))
- grad_shifts: float32 [5, 512], P(None, ('dp', 'head'))
The draws below stay inside these ranges and needn't reach their ends.
Inputs may be any that keep to these rules, and one draw needn't show every extreme that they name: `short_lengths`: row 0 holds the source lengths and row 1 the target lengths of the 64 slots, in slot order; each row has a slot of exactly 256. `long_lengths`: row 0 holds the source lengths and row 1 the target lengths of the 16 slots, in slot order; each row has a slot of exactly 1024.
All inputs are finite; a program needn't handle non-finite values.
Results may differ from the reference program's by a relative error of at most 0.025.
The reference program's roundings to bfloat16 on the way count: a program that leaves them out, or rounds other values in their place, can miss the bound.
Values may be sent and summed in bfloat16 or wider, within the bound.
A program may use at most 320 MiB of HBM per device.

```python
import math
import jax
import jax.numpy as jnp
from jax import lax

D = 512
HEADS = 8
FF = 2048
SHORT = 256
LONG = 1024
TOKENS = 16384
SEQ_SHORT = 64
SEQ_LONG = 16


def draw_slot_lengths(seed_key, count, slot_size):
    first_key, second_key = jax.random.split(seed_key)
    values = jax.random.randint(first_key, (2, count), slot_size // 2, slot_size + 1)
    spots = jax.random.randint(second_key, (2,), 0, count)
    return values.at[jnp.arange(2), spots].set(slot_size).astype(jnp.int32)


def draw_short_lengths(key, part):
    return draw_slot_lengths(jax.random.fold_in(key, 11), SEQ_SHORT, SHORT)


def draw_long_lengths(key, part):
    return draw_slot_lengths(jax.random.fold_in(key, 23), SEQ_LONG, LONG)


def raised(entries, own_key, source, target, parts, factor):
    owner, partner = [(jnp.arange(entries.shape[dim]) // (entries.shape[dim] // parts)).reshape([-1 if axis == dim else 1 for axis in range(entries.ndim)]) for dim in (source, target)]
    chosen = jax.random.permutation(own_key, parts)[partner]
    strong = (owner == chosen) | (owner == (partner + parts // 2) % parts)
    return jnp.where(strong, factor * entries, entries)


def level_of(rng, extent, cuts, low, top_value):
    level, own = 1.0, jax.random.fold_in(rng, 6)
    for dim, parts in cuts:
        draws = jnp.exp(jax.random.uniform(jax.random.fold_in(own, dim), (parts,), jnp.float32, low / len(cuts), top_value / len(cuts)))
        level = level * jnp.repeat(draws, extent[dim] // parts).reshape([-1 if axis == dim else 1 for axis in range(len(extent))])
    return level


def normal_values(stream_key, dims, deviation, bound, shards=(), kind=jnp.bfloat16):
    values = jax.random.normal(stream_key, dims, jnp.float32) * deviation
    if len(shards) > 0:
        values = level_of(stream_key, dims, shards, -0.22, 0.18) * values
    return jnp.clip(values, min=-bound, max=bound).astype(kind)


def noise_with(rng, dims, deviation, reach, cuts, heavy, kind=jnp.bfloat16):
    values = deviation * jax.random.normal(rng, dims, jnp.float32)
    if cuts:
        values = values * level_of(rng, dims, cuts, -0.22, 0.18)
    return jnp.clip(raised(values, jax.random.fold_in(rng, 3), *heavy), -reach, reach).astype(kind)


def setup_inputs(seed: int = 0) -> dict:
    streams_of = jax.random.split(jax.random.key(seed), 11)
    source = noise_with(streams_of[0], (2, TOKENS, D), 1.0, 6.0, ((1, 32),), (1, 2, 32, 2.75))
    target = noise_with(streams_of[1], (2, TOKENS, D), 1.0, 6.0, ((1, 32),), (1, 2, 32, 2.75))
    cotangent = normal_values(streams_of[2], (2, TOKENS, D), 1.0, 6.0, ((1, 32),))
    short_lengths = draw_short_lengths(jax.random.fold_in(streams_of[10], 71), 0)
    long_lengths = draw_long_lengths(jax.random.fold_in(streams_of[10], 71), 0)
    attn_weights = normal_values(streams_of[5], (12, D, D), (D // 2) ** -0.5, 0.375)
    up_weights = normal_values(streams_of[6], (2, D, FF), D ** -0.5, 0.25)
    down_weights = normal_values(streams_of[7], (2, FF, D), FF ** -0.5, 0.125)
    norm_gains = jnp.clip(1.0 + 0.15 * jax.random.normal(streams_of[8], (5, D), jnp.float32), 0.25, 1.75)
    norm_shifts = normal_values(streams_of[9], (5, D), 0.2, 1.0, (), jnp.float32)
    return {"source": source, "target": target, "cotangent": cotangent, "short_lengths": short_lengths, "long_lengths": long_lengths, "attn_weights": attn_weights, "up_weights": up_weights, "down_weights": down_weights, "norm_gains": norm_gains, "norm_shifts": norm_shifts}


@jax.custom_vjp
def low(v):
    return lax.optimization_barrier(v.astype(jnp.bfloat16)).astype(jnp.float32)

@jax.custom_vjp
def low_back(v):
    return v

def low_keep(v):
    return (low(v), None)

def low_pass(kept, grad):
    return (grad,)

def back_keep(v):
    return (v, None)

def back_low(kept, grad):
    return (low(grad),)
low.defvjp(low_keep, low_pass)
low_back.defvjp(back_keep, back_low)
EPSILON = 1e-05
MASKED = -1e+30
PRECISE = lax.Precision.HIGHEST

def layer_norm(residual, gain, shift):
    average = lax.optimization_barrier(jnp.mean(residual, axis=-1, keepdims=True))
    centered = residual - average
    variance = lax.optimization_barrier(jnp.mean(centered * centered, axis=-1, keepdims=True))
    return centered * lax.rsqrt(variance + EPSILON) * gain + shift

def project_low(rows_low, weight):
    return low(low_back(jnp.dot(rows_low, weight, precision=PRECISE)))

def attend_all(query_all, key_all, value_all, key_live, causal, slot_size):
    total_rows, head_count, head_dim = query_all.shape
    block_count = total_rows // LONG
    score_scale = 1.0 / math.sqrt(head_dim)
    position = jnp.arange(LONG)
    allowed_base = position[:, None] // slot_size == position[None, :] // slot_size
    if causal:
        allowed_base = allowed_base & (position[None, :] <= position[:, None])

    def one_block(pieces):
        query_rows, key_rows, value_rows, live_rows = pieces
        scores = jnp.einsum('qhd,khd->hqk', query_rows, key_rows, precision=PRECISE) * score_scale
        allowed = allowed_base & live_rows[None, :]
        scores = low_back(jnp.where(allowed[None, :, :], scores, MASKED))
        softmax_full = jax.nn.softmax(scores, axis=-1)
        output = jnp.einsum('hqk,khd->qhd', low(softmax_full), value_rows, precision=PRECISE)
        return low(low_back(output))
    block_shape = (block_count, LONG, head_count, head_dim)
    mixed = lax.map(jax.checkpoint(one_block), (query_all.reshape(block_shape), key_all.reshape(block_shape), value_all.reshape(block_shape), key_live.reshape(block_count, LONG)))
    return mixed.reshape(total_rows, head_count * head_dim)

def attention_sub(rows_query, rows_source, attn, base_index, key_live, causal, slot_size):
    row_count = rows_query.shape[0]
    head_shape = (row_count, HEADS, -1)
    query_all = project_low(rows_query, attn[base_index]).reshape(head_shape)
    key_all = project_low(rows_source, attn[base_index + 1]).reshape(head_shape)
    value_all = project_low(rows_source, attn[base_index + 2]).reshape(head_shape)
    mixed = attend_all(query_all, key_all, value_all, key_live, causal, slot_size)
    return low_back(jnp.dot(mixed, attn[base_index + 3], precision=PRECISE))

def feed_ref(hidden_low, up_weight, down_weight):
    upward = low_back(jnp.dot(hidden_low, up_weight, precision=PRECISE))
    activated = low(jax.nn.silu(upward))
    return low_back(jnp.dot(activated, down_weight, precision=PRECISE))

def encoder_ref(source_rows, attn, ups, downs, gains, shifts, live_source, slot_size):
    source_low = low(source_rows)
    first_resid = source_rows + attention_sub(source_low, source_low, attn, 0, live_source, False, slot_size)
    first_hidden = layer_norm(first_resid, gains[0], shifts[0])
    second_resid = first_hidden + feed_ref(low(first_hidden), ups[0], downs[0])
    return layer_norm(second_resid, gains[1], shifts[1])

def decoder_ref(target_rows, encoded, attn, ups, downs, gains, shifts, live_source, live_target, slot_size):
    target_low = low(target_rows)
    first_resid = target_rows + attention_sub(target_low, target_low, attn, 4, live_target, True, slot_size)
    first_hidden = layer_norm(first_resid, gains[2], shifts[2])
    encoded_low = low(encoded)
    second_resid = first_hidden + attention_sub(low(first_hidden), encoded_low, attn, 8, live_source, False, slot_size)
    second_hidden = layer_norm(second_resid, gains[3], shifts[3])
    third_resid = second_hidden + feed_ref(low(second_hidden), ups[1], downs[1])
    return layer_norm(third_resid, gains[4], shifts[4])

def live_rows_of(lengths, slot_size):
    return (jnp.arange(slot_size)[None, :] < lengths[:, None]).reshape(-1)

def reference(source, target, cotangent, short_lengths, long_lengths, attn_weights, up_weights, down_weights, norm_gains, norm_shifts):
    plan = ((SHORT, short_lengths), (LONG, long_lengths))

    def forward(source_all, target_all, attn, ups, downs, gains, shifts):
        decoded_list = []
        for batch_index in range(2):
            slot_size, lengths = plan[batch_index]
            live_source = live_rows_of(lengths[0], slot_size)
            live_target = live_rows_of(lengths[1], slot_size)
            encoded = encoder_ref(source_all[batch_index], attn, ups, downs, gains, shifts, live_source, slot_size)
            decoded_list.append(decoder_ref(target_all[batch_index], encoded, attn, ups, downs, gains, shifts, live_source, live_target, slot_size))
        return jnp.stack(decoded_list)
    decoded, pullback = jax.vjp(forward, source.astype(jnp.float32), target.astype(jnp.float32), attn_weights.astype(jnp.float32), up_weights.astype(jnp.float32), down_weights.astype(jnp.float32), norm_gains.astype(jnp.float32), norm_shifts.astype(jnp.float32))
    grads = pullback(cotangent.astype(jnp.float32))
    return (decoded.astype(jnp.bfloat16), grads[0], grads[1], grads[2], grads[3], grads[4], grads[5], grads[6])
```

```python
import functools
import math

import jax
import jax.numpy as jnp
from jax import lax
from jax.experimental import pallas as pl
from jax.experimental.pallas import tpu as pltpu
from jax.sharding import PartitionSpec as P

HEADS = 8
SHORT = 256
LONG = 1024

EPSILON = 1e-05
MASKED = -1e30
F32 = jnp.float32
BF16 = jnp.bfloat16
AXES = ("dp", "head")
COLS = 256
CHUNK = 512

NN = (((1,), (0,)), ((), ()))
NT = (((1,), (1,)), ((), ()))
TN = (((0,), (0,)), ((), ()))


def dot(left, right, dims=NN):
    return lax.dot_general(left, right, dims, preferred_element_type=F32)


def params():
    return pltpu.CompilerParams(vmem_limit_bytes=63 << 20)


def cost(flops, moved, powers=0):
    return pl.CostEstimate(flops=int(flops), bytes_accessed=int(moved), transcendentals=int(powers))


def whole(array):
    return pl.BlockSpec(array.shape, lambda *step: (0,) * array.ndim)


def shaped(shape, kind):
    return jax.ShapeDtypeStruct(shape, kind)


def lanes():
    return lax.broadcasted_iota(jnp.int32, (1, 128), 1)


def one_head(which, pair):
    keep = (lanes() < 64) if which == 0 else (lanes() >= 64)
    return jnp.where(keep, pair, jnp.zeros_like(pair))


def join_heads(first, second):
    return jnp.where(lanes() < 64, first, second)


def scores_bias(bias_ref, slot, width, causal):
    bias = bias_ref[slot : slot + 1, :]
    if not causal:
        return bias
    keys = bias.shape[1]
    row = lax.broadcasted_iota(jnp.int32, (width, width), 0)
    column = lax.broadcasted_iota(jnp.int32, (width, width), 1)
    own = jnp.where(column <= row, bias[:, :width], MASKED)
    if keys == width:
        return own
    rest = jnp.broadcast_to(bias[:, width:], (width, keys - width))
    return jnp.concatenate([own, rest], axis=1)


def attend_rows(bias, q_ref, k_ref, v_ref, e_ref, o_ref, inv_ref, rows, keys):
    count = bias.shape[1]
    ones = jnp.ones((count, 128), BF16)
    for pair in range(COLS // 128):
        cols = slice(pair * 128, pair * 128 + 128)
        queries = q_ref[rows, cols]
        key_pair = k_ref[keys, cols]
        value_ext = jnp.concatenate([v_ref[keys, cols], ones], axis=1)
        outs, inverses = [], []
        for which in range(2):
            scores = dot(one_head(which, queries), key_pair, NT) + bias
            highest = jnp.max(scores, axis=1, keepdims=True)
            powers = jnp.exp(scores - highest).astype(BF16)
            e_ref[pair * 2 + which, rows, :] = powers
            mixed = dot(powers, value_ext)
            inverse = 1.0 / mixed[:, 128:]
            outs.append(mixed[:, :128] * inverse)
            inverses.append(inverse)
        o_ref[rows, cols] = join_heads(*outs).astype(BF16)
        inv_ref[rows, cols] = join_heads(*inverses)


def attend_kernel(causal, self_keys, *refs):
    xq_ref, *rest = refs
    xk_ref = xq_ref if self_keys else rest.pop(0)
    (
        mate_ref,
        wq_ref,
        wk_ref,
        wv_ref,
        bias_s_ref,
        bias_l_ref,
        o_ref,
        inv_ref,
        q_ref,
        ks_ref,
        vs_ref,
        kl_ref,
        vl_ref,
        es_ref,
        el_ref,
    ) = rest
    rows = xq_ref.shape[1]
    scale = 0.125
    for batch in range(2):
        q_ref[batch] = (dot(xq_ref[batch], wq_ref[0]) * scale).astype(BF16)
    ks_ref[...] = dot(xk_ref[0], wk_ref[0]).astype(BF16)
    vs_ref[...] = dot(xk_ref[0], wv_ref[0]).astype(BF16)
    kl_ref[:rows] = dot(xk_ref[1], wk_ref[0]).astype(BF16)
    vl_ref[:rows] = dot(xk_ref[1], wv_ref[0]).astype(BF16)
    kl_ref[rows:] = dot(mate_ref[...], wk_ref[0]).astype(BF16)
    vl_ref[rows:] = dot(mate_ref[...], wv_ref[0]).astype(BF16)
    everything = slice(None)
    bias = scores_bias(bias_l_ref, 0, rows, causal)
    attend_rows(
        bias, q_ref.at[1], kl_ref, vl_ref, el_ref, o_ref.at[1], inv_ref.at[1], everything, everything
    )
    for slot in range(rows // SHORT):
        bias = scores_bias(bias_s_ref, slot, SHORT, causal)
        here = slice(slot * SHORT, (slot + 1) * SHORT)
        attend_rows(
            bias, q_ref.at[0], ks_ref, vs_ref, es_ref, o_ref.at[0], inv_ref.at[0], here, here
        )


def attend(queries, keys, mate, weights, base, bias_s, bias_l, causal):
    _, rows, width = queries.shape
    self_keys = keys is None
    heads = width // 64
    weight = lambda index: pl.BlockSpec((1, width, COLS), lambda step: (index, 0, step))
    both = pl.BlockSpec((2, rows, COLS), lambda step: (0, 0, step))
    cols = lambda count: pl.BlockSpec((count, COLS), lambda step: (0, step))
    powers = lambda count: pl.BlockSpec((COLS // 64, rows, count), lambda step: (step, 0, 0))
    xs = (queries,) if self_keys else (queries, keys)
    flops = 2 * rows * width * width * 7 + 4 * rows * width * (SHORT + LONG)
    return pl.pallas_call(
        functools.partial(attend_kernel, causal, self_keys),
        grid=(width // COLS,),
        out_shape=(
            shaped((2, rows, width), BF16),
            shaped((2, rows, width), F32),
            shaped((2, rows, width), BF16),
            shaped((rows, width), BF16),
            shaped((rows, width), BF16),
            shaped((LONG, width), BF16),
            shaped((LONG, width), BF16),
            shaped((heads, rows, SHORT), BF16),
            shaped((heads, rows, LONG), BF16),
        ),
        in_specs=[whole(x) for x in xs]
        + [whole(mate)]
        + [weight(base), weight(base + 1), weight(base + 2)]
        + [whole(bias_s), whole(bias_l)],
        out_specs=(
            both,
            both,
            both,
            cols(rows),
            cols(rows),
            cols(LONG),
            cols(LONG),
            powers(SHORT),
            powers(LONG),
        ),
        compiler_params=params(),
        cost_estimate=cost(flops * 2, 22 << 20, heads * rows * (SHORT + LONG)),
        name="attend",
    )(*xs, mate, weights, weights, weights, bias_s, bias_l)


def attend_back_rows(
    do_ref, o_ref, inv_ref, q_ref, k_ref, v_ref, e_ref, dq_ref, dk_ref, dv_ref, rows, keys, scale
):
    for pair in range(COLS // 128):
        cols = slice(pair * 128, pair * 128 + 128)
        grad = do_ref[rows, cols].astype(F32) * inv_ref[rows, cols]
        product = grad * o_ref[rows, cols].astype(F32)
        grad_low = grad.astype(BF16)
        queries = q_ref[rows, cols]
        key_pair = k_ref[keys, cols]
        value_pair = v_ref[keys, cols]
        grad_turned = grad.T.astype(BF16)
        queries_turned = queries.astype(F32).T.astype(BF16)
        grad_q, grad_k, grad_v = [], [], []
        for which in range(2):
            inner = jnp.sum(one_head(which, product), axis=1, keepdims=True)
            grad_probs = dot(one_head(which, grad_low), value_pair, NT)
            powers = e_ref[pair * 2 + which, rows, :]
            grad_scores = (powers.astype(F32) * (grad_probs - inner)).astype(BF16)
            grad_q.append(dot(grad_scores, key_pair))
            head = slice(which * 64, which * 64 + 64)
            grad_v.append(dot(grad_turned[head], powers))
            grad_k.append(dot(queries_turned[head], grad_scores))
        dq_ref[rows, cols] = (join_heads(*grad_q) * scale).astype(BF16)
        dk_ref[keys, cols] = jnp.concatenate(grad_k, axis=0).T.astype(BF16)
        dv_ref[keys, cols] = jnp.concatenate(grad_v, axis=0).T.astype(BF16)


def attend_back_kernel(self_keys, *refs):
    (
        do_ref,
        o_ref,
        inv_ref,
        q_ref,
        ks_ref,
        vs_ref,
        kl_ref,
        vl_ref,
        es_ref,
        el_ref,
        resid_ref,
        xq_ref,
        *rest,
    ) = refs
    xk_ref = xq_ref if self_keys else rest.pop(0)
    mate_ref, wq_ref, wk_ref, wv_ref, *rest = rest
    dx_ref = rest.pop(0)
    dy_ref = dx_ref if self_keys else rest.pop(0)
    dmate_ref, dwq_ref, dwk_ref, dwv_ref, dqs, dks, dvs, dql, dkl, dvl, mate_sum = rest
    rows = xq_ref.shape[1]
    scale = 0.125
    everything = slice(None)
    attend_back_rows(
        do_ref.at[1],
        o_ref.at[1],
        inv_ref.at[1],
        q_ref.at[1],
        kl_ref,
        vl_ref,
        el_ref,
        dql,
        dkl,
        dvl,
        everything,
        everything,
        scale,
    )
    for slot in range(rows // SHORT):
        here = slice(slot * SHORT, (slot + 1) * SHORT)
        attend_back_rows(
            do_ref.at[0],
            o_ref.at[0],
            inv_ref.at[0],
            q_ref.at[0],
            ks_ref,
            vs_ref,
            es_ref,
            dqs,
            dks,
            dvs,
            here,
            here,
            scale,
        )
    wq, wk, wv = wq_ref[0], wk_ref[0], wv_ref[0]

    @pl.when(pl.program_id(0) == 0)
    def _():
        dx_ref[...] = resid_ref[...]
        if not self_keys:
            dy_ref[...] = jnp.zeros_like(dy_ref)
        mate_sum[...] = jnp.zeros_like(mate_sum)

    own = slice(0, rows)
    other = slice(rows, 2 * rows)
    dx_ref[0] += dot(dqs[...], wq, NT)
    dx_ref[1] += dot(dql[...], wq, NT)
    dy_ref[0] += dot(dks[...], wk, NT) + dot(dvs[...], wv, NT)
    dy_ref[1] += dot(dkl[own], wk, NT) + dot(dvl[own], wv, NT)
    mate_sum[...] += dot(dkl[other], wk, NT) + dot(dvl[other], wv, NT)
    dwq_ref[...] = (dot(xq_ref[0], dqs[...], TN) + dot(xq_ref[1], dql[...], TN)).astype(BF16)
    short, long, mate = xk_ref[0], xk_ref[1], mate_ref[...]
    dwk_ref[...] = (
        dot(short, dks[...], TN) + dot(long, dkl[own], TN) + dot(mate, dkl[other], TN)
    ).astype(BF16)
    dwv_ref[...] = (
        dot(short, dvs[...], TN) + dot(long, dvl[own], TN) + dot(mate, dvl[other], TN)
    ).astype(BF16)

    @pl.when(pl.program_id(0) == pl.num_programs(0) - 1)
    def _():
        dmate_ref[...] = mate_sum[...].astype(BF16)


def attend_back(grad, saved, resid, queries, keys, mate, weights, base):
    o, inverse, q, ks, vs, kl, vl, es, el = saved
    _, rows, width = queries.shape
    self_keys = keys is None
    heads = width // 64
    weight = lambda index: pl.BlockSpec((1, width, COLS), lambda step: (index, 0, step))
    both = pl.BlockSpec((2, rows, COLS), lambda step: (0, 0, step))
    cols = lambda count: pl.BlockSpec((count, COLS), lambda step: (0, step))
    powers = lambda count: pl.BlockSpec((COLS // 64, rows, count), lambda step: (step, 0, 0))
    full = pl.BlockSpec((2, rows, width), lambda step: (0, 0, 0))
    xs = (queries,) if self_keys else (queries, keys)
    flops = 2 * rows * width * width * 14 + 8 * rows * width * (SHORT + LONG)
    data = (shaped((2, rows, width), F32),) * len(xs)
    return pl.pallas_call(
        functools.partial(attend_back_kernel, self_keys),
        grid=(width // COLS,),
        out_shape=data + (shaped((rows, width), BF16),) + (shaped((width, width), BF16),) * 3,
        in_specs=[both] * 4
        + [cols(rows)] * 2
        + [cols(LONG)] * 2
        + [powers(SHORT), powers(LONG), whole(resid)]
        + [whole(x) for x in xs]
        + [whole(mate), weight(base), weight(base + 1), weight(base + 2)],
        out_specs=(full,) * len(xs)
        + (pl.BlockSpec((rows, width), lambda step: (0, 0)),)
        + (cols(width),) * 3,
        scratch_shapes=[pltpu.VMEM((rows, COLS), BF16)] * 4
        + [pltpu.VMEM((LONG, COLS), BF16)] * 2
        + [pltpu.VMEM((rows, width), F32)],
        compiler_params=params(),
        cost_estimate=cost(flops * 2, 28 << 20),
        name="attend_back",
    )(grad, o, inverse, q, ks, vs, kl, vl, es, el, resid, *xs, mate, weights, weights, weights)


def norm_parts(resid):
    average = jnp.mean(resid, axis=-1, keepdims=True)
    centered = resid - average
    variance = jnp.mean(centered * centered, axis=-1, keepdims=True)
    spread = lax.rsqrt(variance + EPSILON)
    return centered * spread, spread


def norm_back(normal, spread, gain, grad):
    scaled = grad * gain
    first = jnp.mean(scaled, axis=-1, keepdims=True)
    second = jnp.mean(scaled * normal, axis=-1, keepdims=True)
    return (scaled - first - normal * second) * spread


def add_norm_grads(ref, place, grad, normal):
    ref[place : place + 1, :] += jnp.sum(grad * normal, axis=0, keepdims=True)
    ref[place + 1 : place + 2, :] += jnp.sum(grad, axis=0, keepdims=True)


def logistic(value):
    return 1.0 / (1.0 + jnp.exp(-value))


def feed_kernel(chunks, o_ref, x_ref, wo_ref, up_ref, down_ref, gain_ref, shift_ref, r1_ref, u_ref, r2_ref, enc_ref):
    resid = x_ref[0].astype(F32) + dot(o_ref[0], wo_ref[0])
    r1_ref[0] = resid
    normal, _ = norm_parts(resid)
    hidden = normal * gain_ref[0:1] + shift_ref[0:1]
    hidden_low = hidden.astype(BF16)
    total = hidden
    for chunk in range(chunks):
        part = slice(chunk * CHUNK, (chunk + 1) * CHUNK)
        upward = dot(hidden_low, up_ref[0, :, part])
        u_ref[0, :, part] = upward
        active = (upward * logistic(upward)).astype(BF16)
        total = total + dot(active, down_ref[0, part, :])
    r2_ref[0] = total
    normal, _ = norm_parts(total)
    enc_ref[0] = (normal * gain_ref[1:2] + shift_ref[1:2]).astype(BF16)


def feed(o, x, attn, ups, downs, gains, shifts):
    _, rows, width = x.shape
    inner = ups.shape[2]
    row = lambda count: pl.BlockSpec((1, rows, count), lambda batch: (batch, 0, 0))
    pick = lambda array, index: pl.BlockSpec((1,) + array.shape[1:], lambda batch: (index, 0, 0))
    return pl.pallas_call(
        functools.partial(feed_kernel, inner // CHUNK),
        grid=(2,),
        out_shape=(
            shaped((2, rows, width), F32),
            shaped((2, rows, inner), F32),
            shaped((2, rows, width), F32),
            shaped((2, rows, width), BF16),
        ),
        in_specs=[row(width), row(width), pick(attn, 3), pick(ups, 0), pick(downs, 0), whole(gains), whole(shifts)],
        out_specs=(row(width), row(inner), row(width), row(width)),
        compiler_params=params(),
        cost_estimate=cost(4 * rows * width * (width + 2 * inner), 22 << 20, 2 * rows * inner),
        name="feed",
    )(o, x, attn, ups, downs, gains, shifts)


def middle_kernel(o_ref, x_ref, wo_ref, gain_ref, shift_ref, r_ref, low_ref):
    resid = x_ref[0].astype(F32) + dot(o_ref[0], wo_ref[0])
    r_ref[0] = resid
    normal, _ = norm_parts(resid)
    low_ref[0] = (normal * gain_ref[2:3] + shift_ref[2:3]).astype(BF16)


def middle(o, x, attn, gains, shifts):
    _, rows, width = x.shape
    row = lambda count: pl.BlockSpec((1, rows, count), lambda batch: (batch, 0, 0))
    pick = lambda array, index: pl.BlockSpec((1,) + array.shape[1:], lambda batch: (index, 0, 0))
    return pl.pallas_call(
        middle_kernel,
        grid=(2,),
        out_shape=(shaped((2, rows, width), F32), shaped((2, rows, width), BF16)),
        in_specs=[row(width), row(width), pick(attn, 7), whole(gains), whole(shifts)],
        out_specs=(row(width), row(width)),
        compiler_params=params(),
        cost_estimate=cost(4 * rows * width * width, 7 << 20),
        name="middle",
    )(o, x, attn, gains, shifts)


def feed_back_chunks(
    chunks, grad, low, hidden_low, u_ref, a_ref, up_ref, down_ref, up_sum, down_sum
):
    total = grad
    for chunk in range(chunks):
        part = slice(chunk * CHUNK, (chunk + 1) * CHUNK)
        upward = u_ref[:, part]
        gate = logistic(upward)
        if a_ref is None:
            active = (upward * gate).astype(BF16)
        else:
            active = a_ref[:, part]
        grad_active = dot(low, down_ref[0, part, :], NT)
        grad_up = (grad_active * gate * (1.0 + upward * (1.0 - gate))).astype(BF16)
        down_sum[part, :] += dot(active, low, TN)
        up_sum[:, part] += dot(hidden_low, grad_up, TN)
        total = total + dot(grad_up, up_ref[0, :, part], NT)
    return total


def clear_first(*refs):
    @pl.when(pl.program_id(0) == 0)
    def _():
        for ref in refs:
            ref[...] = jnp.zeros_like(ref)


def write_last(*pairs):
    @pl.when(pl.program_id(0) == pl.num_programs(0) - 1)
    def _():
        for ref, total in pairs:
            ref[...] = total[...].astype(BF16)


def turn_kernel(
    chunks,
    o_ref,
    r3_ref,
    cot_ref,
    wo_ref,
    up_ref,
    down_ref,
    gain_ref,
    shift_ref,
    out_ref,
    dr_ref,
    do_ref,
    dup_ref,
    ddown_ref,
    dwo_ref,
    norm_ref,
    u_s,
    a_s,
    up_sum,
    down_sum,
    wo_sum,
):
    clear_first(up_sum, down_sum, wo_sum, norm_ref)
    mixed = o_ref[0]
    normal3, _ = norm_parts(r3_ref[0])
    resid4 = normal3 * gain_ref[2:3] + shift_ref[2:3] + dot(mixed, wo_ref[0])
    normal4, spread4 = norm_parts(resid4)
    hidden = normal4 * gain_ref[3:4] + shift_ref[3:4]
    hidden_low = hidden.astype(BF16)
    total = hidden
    for chunk in range(chunks):
        part = slice(chunk * CHUNK, (chunk + 1) * CHUNK)
        upward = dot(hidden_low, up_ref[0, :, part])
        u_s[:, part] = upward
        active = (upward * logistic(upward)).astype(BF16)
        a_s[:, part] = active
        total = total + dot(active, down_ref[0, part, :])
    normal5, spread5 = norm_parts(total)
    out_ref[0] = (normal5 * gain_ref[4:5] + shift_ref[4:5]).astype(BF16)
    grad = cot_ref[0].astype(F32)
    add_norm_grads(norm_ref, 0, grad, normal5)
    grad = norm_back(normal5, spread5, gain_ref[4:5], grad)
    grad = feed_back_chunks(
        chunks, grad, grad.astype(BF16), hidden_low, u_s, a_s, up_ref, down_ref, up_sum, down_sum
    )
    add_norm_grads(norm_ref, 2, grad, normal4)
    grad = norm_back(normal4, spread4, gain_ref[3:4], grad)
    dr_ref[0] = grad
    low = grad.astype(BF16)
    wo_sum[...] += dot(mixed, low, TN)
    do_ref[0] = dot(low, wo_ref[0], NT).astype(BF16)
    write_last((dup_ref, up_sum), (ddown_ref, down_sum), (dwo_ref, wo_sum))


def turn(o, r3, cot, attn, ups, downs, gains, shifts):
    _, rows, width = r3.shape
    inner = ups.shape[2]
    row = pl.BlockSpec((1, rows, width), lambda batch: (batch, 0, 0))
    pick = lambda array, index: pl.BlockSpec((1,) + array.shape[1:], lambda batch: (index, 0, 0))
    still = lambda *shape: pl.BlockSpec(shape, lambda batch: (0,) * len(shape))
    return pl.pallas_call(
        functools.partial(turn_kernel, inner // CHUNK),
        grid=(2,),
        out_shape=(
            shaped((2, rows, width), BF16),
            shaped((2, rows, width), F32),
            shaped((2, rows, width), BF16),
            shaped((width, inner), BF16),
            shaped((inner, width), BF16),
            shaped((width, width), BF16),
            shaped((8, width), F32),
        ),
        in_specs=[row, row, row, pick(attn, 11), pick(ups, 1), pick(downs, 1), whole(gains), whole(shifts)],
        out_specs=(row, row, row, still(width, inner), still(inner, width), still(width, width), still(8, width)),
        scratch_shapes=[
            pltpu.VMEM((rows, inner), F32),
            pltpu.VMEM((rows, inner), BF16),
            pltpu.VMEM((width, inner), F32),
            pltpu.VMEM((inner, width), F32),
            pltpu.VMEM((width, width), F32),
        ],
        compiler_params=params(),
        cost_estimate=cost(12 * rows * width * (width + 2 * inner), 20 << 20, 4 * rows * inner),
        name="turn",
    )(o, r3, cot, attn, ups, downs, gains, shifts)


def feed_back_kernel(
    chunks,
    grad_ref,
    mate_ref,
    r2_ref,
    r1_ref,
    u_ref,
    o_ref,
    wo_ref,
    up_ref,
    down_ref,
    gain_ref,
    shift_ref,
    dr_ref,
    do_ref,
    dup_ref,
    ddown_ref,
    dwo_ref,
    norm_ref,
    grad_s,
    up_sum,
    down_sum,
    wo_sum,
):
    clear_first(up_sum, down_sum, wo_sum, norm_ref)
    grad_s[...] = grad_ref[0]

    @pl.when(pl.program_id(0) == 1)
    def _():
        grad_s[...] += mate_ref[...].astype(F32)

    grad = grad_s[...]
    normal2, spread2 = norm_parts(r2_ref[0])
    add_norm_grads(norm_ref, 2, grad, normal2)
    grad = norm_back(normal2, spread2, gain_ref[1:2], grad)
    normal1, spread1 = norm_parts(r1_ref[0])
    hidden_low = (normal1 * gain_ref[0:1] + shift_ref[0:1]).astype(BF16)
    grad = feed_back_chunks(
        chunks,
        grad,
        grad.astype(BF16),
        hidden_low,
        u_ref.at[0],
        None,
        up_ref,
        down_ref,
        up_sum,
        down_sum,
    )
    add_norm_grads(norm_ref, 0, grad, normal1)
    grad = norm_back(normal1, spread1, gain_ref[0:1], grad)
    dr_ref[0] = grad
    low = grad.astype(BF16)
    wo_sum[...] += dot(o_ref[0], low, TN)
    do_ref[0] = dot(low, wo_ref[0], NT).astype(BF16)
    write_last((dup_ref, up_sum), (ddown_ref, down_sum), (dwo_ref, wo_sum))


def feed_back(grad, mate, r2, r1, u, o, attn, ups, downs, gains, shifts):
    _, rows, width = r1.shape
    inner = ups.shape[2]
    row = lambda count: pl.BlockSpec((1, rows, count), lambda batch: (batch, 0, 0))
    pick = lambda array, index: pl.BlockSpec((1,) + array.shape[1:], lambda batch: (index, 0, 0))
    still = lambda *shape: pl.BlockSpec(shape, lambda batch: (0,) * len(shape))
    return pl.pallas_call(
        functools.partial(feed_back_kernel, inner // CHUNK),
        grid=(2,),
        out_shape=(
            shaped((2, rows, width), F32),
            shaped((2, rows, width), BF16),
            shaped((width, inner), BF16),
            shaped((inner, width), BF16),
            shaped((width, width), BF16),
            shaped((8, width), F32),
        ),
        in_specs=[
            row(width),
            whole(mate),
            row(width),
            row(width),
            row(inner),
            row(width),
            pick(attn, 3),
            pick(ups, 0),
            pick(downs, 0),
            whole(gains),
            whole(shifts),
        ],
        out_specs=(row(width), row(width), still(width, inner), still(inner, width), still(width, width), still(8, width)),
        scratch_shapes=[
            pltpu.VMEM((rows, width), F32),
            pltpu.VMEM((width, inner), F32),
            pltpu.VMEM((inner, width), F32),
            pltpu.VMEM((width, width), F32),
        ],
        compiler_params=params(),
        cost_estimate=cost(8 * rows * width * (width + 2 * inner), 30 << 20, 2 * rows * inner),
        name="feed_back",
    )(grad, mate, r2, r1, u, o, attn, ups, downs, gains, shifts)


def middle_back_kernel(grad_ref, r_ref, o_ref, wo_ref, gain_ref, dr_ref, do_ref, dwo_ref, norm_ref, wo_sum):
    clear_first(wo_sum, norm_ref)
    grad = grad_ref[0]
    normal, spread = norm_parts(r_ref[0])
    add_norm_grads(norm_ref, 0, grad, normal)
    grad = norm_back(normal, spread, gain_ref[2:3], grad)
    dr_ref[0] = grad
    low = grad.astype(BF16)
    wo_sum[...] += dot(o_ref[0], low, TN)
    do_ref[0] = dot(low, wo_ref[0], NT).astype(BF16)
    write_last((dwo_ref, wo_sum))


def middle_back(grad, r, o, attn, gains):
    _, rows, width = r.shape
    row = pl.BlockSpec((1, rows, width), lambda batch: (batch, 0, 0))
    pick = lambda array, index: pl.BlockSpec((1,) + array.shape[1:], lambda batch: (index, 0, 0))
    still = lambda *shape: pl.BlockSpec(shape, lambda batch: (0,) * len(shape))
    return pl.pallas_call(
        middle_back_kernel,
        grid=(2,),
        out_shape=(
            shaped((2, rows, width), F32),
            shaped((2, rows, width), BF16),
            shaped((width, width), BF16),
            shaped((8, width), F32),
        ),
        in_specs=[row, row, row, pick(attn, 7), whole(gains)],
        out_specs=(row, row, still(width, width), still(8, width)),
        scratch_shapes=[pltpu.VMEM((width, width), F32)],
        compiler_params=params(),
        cost_estimate=cost(8 * rows * width * width, 12 << 20),
        name="middle_back",
    )(grad, r, o, attn, gains)


def device_index():
    return lax.axis_index("dp") * lax.axis_size("head") + lax.axis_index("head")


def swap(array, bit):
    count = lax.axis_size("dp") * lax.axis_size("head")
    return lax.ppermute(array, AXES, [(place, place ^ (1 << bit)) for place in range(count)])


def scatter_sum(stack, order):
    count = lax.axis_size("dp") * lax.axis_size("head")
    kinds, rows, columns = stack.shape
    here = device_index()
    current = stack.reshape(kinds, count, rows // count, columns)
    left = sorted(order)
    for bit in order:
        low = 1 << left.index(bit)
        left.remove(bit)
        high = current.shape[1] // (2 * low)
        view = current.reshape(kinds, high, 2, low, rows // count, columns)
        mine = (here >> bit) & 1
        kept = lax.dynamic_index_in_dim(view, mine, axis=2, keepdims=False)
        sent = lax.dynamic_index_in_dim(view, 1 - mine, axis=2, keepdims=False)
        total = kept.astype(F32) + swap(sent, bit).astype(F32)
        current = total.reshape(kinds, high * low, rows // count, columns)
        if left:
            current = current.astype(BF16)
    return current.reshape(kinds, rows // count, columns)


def sum_everywhere(array, bits):
    for bit in range(bits):
        array = array + swap(array, bit)
    return array


def body(
    source,
    target,
    cotangent,
    short_lengths,
    long_lengths,
    attn,
    ups,
    downs,
    gains,
    shifts,
):
    _, rows, width = source.shape
    devices = lax.axis_size("dp") * lax.axis_size("head")
    bits = devices.bit_length() - 1
    assert 2 * rows == LONG and rows % SHORT == 0 and devices == 1 << bits
    place = lax.axis_index("head")
    half = place % 2
    slots = rows // SHORT

    def biases(row, causal):
        short = lax.dynamic_slice_in_dim(short_lengths[row], place * slots, slots)
        bias_s = jnp.where(jnp.arange(SHORT)[None, :] < short[:, None], 0.0, MASKED).astype(F32)
        length = lax.dynamic_index_in_dim(long_lengths[row], place // 2, keepdims=False)
        position = jnp.arange(rows)
        own = position + half * rows < length
        other = position + (1 - half) * rows < length
        if causal:
            other = other & (half == 1)
        allowed = jnp.concatenate([own, other])[None, :]
        return bias_s, jnp.where(allowed, 0.0, MASKED).astype(F32)

    source_bias = biases(0, False)
    target_bias = biases(1, True)
    source_mate = swap(source[1], 0)
    target_mate = swap(target[1], 0)

    enc_saved = attend(source, None, source_mate, attn, 0, *source_bias, False)
    r1, u, r2, enc = feed(enc_saved[0], source, attn, ups, downs, gains, shifts)
    enc_mate = swap(enc[1], 0)
    self_saved = attend(target, None, target_mate, attn, 4, *target_bias, True)
    r3, h3 = middle(self_saved[0], target, attn, gains, shifts)
    cross_saved = attend(h3, enc, enc_mate, attn, 8, *source_bias, False)
    decoded, dr4, do_cross, dup1, ddown1, dw11, norms_a = turn(
        cross_saved[0], r3, cotangent, attn, ups, downs, gains, shifts
    )
    dh3, denc, denc_mate, dw8, dw9, dw10 = attend_back(
        do_cross, cross_saved, dr4, h3, enc, enc_mate, attn, 8
    )
    denc_mate = swap(denc_mate, 0)
    dr3, do_self, dw7, norms_b = middle_back(dh3, r3, self_saved[0], attn, gains)
    grad_target, dt_mate, dw4, dw5, dw6 = attend_back(
        do_self, self_saved, dr3, target, None, target_mate, attn, 4
    )
    dt_mate = swap(dt_mate, 0)
    dr1, do_enc, dup0, ddown0, dw3, norms_c = feed_back(
        denc, denc_mate, r2, r1, u, enc_saved[0], attn, ups, downs, gains, shifts
    )
    grad_source, ds_mate, dw0, dw1, dw2 = attend_back(
        do_enc, enc_saved, dr1, source, None, source_mate, attn, 0
    )
    ds_mate = swap(ds_mate, 0)
    grad_source = grad_source.at[1].add(ds_mate.astype(F32))
    grad_target = grad_target.at[1].add(dt_mate.astype(F32))

    first = tuple(range(bits))
    second = (0, 2, 1) + tuple(range(3, bits))
    up1 = scatter_sum(dup1[None], first)
    down1 = scatter_sum(ddown1[None], second)
    part_a = scatter_sum(jnp.stack([dw11, dw8]), first)
    part_b = scatter_sum(jnp.stack([dw9, dw10]), second)
    part_c = scatter_sum(jnp.stack([dw7, dw4]), first)
    part_d = scatter_sum(jnp.stack([dw5, dw6]), second)
    up0 = scatter_sum(dup0[None], first)
    down0 = scatter_sum(ddown0[None], second)
    part_e = scatter_sum(jnp.stack([dw3, dw0]), first)
    part_f = scatter_sum(jnp.stack([dw1, dw2]), second)
    grad_attn = jnp.stack(
        [
            part_e[1],
            part_f[0],
            part_f[1],
            part_e[0],
            part_c[1],
            part_d[0],
            part_d[1],
            part_c[0],
            part_a[1],
            part_b[0],
            part_b[1],
            part_a[0],
        ]
    )
    grad_up = jnp.concatenate([up0, up1])
    grad_down = jnp.concatenate([down0, down1])
    norms = jnp.stack(
        [
            norms_c[0],
            norms_c[2],
            norms_b[0],
            norms_a[2],
            norms_a[0],
            norms_c[1],
            norms_c[3],
            norms_b[1],
            norms_a[3],
            norms_a[1],
        ]
    )
    norms = sum_everywhere(norms, bits)
    share = width // devices
    norms = lax.dynamic_slice_in_dim(norms, device_index() * share, share, axis=1)
    return (
        decoded,
        grad_source,
        grad_target,
        grad_attn,
        grad_up,
        grad_down,
        norms[:5],
        norms[5:],
    )


def solution(mesh):
    rows = P(None, AXES, None)
    return jax.shard_map(
        body,
        mesh=mesh,
        in_specs=(rows, rows, rows, P(None, "dp"), P(None, "dp"), P(), P(), P(), P(), P()),
        out_specs=(rows, rows, rows, rows, rows, rows, P(None, AXES), P(None, AXES)),
        check_vma=False,
    )
```

```python
import functools
import math

import jax
import jax.numpy as jnp
from jax import lax
from jax.experimental import pallas as pl
from jax.experimental.pallas import tpu as pltpu
from jax.sharding import PartitionSpec as P

HEADS = 8
SHORT = 256
LONG = 1024

EPSILON = 1e-05
MASKED = -1e30
F32 = jnp.float32
BF16 = jnp.bfloat16
AXES = ("dp", "head")
COLS = 256
CHUNK = 512

NN = (((1,), (0,)), ((), ()))
NT = (((1,), (1,)), ((), ()))
TN = (((0,), (0,)), ((), ()))


def dot(left, right, dims=NN):
    return lax.dot_general(left, right, dims, preferred_element_type=F32)


def params():
    return pltpu.CompilerParams(vmem_limit_bytes=63 << 20)


def cost(flops, moved, powers=0):
    return pl.CostEstimate(flops=int(flops), bytes_accessed=int(moved), transcendentals=int(powers))


def whole(array):
    return pl.BlockSpec(array.shape, lambda *step: (0,) * array.ndim)


def shaped(shape, kind):
    return jax.ShapeDtypeStruct(shape, kind)


def lanes():
    return lax.broadcasted_iota(jnp.int32, (1, 128), 1)


def one_head(which, pair):
    keep = (lanes() < 64) if which == 0 else (lanes() >= 64)
    return jnp.where(keep, pair, jnp.zeros_like(pair))


def join_heads(first, second):
    return jnp.where(lanes() < 64, first, second)


MESH = pl.DeviceIdType.MESH


def partner(bit):
    head_bits = lax.axis_size("head").bit_length() - 1
    data, head = lax.axis_index("dp"), lax.axis_index("head")
    if bit < head_bits:
        step = 1 << bit
        mine = (head // step) % 2
        return mine, (data, head + (1 - 2 * mine) * step)
    step = 1 << (bit - head_bits)
    mine = (data // step) % 2
    return mine, (data + (1 - 2 * mine) * step, head)


class Flow:
    def __init__(self, order, first, last, pieces):
        self.order, self.first, self.last = order, first, last
        self.arrays = []
        self.pieces = []
        total = 0
        for array, lead in pieces:
            known = [index for index, other in enumerate(self.arrays) if other is array]
            if not known:
                self.arrays.append(array)
            index = known[0] if known else len(self.arrays) - 1
            self.pieces.append((index, lead, total, array.shape[-3]))
            total += array.shape[-3]
        self.block = (total,) + pieces[0][0].shape[-2:]

    def shape(self, stage):
        return (2,) * (len(self.order) - stage) + self.block

    def out(self):
        done = self.last == len(self.order)
        return shaped(self.shape(self.last), F32 if done else BF16)

    def scratch(self):
        stages = range(self.first, self.last)
        count = len(self.pieces)
        dma = pltpu.SemaphoreType.DMA
        return (
            [pltpu.VMEM(self.shape(self.first + 1), BF16)]
            + [pltpu.VMEM(self.shape(stage + 1), BF16) for stage in stages]
            + [pltpu.VMEM(self.shape(stage + 1), BF16) for stage in stages[:-1]]
            + [dma((count,)), dma((count,)), dma((count,)), dma((len(stages),)), dma((len(stages),))]
        )

    def bind(self, inputs, out, scratch):
        stages = range(self.first, self.last)
        self.in_refs, self.out_ref = inputs, out
        self.own = scratch[0]
        self.got = dict(zip(stages, scratch[1 : 1 + len(stages)]))
        self.sum = dict(zip(stages[:-1], scratch[1 + len(stages) :]))
        self.local_sem, self.piece_send, self.piece_recv, self.send, self.recv = scratch[-5:]

    def where(self, stage, index):
        left = sorted(self.order[stage:])
        place = len(left) - 1 - left.index(self.order[stage])
        return (slice(None),) * place + (index,)

    def piece_copies(self):
        stage = self.first
        mine, device = partner(self.order[stage])
        for number, (index, lead, start, count) in enumerate(self.pieces):
            prefix = () if lead is None else (lead,)
            target = (slice(None),) * (len(self.order) - stage - 1) + (slice(start, start + count),)
            ref = self.in_refs[index]
            yield pltpu.make_async_remote_copy(
                src_ref=ref.at[prefix + self.where(stage, 1 - mine)],
                dst_ref=self.got[stage].at[target],
                send_sem=self.piece_send.at[number],
                recv_sem=self.piece_recv.at[number],
                device_id=device,
                device_id_type=MESH,
            )
            yield pltpu.make_async_copy(
                ref.at[prefix + self.where(stage, mine)],
                self.own.at[target],
                self.local_sem.at[number],
            )

    def stage_copy(self, stage):
        mine, device = partner(self.order[stage])
        return pltpu.make_async_remote_copy(
            src_ref=self.sum[stage - 1].at[self.where(stage, 1 - mine)],
            dst_ref=self.got[stage],
            send_sem=self.send.at[stage - self.first],
            recv_sem=self.recv.at[stage - self.first],
            device_id=device,
            device_id_type=MESH,
        )

    def start(self):
        for copy in self.piece_copies():
            copy.start()

    def step(self, stage):
        if stage == self.first:
            for copy in self.piece_copies():
                copy.wait()
            kept = self.own[...]
        else:
            self.stage_copy(stage).wait()
            mine, _ = partner(self.order[stage])
            kept = self.sum[stage - 1][self.where(stage, mine)]
        total = kept.astype(F32) + self.got[stage][...].astype(F32)
        if stage == self.last - 1:
            self.out_ref[...] = total.astype(self.out_ref.dtype)
        else:
            self.sum[stage][...] = total.astype(BF16)
            self.stage_copy(stage + 1).start()


def greet(bits):
    ready = pltpu.get_barrier_semaphore()
    for bit in bits:
        _, device = partner(bit)
        pl.semaphore_signal(ready, inc=1, device_id=device, device_id_type=MESH)
    pl.semaphore_wait(ready, len(bits))


def call(kernel, steps, ins, outs, scratch, name, estimate, flows=(), plan=None, collective=None):
    extra_in = [array for flow in flows for array in flow.arrays]
    bits = sorted({bit for flow in flows for bit in flow.order[flow.first : flow.last]})
    counts = (len(ins), len(outs), len(scratch))

    def body(*refs):
        refs = list(refs)
        take = lambda count: [refs.pop(0) for _ in range(count)]
        main = take(counts[0])
        inputs = [take(len(flow.arrays)) for flow in flows]
        main += take(counts[1])
        results = take(len(flows))
        main += take(counts[2])
        for flow, given, result in zip(flows, inputs, results):
            flow.bind(given, result, take(len(flow.scratch())))

        def tick(slot):
            for (step, place), actions in (plan or {}).items():
                if place == slot:

                    @pl.when(pl.program_id(0) == step)
                    def _():
                        if (step, slot) == (0, 0):
                            greet(bits)
                        for number, stage in actions:
                            if stage is None:
                                flows[number].start()
                            else:
                                flows[number].step(stage)

        kernel(tick, *main)

    still = lambda shape: pl.BlockSpec(shape, lambda step: (0,) * len(shape))
    remote = dict(collective_id=collective, has_side_effects=True) if flows else {}
    result = pl.pallas_call(
        body,
        grid=(steps,),
        out_shape=[shape for shape, _ in outs] + [flow.out() for flow in flows],
        in_specs=[spec for _, spec in ins] + [pl.BlockSpec(memory_space=pl.ANY)] * len(extra_in),
        out_specs=[spec for _, spec in outs] + [still(flow.out().shape) for flow in flows],
        scratch_shapes=list(scratch) + [shape for flow in flows for shape in flow.scratch()],
        compiler_params=pltpu.CompilerParams(vmem_limit_bytes=63 << 20, **remote),
        cost_estimate=estimate,
        name=name,
    )(*[array for array, _ in ins], *extra_in)
    return result[: len(outs)], result[len(outs) :]


def scores_bias(bias_ref, slot, width, causal):
    bias = bias_ref[slot : slot + 1, :]
    if not causal:
        return bias
    keys = bias.shape[1]
    row = lax.broadcasted_iota(jnp.int32, (width, width), 0)
    column = lax.broadcasted_iota(jnp.int32, (width, width), 1)
    own = jnp.where(column <= row, bias[:, :width], MASKED)
    if keys == width:
        return own
    rest = jnp.broadcast_to(bias[:, width:], (width, keys - width))
    return jnp.concatenate([own, rest], axis=1)


def attend_rows(bias, q_ref, k_ref, v_ref, e_ref, o_ref, inv_ref, rows, keys):
    count = bias.shape[1]
    ones = jnp.ones((count, 128), BF16)
    for pair in range(COLS // 128):
        cols = slice(pair * 128, pair * 128 + 128)
        queries = q_ref[rows, cols]
        key_pair = k_ref[keys, cols]
        value_ext = jnp.concatenate([v_ref[keys, cols], ones], axis=1)
        outs, inverses = [], []
        for which in range(2):
            scores = dot(one_head(which, queries), key_pair, NT) + bias
            highest = jnp.max(scores, axis=1, keepdims=True)
            powers = jnp.exp(scores - highest).astype(BF16)
            e_ref[pair * 2 + which, rows, :] = powers
            mixed = dot(powers, value_ext)
            inverse = 1.0 / mixed[:, 128:]
            outs.append(mixed[:, :128] * inverse)
            inverses.append(inverse)
        o_ref[rows, cols] = join_heads(*outs).astype(BF16)
        inv_ref[rows, cols] = join_heads(*inverses)


def attend_kernel(causal, self_keys, *refs):
    xq_ref, *rest = refs
    xk_ref = xq_ref if self_keys else rest.pop(0)
    (
        mate_ref,
        wq_ref,
        wk_ref,
        wv_ref,
        bias_s_ref,
        bias_l_ref,
        o_ref,
        inv_ref,
        q_ref,
        ks_ref,
        vs_ref,
        kl_ref,
        vl_ref,
        es_ref,
        el_ref,
    ) = rest
    rows = xq_ref.shape[1]
    scale = 0.125
    for batch in range(2):
        q_ref[batch] = (dot(xq_ref[batch], wq_ref[0]) * scale).astype(BF16)
    ks_ref[...] = dot(xk_ref[0], wk_ref[0]).astype(BF16)
    vs_ref[...] = dot(xk_ref[0], wv_ref[0]).astype(BF16)
    kl_ref[:rows] = dot(xk_ref[1], wk_ref[0]).astype(BF16)
    vl_ref[:rows] = dot(xk_ref[1], wv_ref[0]).astype(BF16)
    kl_ref[rows:] = dot(mate_ref[...], wk_ref[0]).astype(BF16)
    vl_ref[rows:] = dot(mate_ref[...], wv_ref[0]).astype(BF16)
    everything = slice(None)
    bias = scores_bias(bias_l_ref, 0, rows, causal)
    attend_rows(
        bias, q_ref.at[1], kl_ref, vl_ref, el_ref, o_ref.at[1], inv_ref.at[1], everything, everything
    )
    for slot in range(rows // SHORT):
        bias = scores_bias(bias_s_ref, slot, SHORT, causal)
        here = slice(slot * SHORT, (slot + 1) * SHORT)
        attend_rows(
            bias, q_ref.at[0], ks_ref, vs_ref, es_ref, o_ref.at[0], inv_ref.at[0], here, here
        )


def attend(queries, keys, mate, weights, base, bias_s, bias_l, causal):
    _, rows, width = queries.shape
    self_keys = keys is None
    heads = width // 64
    weight = lambda index: pl.BlockSpec((1, width, COLS), lambda step: (index, 0, step))
    both = pl.BlockSpec((2, rows, COLS), lambda step: (0, 0, step))
    cols = lambda count: pl.BlockSpec((count, COLS), lambda step: (0, step))
    powers = lambda count: pl.BlockSpec((COLS // 64, rows, count), lambda step: (step, 0, 0))
    xs = (queries,) if self_keys else (queries, keys)
    flops = 2 * rows * width * width * 7 + 4 * rows * width * (SHORT + LONG)
    return pl.pallas_call(
        functools.partial(attend_kernel, causal, self_keys),
        grid=(width // COLS,),
        out_shape=(
            shaped((2, rows, width), BF16),
            shaped((2, rows, width), F32),
            shaped((2, rows, width), BF16),
            shaped((rows, width), BF16),
            shaped((rows, width), BF16),
            shaped((LONG, width), BF16),
            shaped((LONG, width), BF16),
            shaped((heads, rows, SHORT), BF16),
            shaped((heads, rows, LONG), BF16),
        ),
        in_specs=[whole(x) for x in xs]
        + [whole(mate)]
        + [weight(base), weight(base + 1), weight(base + 2)]
        + [whole(bias_s), whole(bias_l)],
        out_specs=(
            both,
            both,
            both,
            cols(rows),
            cols(rows),
            cols(LONG),
            cols(LONG),
            powers(SHORT),
            powers(LONG),
        ),
        compiler_params=params(),
        cost_estimate=cost(flops * 2, 22 << 20, heads * rows * (SHORT + LONG)),
        name="attend",
    )(*xs, mate, weights, weights, weights, bias_s, bias_l)


def attend_back_rows(
    do_ref,
    o_ref,
    inv_ref,
    q_ref,
    k_ref,
    v_ref,
    e_ref,
    dq_ref,
    dk_ref,
    dv_ref,
    rows,
    keys,
    pair,
    scale,
):
    cols = slice(pair * 128, pair * 128 + 128)
    grad = do_ref[rows, cols].astype(F32) * inv_ref[rows, cols]
    product = grad * o_ref[rows, cols].astype(F32)
    grad_low = grad.astype(BF16)
    queries = q_ref[rows, cols]
    key_pair = k_ref[keys, cols]
    value_pair = v_ref[keys, cols]
    grad_turned = grad.T.astype(BF16)
    queries_turned = queries.astype(F32).T.astype(BF16)
    grad_q, grad_k, grad_v = [], [], []
    for which in range(2):
        inner = jnp.sum(one_head(which, product), axis=1, keepdims=True)
        grad_probs = dot(one_head(which, grad_low), value_pair, NT)
        powers = e_ref[pair * 2 + which, rows, :]
        grad_scores = (powers.astype(F32) * (grad_probs - inner)).astype(BF16)
        grad_q.append(dot(grad_scores, key_pair))
        head = slice(which * 64, which * 64 + 64)
        grad_v.append(dot(grad_turned[head], powers))
        grad_k.append(dot(queries_turned[head], grad_scores))
    dq_ref[rows, cols] = (join_heads(*grad_q) * scale).astype(BF16)
    dk_ref[keys, cols] = jnp.concatenate(grad_k, axis=0).T.astype(BF16)
    dv_ref[keys, cols] = jnp.concatenate(grad_v, axis=0).T.astype(BF16)


def attend_back_kernel(self_keys, tick, *refs):
    (
        do_ref,
        o_ref,
        inv_ref,
        q_ref,
        ks_ref,
        vs_ref,
        kl_ref,
        vl_ref,
        es_ref,
        el_ref,
        resid_ref,
        xq_ref,
        *rest,
    ) = refs
    xk_ref = xq_ref if self_keys else rest.pop(0)
    mate_ref, wq_ref, wk_ref, wv_ref, *rest = rest
    dx_ref = rest.pop(0)
    dy_ref = dx_ref if self_keys else rest.pop(0)
    dmate_ref, dwq_ref, dwk_ref, dwv_ref, dqs, dks, dvs, dql, dkl, dvl, mate_sum = rest
    rows = xq_ref.shape[1]
    scale = 0.125
    everything = slice(None)
    tick(0)
    for pair in range(COLS // 128):
        attend_back_rows(
            do_ref.at[1],
            o_ref.at[1],
            inv_ref.at[1],
            q_ref.at[1],
            kl_ref,
            vl_ref,
            el_ref,
            dql,
            dkl,
            dvl,
            everything,
            everything,
            pair,
            scale,
        )
        tick(1 + pair)
    for slot in range(rows // SHORT):
        here = slice(slot * SHORT, (slot + 1) * SHORT)
        for pair in range(COLS // 128):
            attend_back_rows(
                do_ref.at[0],
                o_ref.at[0],
                inv_ref.at[0],
                q_ref.at[0],
                ks_ref,
                vs_ref,
                es_ref,
                dqs,
                dks,
                dvs,
                here,
                here,
                pair,
                scale,
            )
    tick(3)
    wq, wk, wv = wq_ref[0], wk_ref[0], wv_ref[0]

    @pl.when(pl.program_id(0) == 0)
    def _():
        dx_ref[...] = resid_ref[...]
        if not self_keys:
            dy_ref[...] = jnp.zeros_like(dy_ref)
        mate_sum[...] = jnp.zeros_like(mate_sum)

    own = slice(0, rows)
    other = slice(rows, 2 * rows)
    dx_ref[0] += dot(dqs[...], wq, NT)
    dx_ref[1] += dot(dql[...], wq, NT)
    dy_ref[0] += dot(dks[...], wk, NT) + dot(dvs[...], wv, NT)
    dy_ref[1] += dot(dkl[own], wk, NT) + dot(dvl[own], wv, NT)
    mate_sum[...] += dot(dkl[other], wk, NT) + dot(dvl[other], wv, NT)
    dwq_ref[...] = (dot(xq_ref[0], dqs[...], TN) + dot(xq_ref[1], dql[...], TN)).astype(BF16)
    short, long, mate = xk_ref[0], xk_ref[1], mate_ref[...]
    dwk_ref[...] = (
        dot(short, dks[...], TN) + dot(long, dkl[own], TN) + dot(mate, dkl[other], TN)
    ).astype(BF16)
    dwv_ref[...] = (
        dot(short, dvs[...], TN) + dot(long, dvl[own], TN) + dot(mate, dvl[other], TN)
    ).astype(BF16)

    tick(4)

    @pl.when(pl.program_id(0) == pl.num_programs(0) - 1)
    def _():
        dmate_ref[...] = mate_sum[...].astype(BF16)


def attend_back(grad, saved, resid, queries, keys, mate, weights, base, flows, plan, collective):
    _, rows, width = queries.shape
    self_keys = keys is None
    weight = lambda index: (weights, pl.BlockSpec((1, width, COLS), lambda step: (index, 0, step)))
    both = pl.BlockSpec((2, rows, COLS), lambda step: (0, 0, step))
    cols = lambda count: pl.BlockSpec((count, COLS), lambda step: (0, step))
    powers = lambda count: pl.BlockSpec((COLS // 64, rows, count), lambda step: (step, 0, 0))
    full = pl.BlockSpec((2, rows, width), lambda step: (0, 0, 0))
    xs = (queries,) if self_keys else (queries, keys)
    flops = 2 * rows * width * width * 14 + 8 * rows * width * (SHORT + LONG)
    specs = [both] * 4 + [cols(rows)] * 2 + [cols(LONG)] * 2 + [powers(SHORT), powers(LONG)]
    o, inverse, *rest = saved
    return call(
        functools.partial(attend_back_kernel, self_keys),
        width // COLS,
        list(zip((grad, o, inverse, *rest), specs))
        + [(array, whole(array)) for array in (resid, *xs, mate)]
        + [weight(base), weight(base + 1), weight(base + 2)],
        [(shaped((2, rows, width), F32), full)] * len(xs)
        + [(shaped((rows, width), BF16), pl.BlockSpec((rows, width), lambda step: (0, 0)))]
        + [(shaped((width, width), BF16), cols(width))] * 3,
        [pltpu.VMEM((rows, COLS), BF16)] * 4
        + [pltpu.VMEM((LONG, COLS), BF16)] * 2
        + [pltpu.VMEM((rows, width), F32)],
        "attend_back",
        cost(flops * 2, 28 << 20),
        flows,
        plan,
        collective,
    )


def norm_parts(resid):
    average = jnp.mean(resid, axis=-1, keepdims=True)
    centered = resid - average
    variance = jnp.mean(centered * centered, axis=-1, keepdims=True)
    spread = lax.rsqrt(variance + EPSILON)
    return centered * spread, spread


def norm_back(normal, spread, gain, grad):
    scaled = grad * gain
    first = jnp.mean(scaled, axis=-1, keepdims=True)
    second = jnp.mean(scaled * normal, axis=-1, keepdims=True)
    return (scaled - first - normal * second) * spread


def add_norm_grads(ref, place, grad, normal):
    ref[place : place + 1, :] += jnp.sum(grad * normal, axis=0, keepdims=True)
    ref[place + 1 : place + 2, :] += jnp.sum(grad, axis=0, keepdims=True)


def logistic(value):
    return 1.0 / (1.0 + jnp.exp(-value))


def feed_kernel(chunks, o_ref, x_ref, wo_ref, up_ref, down_ref, gain_ref, shift_ref, r1_ref, u_ref, r2_ref, enc_ref):
    resid = x_ref[0].astype(F32) + dot(o_ref[0], wo_ref[0])
    r1_ref[0] = resid
    normal, _ = norm_parts(resid)
    hidden = normal * gain_ref[0:1] + shift_ref[0:1]
    hidden_low = hidden.astype(BF16)
    total = hidden
    for chunk in range(chunks):
        part = slice(chunk * CHUNK, (chunk + 1) * CHUNK)
        upward = dot(hidden_low, up_ref[0, :, part])
        u_ref[0, :, part] = upward
        active = (upward * logistic(upward)).astype(BF16)
        total = total + dot(active, down_ref[0, part, :])
    r2_ref[0] = total
    normal, _ = norm_parts(total)
    enc_ref[0] = (normal * gain_ref[1:2] + shift_ref[1:2]).astype(BF16)


def feed(o, x, attn, ups, downs, gains, shifts):
    _, rows, width = x.shape
    inner = ups.shape[2]
    row = lambda count: pl.BlockSpec((1, rows, count), lambda batch: (batch, 0, 0))
    pick = lambda array, index: pl.BlockSpec((1,) + array.shape[1:], lambda batch: (index, 0, 0))
    return pl.pallas_call(
        functools.partial(feed_kernel, inner // CHUNK),
        grid=(2,),
        out_shape=(
            shaped((2, rows, width), F32),
            shaped((2, rows, inner), F32),
            shaped((2, rows, width), F32),
            shaped((2, rows, width), BF16),
        ),
        in_specs=[row(width), row(width), pick(attn, 3), pick(ups, 0), pick(downs, 0), whole(gains), whole(shifts)],
        out_specs=(row(width), row(inner), row(width), row(width)),
        compiler_params=params(),
        cost_estimate=cost(4 * rows * width * (width + 2 * inner), 22 << 20, 2 * rows * inner),
        name="feed",
    )(o, x, attn, ups, downs, gains, shifts)


def middle_kernel(o_ref, x_ref, wo_ref, gain_ref, shift_ref, r_ref, low_ref):
    resid = x_ref[0].astype(F32) + dot(o_ref[0], wo_ref[0])
    r_ref[0] = resid
    normal, _ = norm_parts(resid)
    low_ref[0] = (normal * gain_ref[2:3] + shift_ref[2:3]).astype(BF16)


def middle(o, x, attn, gains, shifts):
    _, rows, width = x.shape
    row = lambda count: pl.BlockSpec((1, rows, count), lambda batch: (batch, 0, 0))
    pick = lambda array, index: pl.BlockSpec((1,) + array.shape[1:], lambda batch: (index, 0, 0))
    return pl.pallas_call(
        middle_kernel,
        grid=(2,),
        out_shape=(shaped((2, rows, width), F32), shaped((2, rows, width), BF16)),
        in_specs=[row(width), row(width), pick(attn, 7), whole(gains), whole(shifts)],
        out_specs=(row(width), row(width)),
        compiler_params=params(),
        cost_estimate=cost(4 * rows * width * width, 7 << 20),
        name="middle",
    )(o, x, attn, gains, shifts)


def feed_back_chunks(
    tick, chunks, grad, low, hidden_low, u_ref, a_ref, up_ref, down_ref, up_sum, down_sum
):
    total = grad
    for chunk in range(chunks):
        part = slice(chunk * CHUNK, (chunk + 1) * CHUNK)
        upward = u_ref[:, part]
        gate = logistic(upward)
        if a_ref is None:
            active = (upward * gate).astype(BF16)
        else:
            active = a_ref[:, part]
        grad_active = dot(low, down_ref[0, part, :], NT)
        grad_up = (grad_active * gate * (1.0 + upward * (1.0 - gate))).astype(BF16)
        down_sum[part, :] += dot(active, low, TN)
        up_sum[chunk] += dot(hidden_low, grad_up, TN)
        total = total + dot(grad_up, up_ref[0, :, part], NT)
        tick(1 + chunk)
    return total


def clear_first(*refs):
    @pl.when(pl.program_id(0) == 0)
    def _():
        for ref in refs:
            ref[...] = jnp.zeros_like(ref)


def write_last(*pairs):
    @pl.when(pl.program_id(0) == pl.num_programs(0) - 1)
    def _():
        for ref, total in pairs:
            ref[...] = total[...].astype(BF16)


def turn_kernel(
    chunks,
    tick,
    o_ref,
    r3_ref,
    cot_ref,
    wo_ref,
    up_ref,
    down_ref,
    gain_ref,
    shift_ref,
    out_ref,
    dr_ref,
    do_ref,
    dup_ref,
    ddown_ref,
    dwo_ref,
    norm_ref,
    u_s,
    a_s,
    up_sum,
    down_sum,
    wo_sum,
):
    clear_first(up_sum, down_sum, wo_sum, norm_ref)
    mixed = o_ref[0]
    normal3, _ = norm_parts(r3_ref[0])
    resid4 = normal3 * gain_ref[2:3] + shift_ref[2:3] + dot(mixed, wo_ref[0])
    normal4, spread4 = norm_parts(resid4)
    hidden = normal4 * gain_ref[3:4] + shift_ref[3:4]
    hidden_low = hidden.astype(BF16)
    total = hidden
    for chunk in range(chunks):
        part = slice(chunk * CHUNK, (chunk + 1) * CHUNK)
        upward = dot(hidden_low, up_ref[0, :, part])
        u_s[:, part] = upward
        active = (upward * logistic(upward)).astype(BF16)
        a_s[:, part] = active
        total = total + dot(active, down_ref[0, part, :])
    normal5, spread5 = norm_parts(total)
    out_ref[0] = (normal5 * gain_ref[4:5] + shift_ref[4:5]).astype(BF16)
    grad = cot_ref[0].astype(F32)
    add_norm_grads(norm_ref, 0, grad, normal5)
    grad = norm_back(normal5, spread5, gain_ref[4:5], grad)
    grad = feed_back_chunks(
        tick,
        chunks,
        grad,
        grad.astype(BF16),
        hidden_low,
        u_s,
        a_s,
        up_ref,
        down_ref,
        up_sum,
        down_sum,
    )
    add_norm_grads(norm_ref, 2, grad, normal4)
    grad = norm_back(normal4, spread4, gain_ref[3:4], grad)
    dr_ref[0] = grad
    low = grad.astype(BF16)
    wo_sum[...] += dot(mixed, low, TN)
    do_ref[0] = dot(low, wo_ref[0], NT).astype(BF16)
    write_last((dup_ref, up_sum), (ddown_ref, down_sum), (dwo_ref, wo_sum))


def turn(o, r3, cot, attn, ups, downs, gains, shifts):
    _, rows, width = r3.shape
    inner = ups.shape[2]
    chunks = inner // CHUNK
    row = pl.BlockSpec((1, rows, width), lambda batch: (batch, 0, 0))
    pick = lambda array, index: (array, pl.BlockSpec((1,) + array.shape[1:], lambda batch: (index, 0, 0)))
    still = lambda *shape: pl.BlockSpec(shape, lambda batch: (0,) * len(shape))
    out = lambda kind, *shape: (shaped(shape, kind), still(*shape))
    results, _ = call(
        functools.partial(turn_kernel, chunks),
        2,
        [(o, row), (r3, row), (cot, row), pick(attn, 11), pick(ups, 1), pick(downs, 1)]
        + [(gains, whole(gains)), (shifts, whole(shifts))],
        [
            (shaped((2, rows, width), BF16), row),
            (shaped((2, rows, width), F32), row),
            (shaped((2, rows, width), BF16), row),
            out(BF16, chunks, width, CHUNK),
            out(BF16, inner, width),
            out(BF16, width, width),
            out(F32, 8, width),
        ],
        [
            pltpu.VMEM((rows, inner), F32),
            pltpu.VMEM((rows, inner), BF16),
            pltpu.VMEM((chunks, width, CHUNK), F32),
            pltpu.VMEM((inner, width), F32),
            pltpu.VMEM((width, width), F32),
        ],
        "turn",
        cost(12 * rows * width * (width + 2 * inner), 20 << 20, 4 * rows * inner),
    )
    return results


def feed_back_kernel(
    chunks,
    tick,
    grad_ref,
    mate_ref,
    r2_ref,
    r1_ref,
    u_ref,
    o_ref,
    wo_ref,
    up_ref,
    down_ref,
    gain_ref,
    shift_ref,
    dr_ref,
    do_ref,
    dup_ref,
    ddown_ref,
    dwo_ref,
    norm_ref,
    grad_s,
    up_sum,
    down_sum,
    wo_sum,
):
    tick(0)
    clear_first(up_sum, down_sum, wo_sum, norm_ref)
    grad_s[...] = grad_ref[0]

    @pl.when(pl.program_id(0) == 1)
    def _():
        grad_s[...] += mate_ref[...].astype(F32)

    grad = grad_s[...]
    normal2, spread2 = norm_parts(r2_ref[0])
    add_norm_grads(norm_ref, 2, grad, normal2)
    grad = norm_back(normal2, spread2, gain_ref[1:2], grad)
    normal1, spread1 = norm_parts(r1_ref[0])
    hidden_low = (normal1 * gain_ref[0:1] + shift_ref[0:1]).astype(BF16)
    grad = feed_back_chunks(
        tick,
        chunks,
        grad,
        grad.astype(BF16),
        hidden_low,
        u_ref.at[0],
        None,
        up_ref,
        down_ref,
        up_sum,
        down_sum,
    )
    add_norm_grads(norm_ref, 0, grad, normal1)
    grad = norm_back(normal1, spread1, gain_ref[0:1], grad)
    dr_ref[0] = grad
    low = grad.astype(BF16)
    wo_sum[...] += dot(o_ref[0], low, TN)
    do_ref[0] = dot(low, wo_ref[0], NT).astype(BF16)
    write_last((dup_ref, up_sum), (ddown_ref, down_sum), (dwo_ref, wo_sum))


def feed_back(grad, mate, r2, r1, u, o, attn, ups, downs, gains, shifts, flows, plan, collective):
    _, rows, width = r1.shape
    inner = ups.shape[2]
    chunks = inner // CHUNK
    row = lambda count: pl.BlockSpec((1, rows, count), lambda batch: (batch, 0, 0))
    pick = lambda array, index: (array, pl.BlockSpec((1,) + array.shape[1:], lambda batch: (index, 0, 0)))
    still = lambda *shape: pl.BlockSpec(shape, lambda batch: (0,) * len(shape))
    out = lambda kind, *shape: (shaped(shape, kind), still(*shape))
    return call(
        functools.partial(feed_back_kernel, chunks),
        2,
        [(grad, row(width)), (mate, whole(mate)), (r2, row(width)), (r1, row(width)), (u, row(inner)), (o, row(width))]
        + [pick(attn, 3), pick(ups, 0), pick(downs, 0), (gains, whole(gains)), (shifts, whole(shifts))],
        [
            (shaped((2, rows, width), F32), row(width)),
            (shaped((2, rows, width), BF16), row(width)),
            out(BF16, chunks, width, CHUNK),
            out(BF16, inner, width),
            out(BF16, width, width),
            out(F32, 8, width),
        ],
        [
            pltpu.VMEM((rows, width), F32),
            pltpu.VMEM((chunks, width, CHUNK), F32),
            pltpu.VMEM((inner, width), F32),
            pltpu.VMEM((width, width), F32),
        ],
        "feed_back",
        cost(8 * rows * width * (width + 2 * inner), 30 << 20, 2 * rows * inner),
        flows,
        plan,
        collective,
    )


def middle_back_kernel(grad_ref, r_ref, o_ref, wo_ref, gain_ref, dr_ref, do_ref, dwo_ref, norm_ref, wo_sum):
    clear_first(wo_sum, norm_ref)
    grad = grad_ref[0]
    normal, spread = norm_parts(r_ref[0])
    add_norm_grads(norm_ref, 0, grad, normal)
    grad = norm_back(normal, spread, gain_ref[2:3], grad)
    dr_ref[0] = grad
    low = grad.astype(BF16)
    wo_sum[...] += dot(o_ref[0], low, TN)
    do_ref[0] = dot(low, wo_ref[0], NT).astype(BF16)
    write_last((dwo_ref, wo_sum))


def middle_back(grad, r, o, attn, gains):
    _, rows, width = r.shape
    row = pl.BlockSpec((1, rows, width), lambda batch: (batch, 0, 0))
    pick = lambda array, index: pl.BlockSpec((1,) + array.shape[1:], lambda batch: (index, 0, 0))
    still = lambda *shape: pl.BlockSpec(shape, lambda batch: (0,) * len(shape))
    return pl.pallas_call(
        middle_back_kernel,
        grid=(2,),
        out_shape=(
            shaped((2, rows, width), F32),
            shaped((2, rows, width), BF16),
            shaped((width, width), BF16),
            shaped((8, width), F32),
        ),
        in_specs=[row, row, row, pick(attn, 7), whole(gains)],
        out_specs=(row, row, still(width, width), still(8, width)),
        scratch_shapes=[pltpu.VMEM((width, width), F32)],
        compiler_params=params(),
        cost_estimate=cost(8 * rows * width * width, 12 << 20),
        name="middle_back",
    )(grad, r, o, attn, gains)


def tail_kernel(slots, tick):
    for slot in range(slots):
        tick(slot)


def swap(array, bit):
    count = lax.axis_size("dp") * lax.axis_size("head")
    return lax.ppermute(array, AXES, [(place, place ^ (1 << bit)) for place in range(count)])


def sum_everywhere(array, bits):
    for bit in range(bits):
        array = array + swap(array, bit)
    return array


def body(
    source,
    target,
    cotangent,
    short_lengths,
    long_lengths,
    attn,
    ups,
    downs,
    gains,
    shifts,
):
    _, rows, width = source.shape
    inner = ups.shape[2]
    devices = lax.axis_size("dp") * lax.axis_size("head")
    bits = devices.bit_length() - 1
    assert 2 * rows == LONG and rows % SHORT == 0 and devices == 1 << bits
    place = lax.axis_index("head")
    half = place % 2
    slots = rows // SHORT
    share = width // devices
    parts = (2,) * bits

    def biases(row, causal):
        short = lax.dynamic_slice_in_dim(short_lengths[row], place * slots, slots)
        bias_s = jnp.where(jnp.arange(SHORT)[None, :] < short[:, None], 0.0, MASKED).astype(F32)
        length = lax.dynamic_index_in_dim(long_lengths[row], place // 2, keepdims=False)
        position = jnp.arange(rows)
        own = position + half * rows < length
        other = position + (1 - half) * rows < length
        if causal:
            other = other & (half == 1)
        allowed = jnp.concatenate([own, other])[None, :]
        return bias_s, jnp.where(allowed, 0.0, MASKED).astype(F32)

    first = tuple(range(bits))
    second = (0, 2, 1) + tuple(range(3, bits))

    def square(array):
        return array.reshape(parts + (1, share, width)), None

    def tall(array):
        return array.reshape(parts + (inner // width, share, width)), None

    def chunked(array):
        array = array.reshape(array.shape[:1] + parts + (1, share, array.shape[2]))
        return [(array, index) for index in range(array.shape[0])]

    def ffn_flows(dup, ddown, dwo):
        pieces = (chunked(dup) + [square(dwo)], [tall(ddown)])
        return [Flow(order, 0, 2, piece) for order, piece in zip((first, second), pieces)]

    def later(partial):
        return [Flow(order, 2, bits, [(part, None)]) for order, part in zip((first, second), partial)]

    def attn_flows(left, right):
        pieces = ([square(array) for array in left], [square(array) for array in right])
        return [Flow(order, 0, bits, piece) for order, piece in zip((first, second), pieces)]

    ffn_plan = {(0, 0): [(0, None), (1, None)], (0, 2): [(0, 0), (1, 0)], (1, 3): [(0, 1), (1, 1)]}

    def mixed_plan(spots):
        plan = {(0, 0): [(number, None) for number in range(4)]}
        late, early = spots
        for numbers, stages, places in (((2, 3), range(bits), early), ((0, 1), range(2, bits), late)):
            for stage in stages:
                spot = places[min(stage - stages[0], len(places) - 1)]
                plan.setdefault(spot, []).extend((number, stage) for number in numbers)
        return plan

    source_bias = biases(0, False)
    target_bias = biases(1, True)
    source_mate = swap(source[1], 0)
    target_mate = swap(target[1], 0)

    enc_saved = attend(source, None, source_mate, attn, 0, *source_bias, False)
    r1, u, r2, enc = feed(enc_saved[0], source, attn, ups, downs, gains, shifts)
    enc_mate = swap(enc[1], 0)
    self_saved = attend(target, None, target_mate, attn, 4, *target_bias, True)
    r3, h3 = middle(self_saved[0], target, attn, gains, shifts)
    cross_saved = attend(h3, enc, enc_mate, attn, 8, *source_bias, False)
    decoded, dr4, do_cross, dup1, ddown1, dw11, norms_a = turn(
        cross_saved[0], r3, cotangent, attn, ups, downs, gains, shifts
    )
    (dh3, denc, denc_mate, dw8, dw9, dw10), partial = attend_back(
        do_cross,
        cross_saved,
        dr4,
        h3,
        enc,
        enc_mate,
        attn,
        8,
        ffn_flows(dup1, ddown1, dw11),
        ffn_plan,
        0,
    )
    denc_mate = swap(denc_mate, 0)
    dr3, do_self, dw7, norms_b = middle_back(dh3, r3, self_saved[0], attn, gains)
    (dr1, do_enc, dup0, ddown0, dw3, norms_c), sums_a = feed_back(
        denc,
        denc_mate,
        r2,
        r1,
        u,
        enc_saved[0],
        attn,
        ups,
        downs,
        gains,
        shifts,
        later(partial) + attn_flows([dw8], [dw9, dw10]),
        mixed_plan(([(0, 3), (1, 1), (1, 3)], [(0, 1), (0, 2), (0, 4), (1, 2), (1, 4)])),
        1,
    )
    (grad_source, ds_mate, dw0, dw1, dw2), partial = attend_back(
        do_enc,
        enc_saved,
        dr1,
        source,
        None,
        source_mate,
        attn,
        0,
        ffn_flows(dup0, ddown0, dw3),
        ffn_plan,
        2,
    )
    ds_mate = swap(ds_mate, 0)
    (grad_target, dt_mate, dw4, dw5, dw6), sums_b = attend_back(
        do_self,
        self_saved,
        dr3,
        target,
        None,
        target_mate,
        attn,
        4,
        later(partial) + attn_flows([dw0], [dw1, dw2]),
        mixed_plan(([(0, 2), (1, 0), (1, 2)], [(0, 1), (0, 3), (0, 4), (1, 1), (1, 3)])),
        3,
    )
    dt_mate = swap(dt_mate, 0)
    _, sums_c = call(
        functools.partial(tail_kernel, bits + 1),
        1,
        [],
        [],
        [],
        "tail",
        cost(0, 4 << 20),
        attn_flows([dw7, dw4], [dw5, dw6]),
        {(0, 0): [(0, None), (1, None)]}
        | {(0, 1 + stage): [(0, stage), (1, stage)] for stage in range(bits)},
        4,
    )
    grad_source = grad_source.at[1].add(ds_mate.astype(F32))
    grad_target = grad_target.at[1].add(dt_mate.astype(F32))

    up1, down1, (dw8,), (dw9, dw10) = sums_a
    up0, down0, (dw0,), (dw1, dw2) = sums_b
    (dw7, dw4), (dw5, dw6) = sums_c
    count = dup0.shape[0]
    dw11, dw3 = up1[count], up0[count]
    grad_attn = jnp.stack([dw0, dw1, dw2, dw3, dw4, dw5, dw6, dw7, dw8, dw9, dw10, dw11])
    grad_up = jnp.stack(
        [jnp.transpose(up[:count], (1, 0, 2)).reshape(share, inner) for up in (up0, up1)]
    )
    grad_down = jnp.stack([down.reshape(inner // devices, width) for down in (down0, down1)])
    norms = jnp.stack(
        [
            norms_c[0],
            norms_c[2],
            norms_b[0],
            norms_a[2],
            norms_a[0],
            norms_c[1],
            norms_c[3],
            norms_b[1],
            norms_a[3],
            norms_a[1],
        ]
    )
    norms = sum_everywhere(norms, bits)
    here = place + lax.axis_index("dp") * lax.axis_size("head")
    norms = lax.dynamic_slice_in_dim(norms, here * share, share, axis=1)
    return (
        decoded,
        grad_source,
        grad_target,
        grad_attn,
        grad_up,
        grad_down,
        norms[:5],
        norms[5:],
    )


def solution(mesh):
    rows = P(None, AXES, None)
    return jax.shard_map(
        body,
        mesh=mesh,
        in_specs=(rows, rows, rows, P(None, "dp"), P(None, "dp"), P(), P(), P(), P(), P()),
        out_specs=(rows, rows, rows, rows, rows, rows, P(None, AXES), P(None, AXES)),
        check_vma=False,
    )
```

```python
import functools
import math

import jax
import jax.numpy as jnp
from jax import lax
from jax.experimental import pallas as pl
from jax.experimental.pallas import tpu as pltpu
from jax.sharding import PartitionSpec as P

HEADS = 8
SHORT = 256
LONG = 1024

EPSILON = 1e-05
MASKED = -1e30
F32 = jnp.float32
BF16 = jnp.bfloat16
AXES = ("dp", "head")
COLS = 256
CHUNK = 512

NN = (((1,), (0,)), ((), ()))
NT = (((1,), (1,)), ((), ()))
TN = (((0,), (0,)), ((), ()))


def dot(left, right, dims=NN):
    return lax.dot_general(left, right, dims, preferred_element_type=F32)


def params():
    return pltpu.CompilerParams(vmem_limit_bytes=63 << 20)


def cost(flops, moved, powers=0):
    return pl.CostEstimate(flops=int(flops), bytes_accessed=int(moved), transcendentals=int(powers))


def whole(array):
    return pl.BlockSpec(array.shape, lambda *step: (0,) * array.ndim)


def shaped(shape, kind):
    return jax.ShapeDtypeStruct(shape, kind)


def lanes():
    return lax.broadcasted_iota(jnp.int32, (1, 128), 1)


def one_head(which, pair):
    keep = (lanes() < 64) if which == 0 else (lanes() >= 64)
    return jnp.where(keep, pair, jnp.zeros_like(pair))


def join_heads(first, second):
    return jnp.where(lanes() < 64, first, second)


MESH = pl.DeviceIdType.MESH


def partner(bit):
    head_bits = lax.axis_size("head").bit_length() - 1
    data, head = lax.axis_index("dp"), lax.axis_index("head")
    if bit < head_bits:
        step = 1 << bit
        mine = (head // step) % 2
        return mine, (data, head + (1 - 2 * mine) * step)
    step = 1 << (bit - head_bits)
    mine = (data // step) % 2
    return mine, (data + (1 - 2 * mine) * step, head)


class Flow:
    def __init__(self, order, first, last, pieces, block=None):
        self.order, self.first, self.last = order, first, last
        self.bits = order[first:last]
        self.local = block is not None
        self.arrays = []
        self.pieces = []
        total = 0
        for array, lead, start, count in pieces:
            known = [index for index, other in enumerate(self.arrays) if other is array]
            if not known:
                self.arrays.append(array)
            index = known[0] if known else len(self.arrays) - 1
            self.pieces.append((index, lead, start, total, count))
            total += count
        self.block = block or (total,) + pieces[0][0].shape[-2:]

    def shape(self, stage):
        return (2,) * (len(self.order) - stage) + self.block

    def out(self):
        done = self.last == len(self.order)
        return shaped(self.shape(self.last), F32 if done else BF16)

    def scratch(self):
        stages = range(self.first, self.last)
        count = len(self.pieces)
        dma = pltpu.SemaphoreType.DMA
        return (
            [pltpu.VMEM(self.shape(self.first + (0 if self.local else 1)), BF16)]
            + [pltpu.VMEM(self.shape(stage + 1), BF16) for stage in stages]
            + [pltpu.VMEM(self.shape(stage + 1), BF16) for stage in stages[:-1]]
            + [dma((len(stages),)), dma((len(stages),))]
            + [dma((count,)) for _ in range(0 if self.local else 3)]
        )

    def bind(self, inputs, out, scratch):
        stages = range(self.first, self.last)
        self.in_refs, self.out_ref = inputs, out
        self.own = scratch[0]
        self.got = dict(zip(stages, scratch[1 : 1 + len(stages)]))
        self.sum = dict(zip(stages[:-1], scratch[1 + len(stages) :]))
        if self.local:
            self.send, self.recv = scratch[-2:]
            self.source = self.own
        else:
            self.send, self.recv, self.local_sem, self.piece_send, self.piece_recv = scratch[-5:]

    def where(self, stage, index):
        left = sorted(self.order[stage:])
        place = len(left) - 1 - left.index(self.order[stage])
        return (slice(None),) * place + (index,)

    def piece_copies(self):
        stage = self.first
        mine, device = partner(self.order[stage])
        left = len(self.order) - stage
        for number, (index, lead, start, total, count) in enumerate(self.pieces):
            prefix = () if lead is None else (lead,)
            target = (slice(None),) * (left - 1) + (slice(total, total + count),)
            ref = self.in_refs[index]

            def part(value):
                at = self.where(stage, value)
                at += (slice(None),) * (left - len(at)) + (slice(start, start + count),)
                return ref.at[prefix + at]

            yield pltpu.make_async_remote_copy(
                src_ref=part(1 - mine),
                dst_ref=self.got[stage].at[target],
                send_sem=self.piece_send.at[number],
                recv_sem=self.piece_recv.at[number],
                device_id=device,
                device_id_type=MESH,
            )
            yield pltpu.make_async_copy(
                part(mine),
                self.own.at[target],
                self.local_sem.at[number],
            )

    def stage_copy(self, stage):
        mine, device = partner(self.order[stage])
        source = self.source if stage == self.first else self.sum[stage - 1]
        return pltpu.make_async_remote_copy(
            src_ref=source.at[self.where(stage, 1 - mine)],
            dst_ref=self.got[stage],
            send_sem=self.send.at[stage - self.first],
            recv_sem=self.recv.at[stage - self.first],
            device_id=device,
            device_id_type=MESH,
        )

    def start(self):
        if self.local:
            self.stage_copy(self.first).start()
        else:
            for copy in self.piece_copies():
                copy.start()

    def step(self, stage):
        mine, _ = partner(self.order[stage])
        if stage > self.first:
            self.stage_copy(stage).wait()
            kept = self.sum[stage - 1][self.where(stage, mine)]
        elif self.local:
            self.stage_copy(stage).wait()
            kept = self.source[self.where(stage, mine)]
        else:
            for copy in self.piece_copies():
                copy.wait()
            kept = self.own[...]
        if stage == len(self.order) - 1:
            self.out_ref[...] = kept.astype(F32) + self.got[stage][...].astype(F32)
        elif stage == self.last - 1:
            self.out_ref[...] = kept + self.got[stage][...]
        else:
            self.sum[stage][...] = kept + self.got[stage][...]
            self.stage_copy(stage + 1).start()


class Swap:
    def __init__(self, bit, shape, array=None, kept=True):
        self.bits = (bit,)
        self.wide = shape
        self.kept = kept
        self.arrays = [] if array is None else [array]

    def out(self):
        return shaped(self.wide, BF16) if self.kept else None

    def scratch(self):
        return [pltpu.VMEM(self.wide, BF16), pltpu.SemaphoreType.DMA, pltpu.SemaphoreType.DMA]

    def bind(self, inputs, out, scratch):
        self.source = inputs[0] if inputs else None
        self.out_ref = out
        self.got, self.send, self.recv = scratch

    def copy(self):
        return pltpu.make_async_remote_copy(
            src_ref=self.source,
            dst_ref=self.got,
            send_sem=self.send,
            recv_sem=self.recv,
            device_id=partner(self.bits[0])[1],
            device_id_type=MESH,
        )

    def start(self):
        self.copy().start()

    def step(self, stage):
        self.copy().wait()
        if self.kept:
            self.out_ref[...] = self.got[...]


class Total:
    def __init__(self, bits, arrays):
        self.bits = tuple(range(bits))
        self.arrays = []
        self.terms = arrays

    def out(self):
        return shaped(self.terms[0].shape, F32)

    def scratch(self):
        count = len(self.bits)
        whole_shape = (count,) + self.terms[0].shape
        dma = pltpu.SemaphoreType.DMA((count,))
        return [pltpu.VMEM(whole_shape, F32), pltpu.VMEM(whole_shape, F32), dma, dma]

    def bind(self, inputs, out, scratch):
        self.out_ref = out
        self.held, self.got, self.send, self.recv = scratch

    def copy(self, stage):
        return pltpu.make_async_remote_copy(
            src_ref=self.held.at[stage],
            dst_ref=self.got.at[stage],
            send_sem=self.send.at[stage],
            recv_sem=self.recv.at[stage],
            device_id=partner(stage)[1],
            device_id_type=MESH,
        )

    def start(self):
        self.held[0] = functools.reduce(lambda left, right: left + right, [ref[...] for ref in self.refs])
        self.copy(0).start()

    def step(self, stage):
        self.copy(stage).wait()
        total = self.held[stage] + self.got[stage]
        if stage == len(self.bits) - 1:
            self.out_ref[...] = total
        else:
            self.held[stage + 1] = total
            self.copy(stage + 1).start()


def greet(bits):
    ready = pltpu.get_barrier_semaphore()
    for bit in bits:
        _, device = partner(bit)
        pl.semaphore_signal(ready, inc=1, device_id=device, device_id_type=MESH)
    pl.semaphore_wait(ready, len(bits))


def call(kernel, steps, ins, outs, scratch, name, estimate, flows=(), plan=None, collective=None):
    extra_in = [array for flow in flows for array in flow.arrays]
    bits = sorted({bit for flow in flows for bit in flow.bits})
    counts = (len(ins), len(outs), len(scratch))

    def body(*refs):
        refs = list(refs)
        take = lambda count: [refs.pop(0) for _ in range(count)]
        main = take(counts[0])
        inputs = [take(len(flow.arrays)) for flow in flows]
        main += take(counts[1])
        results = [take(1)[0] if flow.out() else None for flow in flows]
        main += take(counts[2])
        for flow, given, result in zip(flows, inputs, results):
            flow.bind(given, result, take(len(flow.scratch())))

        def tick(slot):
            for (step, place), actions in (plan or {}).items():
                if place == slot:

                    @pl.when(pl.program_id(0) == step)
                    def _():
                        if (step, slot) == (0, 0):
                            greet(bits)
                        for number, stage in actions:
                            if stage is None:
                                flows[number].start()
                            else:
                                flows[number].step(stage)

        kernel(tick, *main)

    still = lambda shape: pl.BlockSpec(shape, lambda step: (0,) * len(shape))
    given_out = [flow.out() for flow in flows if flow.out()]
    remote = dict(collective_id=collective, has_side_effects=True) if flows else {}
    result = pl.pallas_call(
        body,
        grid=(steps,),
        out_shape=[shape for shape, _ in outs] + given_out,
        in_specs=[spec for _, spec in ins] + [pl.BlockSpec(memory_space=pl.ANY)] * len(extra_in),
        out_specs=[spec for _, spec in outs] + [still(shape.shape) for shape in given_out],
        scratch_shapes=list(scratch) + [shape for flow in flows for shape in flow.scratch()],
        compiler_params=pltpu.CompilerParams(vmem_limit_bytes=63 << 20, **remote),
        cost_estimate=estimate,
        name=name,
    )(*[array for array, _ in ins], *extra_in)
    return result[: len(outs)], result[len(outs) :]


def scores_bias(own_length, other_length, width, causal):
    row = lax.broadcasted_iota(jnp.int32, (width if causal else 1, width), 0)
    column = lax.broadcasted_iota(jnp.int32, (width if causal else 1, width), 1)
    allowed = column < own_length
    if causal:
        allowed = allowed & (column <= row)
    own = jnp.where(allowed, 0.0, MASKED).astype(F32)
    if other_length is None:
        return own
    other = jnp.where(column < other_length, 0.0, MASKED).astype(F32)
    return jnp.concatenate([own, other], axis=1)


def attend_rows(bias, q_ref, k_ref, v_ref, e_ref, o_ref, inv_ref, rows, keys):
    count = bias.shape[1]
    ones = jnp.ones((count, 128), BF16)
    for pair in range(COLS // 128):
        cols = slice(pair * 128, pair * 128 + 128)
        queries = q_ref[rows, cols]
        key_pair = k_ref[keys, cols]
        value_ext = jnp.concatenate([v_ref[keys, cols], ones], axis=1)
        outs, inverses = [], []
        for which in range(2):
            scores = dot(one_head(which, queries), key_pair, NT) + bias
            highest = jnp.max(scores, axis=1, keepdims=True)
            powers = jnp.exp(scores - highest).astype(BF16)
            e_ref[pair * 2 + which, rows, :] = powers
            mixed = dot(powers, value_ext)
            inverse = 1.0 / mixed[:, 128:]
            outs.append(mixed[:, :128] * inverse)
            inverses.append(inverse)
        o_ref[rows, cols] = join_heads(*outs).astype(BF16)
        inv_ref[rows, cols] = join_heads(*inverses)


def attend_kernel(causal, self_keys, mate, tick, *refs):
    xq_ref, *rest = refs
    xk_ref = xq_ref if self_keys else rest.pop(0)
    (
        short_ref,
        long_ref,
        wq_ref,
        wk_ref,
        wv_ref,
        o_ref,
        inv_ref,
        q_ref,
        ks_ref,
        vs_ref,
        kl_ref,
        vl_ref,
        es_ref,
        el_ref,
    ) = rest
    rows = xq_ref.shape[1]
    scale = 0.125
    kind = 1 if causal else 0
    place = lax.axis_index("head")
    half = place % 2
    mate.source = xk_ref.at[1]
    tick(0)
    q_ref[0] = (dot(xq_ref[0], wq_ref[0]) * scale).astype(BF16)
    ks_ref[...] = dot(xk_ref[0], wk_ref[0]).astype(BF16)
    vs_ref[...] = dot(xk_ref[0], wv_ref[0]).astype(BF16)
    slots = rows // SHORT
    for slot in range(slots):
        length = short_ref[kind, place * slots + slot]
        bias = scores_bias(length, None, SHORT, causal)
        here = slice(slot * SHORT, (slot + 1) * SHORT)
        attend_rows(
            bias, q_ref.at[0], ks_ref, vs_ref, es_ref, o_ref.at[0], inv_ref.at[0], here, here
        )
    q_ref[1] = (dot(xq_ref[1], wq_ref[0]) * scale).astype(BF16)
    kl_ref[:rows] = dot(xk_ref[1], wk_ref[0]).astype(BF16)
    vl_ref[:rows] = dot(xk_ref[1], wv_ref[0]).astype(BF16)
    tick(1)
    kl_ref[rows:] = dot(mate.got[...], wk_ref[0]).astype(BF16)
    vl_ref[rows:] = dot(mate.got[...], wv_ref[0]).astype(BF16)
    everything = slice(None)
    length = long_ref[kind, place // 2]
    other = length - (1 - half) * rows
    if causal:
        other = other * half
    bias = scores_bias(length - half * rows, other, rows, causal)
    attend_rows(
        bias, q_ref.at[1], kl_ref, vl_ref, el_ref, o_ref.at[1], inv_ref.at[1], everything, everything
    )


def attend(queries, keys, weights, base, lengths, causal, collective):
    _, rows, width = queries.shape
    self_keys = keys is None
    heads = width // 64
    weight = lambda index: (weights, pl.BlockSpec((1, width, COLS), lambda step: (index, 0, step)))
    both = pl.BlockSpec((2, rows, COLS), lambda step: (0, 0, step))
    cols = lambda count: (shaped((count, width), BF16), pl.BlockSpec((count, COLS), lambda step: (0, step)))
    powers = lambda count: (
        shaped((heads, rows, count), BF16),
        pl.BlockSpec((COLS // 64, rows, count), lambda step: (step, 0, 0)),
    )
    xs = (queries,) if self_keys else (queries, keys)
    flops = 2 * rows * width * width * 7 + 4 * rows * width * (SHORT + LONG)
    mate = Swap(0, (rows, width))
    saved, (other,) = call(
        functools.partial(attend_kernel, causal, self_keys, mate),
        width // COLS,
        [(array, whole(array)) for array in xs]
        + [(array, pl.BlockSpec(memory_space=pltpu.SMEM)) for array in lengths]
        + [weight(base), weight(base + 1), weight(base + 2)],
        [
            (shaped((2, rows, width), BF16), both),
            (shaped((2, rows, width), F32), both),
            (shaped((2, rows, width), BF16), both),
            cols(rows),
            cols(rows),
            cols(LONG),
            cols(LONG),
            powers(SHORT),
            powers(LONG),
        ],
        [],
        "attend",
        cost(flops * 2, 22 << 20, heads * rows * (SHORT + LONG)),
        [mate],
        {(0, 0): [(0, None)], (0, 1): [(0, 0)]},
        collective,
    )
    return saved, other


def attend_back_rows(
    do_ref,
    o_ref,
    inv_ref,
    q_ref,
    k_ref,
    v_ref,
    e_ref,
    dq_ref,
    dk_ref,
    dv_ref,
    rows,
    keys,
    pair,
    scale,
):
    cols = slice(pair * 128, pair * 128 + 128)
    grad = do_ref[rows, cols].astype(F32) * inv_ref[rows, cols]
    product = grad * o_ref[rows, cols].astype(F32)
    grad_low = grad.astype(BF16)
    queries = q_ref[rows, cols]
    key_pair = k_ref[keys, cols]
    value_pair = v_ref[keys, cols]
    grad_turned = grad.T.astype(BF16)
    queries_turned = queries.astype(F32).T.astype(BF16)
    grad_q, grad_k, grad_v = [], [], []
    for which in range(2):
        inner = jnp.sum(one_head(which, product), axis=1, keepdims=True)
        grad_probs = dot(one_head(which, grad_low), value_pair, NT)
        powers = e_ref[pair * 2 + which, rows, :]
        grad_scores = (powers.astype(F32) * (grad_probs - inner)).astype(BF16)
        grad_q.append(dot(grad_scores, key_pair))
        head = slice(which * 64, which * 64 + 64)
        grad_v.append(dot(grad_turned[head], powers))
        grad_k.append(dot(queries_turned[head], grad_scores))
    dq_ref[rows, cols] = (join_heads(*grad_q) * scale).astype(BF16)
    dk_ref[keys, cols] = jnp.concatenate(grad_k, axis=0).T.astype(BF16)
    dv_ref[keys, cols] = jnp.concatenate(grad_v, axis=0).T.astype(BF16)


def attend_back_kernel(self_keys, locals_, swap_back, total, after, tick, *refs):
    if total:
        total.refs = refs[: len(total.terms)]
        refs = refs[len(total.terms) :]
    (
        do_ref,
        o_ref,
        inv_ref,
        q_ref,
        ks_ref,
        vs_ref,
        kl_ref,
        vl_ref,
        es_ref,
        el_ref,
        resid_ref,
        xq_ref,
        *rest,
    ) = refs
    xk_ref = xq_ref if self_keys else rest.pop(0)
    mate_ref, wq_ref, wk_ref, wv_ref, *rest = rest
    dx_ref = rest.pop(0)
    dy_ref = dx_ref if self_keys else rest.pop(0)
    if locals_:
        dmate_ref = rest.pop()
        swap_back.source = dmate_ref
    else:
        dmate_ref, dwq_ref, dwk_ref, dwv_ref = rest[:4]
        rest = rest[4:]
    dqs, dks, dvs, dql, dkl, dvl, mate_sum = rest
    rows = xq_ref.shape[1]
    scale = 0.125
    everything = slice(None)
    tick(0)
    for pair in range(COLS // 128):
        attend_back_rows(
            do_ref.at[1],
            o_ref.at[1],
            inv_ref.at[1],
            q_ref.at[1],
            kl_ref,
            vl_ref,
            el_ref,
            dql,
            dkl,
            dvl,
            everything,
            everything,
            pair,
            scale,
        )
        tick(1 + pair)
    for slot in range(rows // SHORT):
        here = slice(slot * SHORT, (slot + 1) * SHORT)
        for pair in range(COLS // 128):
            attend_back_rows(
                do_ref.at[0],
                o_ref.at[0],
                inv_ref.at[0],
                q_ref.at[0],
                ks_ref,
                vs_ref,
                es_ref,
                dqs,
                dks,
                dvs,
                here,
                here,
                pair,
                scale,
            )
    tick(3)
    wq, wk, wv = wq_ref[0], wk_ref[0], wv_ref[0]
    own = slice(0, rows)
    other = slice(rows, 2 * rows)
    dwq = dot(xq_ref[0], dqs[...], TN) + dot(xq_ref[1], dql[...], TN)
    short, long, mate = xk_ref[0], xk_ref[1], mate_ref[...]
    dwk = dot(short, dks[...], TN) + dot(long, dkl[own], TN) + dot(mate, dkl[other], TN)
    dwv = dot(short, dvs[...], TN) + dot(long, dvl[own], TN) + dot(mate, dvl[other], TN)
    if locals_:
        for step in range(2):

            @pl.when(pl.program_id(0) == step)
            def _():
                for color in range(2):
                    flow = locals_[2 * step + color]
                    count, share, columns = flow.block
                    part = slice(color * columns, (color + 1) * columns)
                    for number, total in enumerate((dwq, dwk, dwv)):
                        low = total[:, part].astype(BF16)
                        for device in range(low.shape[0] // share):
                            at = tuple((device >> bit) & 1 for bit in reversed(range(len(flow.order))))
                            flow.source[at + (number,)] = low[device * share : (device + 1) * share]
    else:
        dwq_ref[...] = dwq.astype(BF16)
        dwk_ref[...] = dwk.astype(BF16)
        dwv_ref[...] = dwv.astype(BF16)
    tick(4)

    @pl.when(pl.program_id(0) == 0)
    def _():
        dx_ref[...] = resid_ref[...]
        if not self_keys:
            dy_ref[...] = jnp.zeros_like(dy_ref)
        mate_sum[...] = jnp.zeros_like(mate_sum)

    mate_sum[...] += dot(dkl[other], wk, NT) + dot(dvl[other], wv, NT)
    @pl.when(pl.program_id(0) == pl.num_programs(0) - 1)
    def _():
        dmate_ref[...] = mate_sum[...].astype(BF16)

    tick(5)
    dx_ref[0] += dot(dqs[...], wq, NT)
    dx_ref[1] += dot(dql[...], wq, NT)
    dy_ref[0] += dot(dks[...], wk, NT) + dot(dvs[...], wv, NT)
    dy_ref[1] += dot(dkl[own], wk, NT) + dot(dvl[own], wv, NT)
    for slot in range(6, 6 + after):
        tick(slot)


def attend_back(grad, saved, mate, resid, queries, keys, weights, base, flows, plan, collective, last=None):
    _, rows, width = queries.shape
    self_keys = keys is None
    weight = lambda index: (weights, pl.BlockSpec((1, width, COLS), lambda step: (index, 0, step)))
    both = pl.BlockSpec((2, rows, COLS), lambda step: (0, 0, step))
    cols = lambda count: pl.BlockSpec((count, COLS), lambda step: (0, step))
    powers = lambda count: pl.BlockSpec((COLS // 64, rows, count), lambda step: (step, 0, 0))
    full = pl.BlockSpec((2, rows, width), lambda step: (0, 0, 0))
    xs = (queries,) if self_keys else (queries, keys)
    flops = 2 * rows * width * width * 14 + 8 * rows * width * (SHORT + LONG)
    specs = [both] * 4 + [cols(rows)] * 2 + [cols(LONG)] * 2 + [powers(SHORT), powers(LONG)]
    o, inverse, *rest = saved
    locals_, swap_back, total = last or ((), None, None)
    outs = [(shaped((2, rows, width), F32), full)] * len(xs)
    scratch = (
        [pltpu.VMEM((rows, COLS), BF16)] * 3
        + [pltpu.VMEM((rows, COLS), BF16)]
        + [pltpu.VMEM((LONG, COLS), BF16)] * 2
        + [pltpu.VMEM((rows, width), F32)]
    )
    if last:
        scratch.append(pltpu.VMEM((rows, width), BF16))
    else:
        outs.append((shaped((rows, width), BF16), pl.BlockSpec((rows, width), lambda step: (0, 0))))
        outs += [(shaped((width, width), BF16), cols(width))] * 3
    after = 1 + max([spot for _, spot in plan] + [5]) - 6
    norms = total.terms if total else []
    return call(
        functools.partial(attend_back_kernel, self_keys, locals_, swap_back, total, after),
        width // COLS,
        [(array, whole(array)) for array in norms]
        + list(zip((grad, o, inverse, *rest), specs))
        + [(array, whole(array)) for array in (resid, *xs, mate)]
        + [weight(base), weight(base + 1), weight(base + 2)],
        outs,
        scratch,
        "attend_back",
        cost(flops * 2, 28 << 20),
        flows,
        plan,
        collective,
    )


def norm_parts(resid):
    average = jnp.mean(resid, axis=-1, keepdims=True)
    centered = resid - average
    variance = jnp.mean(centered * centered, axis=-1, keepdims=True)
    spread = lax.rsqrt(variance + EPSILON)
    return centered * spread, spread


def norm_back(normal, spread, gain, grad):
    scaled = grad * gain
    first = jnp.mean(scaled, axis=-1, keepdims=True)
    second = jnp.mean(scaled * normal, axis=-1, keepdims=True)
    return (scaled - first - normal * second) * spread


def add_norm_grads(ref, place, grad, normal):
    ref[place : place + 1, :] += jnp.sum(grad * normal, axis=0, keepdims=True)
    ref[8 + place : 9 + place, :] += jnp.sum(grad, axis=0, keepdims=True)


def logistic(value):
    return 1.0 / (1.0 + jnp.exp(-value))


def feed_kernel(chunks, o_ref, x_ref, wo_ref, up_ref, down_ref, gain_ref, shift_ref, r1_ref, u_ref, r2_ref, enc_ref):
    resid = x_ref[0].astype(F32) + dot(o_ref[0], wo_ref[0])
    r1_ref[0] = resid
    normal, _ = norm_parts(resid)
    hidden = normal * gain_ref[0:1] + shift_ref[0:1]
    hidden_low = hidden.astype(BF16)
    total = hidden
    for chunk in range(chunks):
        part = slice(chunk * CHUNK, (chunk + 1) * CHUNK)
        upward = dot(hidden_low, up_ref[0, :, part])
        u_ref[0, :, part] = upward
        active = (upward * logistic(upward)).astype(BF16)
        total = total + dot(active, down_ref[0, part, :])
    r2_ref[0] = total
    normal, _ = norm_parts(total)
    enc_ref[0] = (normal * gain_ref[1:2] + shift_ref[1:2]).astype(BF16)


def feed(o, x, attn, ups, downs, gains, shifts):
    _, rows, width = x.shape
    inner = ups.shape[2]
    row = lambda count: pl.BlockSpec((1, rows, count), lambda batch: (batch, 0, 0))
    pick = lambda array, index: pl.BlockSpec((1,) + array.shape[1:], lambda batch: (index, 0, 0))
    return pl.pallas_call(
        functools.partial(feed_kernel, inner // CHUNK),
        grid=(2,),
        out_shape=(
            shaped((2, rows, width), F32),
            shaped((2, rows, inner), F32),
            shaped((2, rows, width), F32),
            shaped((2, rows, width), BF16),
        ),
        in_specs=[row(width), row(width), pick(attn, 3), pick(ups, 0), pick(downs, 0), whole(gains), whole(shifts)],
        out_specs=(row(width), row(inner), row(width), row(width)),
        compiler_params=params(),
        cost_estimate=cost(4 * rows * width * (width + 2 * inner), 22 << 20, 2 * rows * inner),
        name="feed",
    )(o, x, attn, ups, downs, gains, shifts)


def middle_kernel(o_ref, x_ref, wo_ref, gain_ref, shift_ref, r_ref, low_ref):
    resid = x_ref[0].astype(F32) + dot(o_ref[0], wo_ref[0])
    r_ref[0] = resid
    normal, _ = norm_parts(resid)
    low_ref[0] = (normal * gain_ref[2:3] + shift_ref[2:3]).astype(BF16)


def middle(o, x, attn, gains, shifts):
    _, rows, width = x.shape
    row = lambda count: pl.BlockSpec((1, rows, count), lambda batch: (batch, 0, 0))
    pick = lambda array, index: pl.BlockSpec((1,) + array.shape[1:], lambda batch: (index, 0, 0))
    return pl.pallas_call(
        middle_kernel,
        grid=(2,),
        out_shape=(shaped((2, rows, width), F32), shaped((2, rows, width), BF16)),
        in_specs=[row(width), row(width), pick(attn, 7), whole(gains), whole(shifts)],
        out_specs=(row(width), row(width)),
        compiler_params=params(),
        cost_estimate=cost(4 * rows * width * width, 7 << 20),
        name="middle",
    )(o, x, attn, gains, shifts)


def feed_back_chunks(
    tick, chunks, grad, low, hidden_low, u_ref, a_ref, up_ref, down_ref, up_sum, down_sum
):
    total = grad
    for chunk in range(chunks):
        part = slice(chunk * CHUNK, (chunk + 1) * CHUNK)
        upward = u_ref[:, part]
        gate = logistic(upward)
        if a_ref is None:
            active = (upward * gate).astype(BF16)
        else:
            active = a_ref[:, part]
        grad_active = dot(low, down_ref[0, part, :], NT)
        grad_up = (grad_active * gate * (1.0 + upward * (1.0 - gate))).astype(BF16)
        down_sum[part, :] += dot(active, low, TN)
        up_sum[chunk] += dot(hidden_low, grad_up, TN)
        total = total + dot(grad_up, up_ref[0, :, part], NT)
        tick(1 + chunk)
    return total


def clear_first(*refs):
    @pl.when(pl.program_id(0) == 0)
    def _():
        for ref in refs:
            ref[...] = jnp.zeros_like(ref)


def write_last(*pairs):
    @pl.when(pl.program_id(0) == pl.num_programs(0) - 1)
    def _():
        for ref, total in pairs:
            ref[...] = total[...].astype(BF16)


def turn_kernel(
    chunks,
    tick,
    o_ref,
    r3_ref,
    cot_ref,
    wo_ref,
    up_ref,
    down_ref,
    gain_ref,
    shift_ref,
    out_ref,
    dr_ref,
    do_ref,
    dup_ref,
    ddown_ref,
    dwo_ref,
    norm_ref,
    u_s,
    a_s,
    up_sum,
    down_sum,
    wo_sum,
):
    clear_first(up_sum, down_sum, wo_sum, norm_ref)
    mixed = o_ref[0]
    normal3, _ = norm_parts(r3_ref[0])
    resid4 = normal3 * gain_ref[2:3] + shift_ref[2:3] + dot(mixed, wo_ref[0])
    normal4, spread4 = norm_parts(resid4)
    hidden = normal4 * gain_ref[3:4] + shift_ref[3:4]
    hidden_low = hidden.astype(BF16)
    total = hidden
    for chunk in range(chunks):
        part = slice(chunk * CHUNK, (chunk + 1) * CHUNK)
        upward = dot(hidden_low, up_ref[0, :, part])
        u_s[:, part] = upward
        active = (upward * logistic(upward)).astype(BF16)
        a_s[:, part] = active
        total = total + dot(active, down_ref[0, part, :])
    normal5, spread5 = norm_parts(total)
    out_ref[0] = (normal5 * gain_ref[4:5] + shift_ref[4:5]).astype(BF16)
    grad = cot_ref[0].astype(F32)
    add_norm_grads(norm_ref, 4, grad, normal5)
    grad = norm_back(normal5, spread5, gain_ref[4:5], grad)
    grad = feed_back_chunks(
        tick,
        chunks,
        grad,
        grad.astype(BF16),
        hidden_low,
        u_s,
        a_s,
        up_ref,
        down_ref,
        up_sum,
        down_sum,
    )
    add_norm_grads(norm_ref, 3, grad, normal4)
    grad = norm_back(normal4, spread4, gain_ref[3:4], grad)
    dr_ref[0] = grad
    low = grad.astype(BF16)
    wo_sum[...] += dot(mixed, low, TN)
    do_ref[0] = dot(low, wo_ref[0], NT).astype(BF16)
    write_last((dup_ref, up_sum), (ddown_ref, down_sum), (dwo_ref, wo_sum))


def turn(o, r3, cot, attn, ups, downs, gains, shifts):
    _, rows, width = r3.shape
    inner = ups.shape[2]
    chunks = inner // CHUNK
    row = pl.BlockSpec((1, rows, width), lambda batch: (batch, 0, 0))
    pick = lambda array, index: (array, pl.BlockSpec((1,) + array.shape[1:], lambda batch: (index, 0, 0)))
    still = lambda *shape: pl.BlockSpec(shape, lambda batch: (0,) * len(shape))
    out = lambda kind, *shape: (shaped(shape, kind), still(*shape))
    results, _ = call(
        functools.partial(turn_kernel, chunks),
        2,
        [(o, row), (r3, row), (cot, row), pick(attn, 11), pick(ups, 1), pick(downs, 1)]
        + [(gains, whole(gains)), (shifts, whole(shifts))],
        [
            (shaped((2, rows, width), BF16), row),
            (shaped((2, rows, width), F32), row),
            (shaped((2, rows, width), BF16), row),
            out(BF16, chunks, width, CHUNK),
            out(BF16, inner, width),
            out(BF16, width, width),
            out(F32, 16, width),
        ],
        [
            pltpu.VMEM((rows, inner), F32),
            pltpu.VMEM((rows, inner), BF16),
            pltpu.VMEM((chunks, width, CHUNK), F32),
            pltpu.VMEM((inner, width), F32),
            pltpu.VMEM((width, width), F32),
        ],
        "turn",
        cost(12 * rows * width * (width + 2 * inner), 20 << 20, 4 * rows * inner),
    )
    return results


def feed_back_kernel(
    chunks,
    mate,
    tick,
    grad_ref,
    r2_ref,
    r1_ref,
    u_ref,
    o_ref,
    wo_ref,
    up_ref,
    down_ref,
    gain_ref,
    shift_ref,
    dr_ref,
    do_ref,
    dup_ref,
    ddown_ref,
    dwo_ref,
    norm_ref,
    grad_s,
    up_sum,
    down_sum,
    wo_sum,
):
    tick(0)
    clear_first(up_sum, down_sum, wo_sum, norm_ref)
    grad_s[...] = grad_ref[0]

    @pl.when(pl.program_id(0) == 1)
    def _():
        grad_s[...] += mate.got[...].astype(F32)

    grad = grad_s[...]
    normal2, spread2 = norm_parts(r2_ref[0])
    add_norm_grads(norm_ref, 1, grad, normal2)
    grad = norm_back(normal2, spread2, gain_ref[1:2], grad)
    normal1, spread1 = norm_parts(r1_ref[0])
    hidden_low = (normal1 * gain_ref[0:1] + shift_ref[0:1]).astype(BF16)
    grad = feed_back_chunks(
        tick,
        chunks,
        grad,
        grad.astype(BF16),
        hidden_low,
        u_ref.at[0],
        None,
        up_ref,
        down_ref,
        up_sum,
        down_sum,
    )
    add_norm_grads(norm_ref, 0, grad, normal1)
    grad = norm_back(normal1, spread1, gain_ref[0:1], grad)
    dr_ref[0] = grad
    low = grad.astype(BF16)
    wo_sum[...] += dot(o_ref[0], low, TN)
    do_ref[0] = dot(low, wo_ref[0], NT).astype(BF16)
    write_last((dup_ref, up_sum), (ddown_ref, down_sum), (dwo_ref, wo_sum))


def feed_back(grad, r2, r1, u, o, attn, ups, downs, gains, shifts, mate, flows, plan, collective):
    _, rows, width = r1.shape
    inner = ups.shape[2]
    chunks = inner // CHUNK
    row = lambda count: pl.BlockSpec((1, rows, count), lambda batch: (batch, 0, 0))
    pick = lambda array, index: (array, pl.BlockSpec((1,) + array.shape[1:], lambda batch: (index, 0, 0)))
    still = lambda *shape: pl.BlockSpec(shape, lambda batch: (0,) * len(shape))
    out = lambda kind, *shape: (shaped(shape, kind), still(*shape))
    return call(
        functools.partial(feed_back_kernel, chunks, mate),
        2,
        [(grad, row(width)), (r2, row(width)), (r1, row(width)), (u, row(inner)), (o, row(width))]
        + [pick(attn, 3), pick(ups, 0), pick(downs, 0), (gains, whole(gains)), (shifts, whole(shifts))],
        [
            (shaped((2, rows, width), F32), row(width)),
            (shaped((2, rows, width), BF16), row(width)),
            out(BF16, chunks, width, CHUNK),
            out(BF16, inner, width),
            out(BF16, width, width),
            out(F32, 16, width),
        ],
        [
            pltpu.VMEM((rows, width), F32),
            pltpu.VMEM((chunks, width, CHUNK), F32),
            pltpu.VMEM((inner, width), F32),
            pltpu.VMEM((width, width), F32),
        ],
        "feed_back",
        cost(8 * rows * width * (width + 2 * inner), 30 << 20, 2 * rows * inner),
        flows,
        plan,
        collective,
    )


def middle_back_kernel(tick, grad_ref, r_ref, o_ref, wo_ref, gain_ref, dr_ref, do_ref, dwo_ref, norm_ref, wo_sum):
    tick(0)
    clear_first(wo_sum, norm_ref)
    grad = grad_ref[0]
    normal, spread = norm_parts(r_ref[0])
    add_norm_grads(norm_ref, 2, grad, normal)
    grad = norm_back(normal, spread, gain_ref[2:3], grad)
    dr_ref[0] = grad
    low = grad.astype(BF16)
    wo_sum[...] += dot(o_ref[0], low, TN)
    do_ref[0] = dot(low, wo_ref[0], NT).astype(BF16)
    write_last((dwo_ref, wo_sum))
    tick(1)


def middle_back(grad, r, o, attn, gains, flows, plan, collective):
    _, rows, width = r.shape
    row = pl.BlockSpec((1, rows, width), lambda batch: (batch, 0, 0))
    pick = lambda array, index: (array, pl.BlockSpec((1,) + array.shape[1:], lambda batch: (index, 0, 0)))
    still = lambda *shape: pl.BlockSpec(shape, lambda batch: (0,) * len(shape))
    out = lambda kind, *shape: (shaped(shape, kind), still(*shape))
    return call(
        middle_back_kernel,
        2,
        [(grad, row), (r, row), (o, row), pick(attn, 7), (gains, whole(gains))],
        [
            (shaped((2, rows, width), F32), row),
            (shaped((2, rows, width), BF16), row),
            out(BF16, width, width),
            out(F32, 16, width),
        ],
        [pltpu.VMEM((width, width), F32)],
        "middle_back",
        cost(8 * rows * width * width, 12 << 20),
        flows,
        plan,
        collective,
    )


def finish_kernel(counts, src_ref, src_mate_ref, tgt_ref, tgt_mate_ref, norm_ref, *refs):
    sums, outs = refs[: -7], refs[-7:]
    gs_ref, gt_ref, attn_ref, up_ref, down_ref, gain_ref, shift_ref = outs
    long = pl.program_id(0) >= pl.num_programs(0) // 2
    for part_ref, mate_ref, out_ref in ((src_ref, src_mate_ref, gs_ref), (tgt_ref, tgt_mate_ref, gt_ref)):

        @pl.when(long)
        def _():
            out_ref[...] = part_ref[...] + mate_ref[...].astype(F32)[None]

        @pl.when(jnp.logical_not(long))
        def _():
            out_ref[...] = part_ref[...]

    @pl.when(pl.program_id(0) == 0)
    def _():
        for ref, (kind, index, cols) in zip(sums, counts):
            share = ref.shape[-2]
            if kind == "attn":
                for number, place in enumerate(index):
                    attn_ref[place, :, cols] = ref[number]
                continue
            tiles = up_ref.shape[2] // CHUNK
            for number in range(ref.shape[0]):
                tile = tiles - 1 if kind == "both" else number
                if kind == "up" or (kind == "both" and number == 0):
                    up_ref[index[0], :, tile * CHUNK : (tile + 1) * CHUNK] = ref[number]
                else:
                    down_ref[index[0], tile * share : (tile + 1) * share, :] = ref[number]
        share = gain_ref.shape[1]
        here = lax.axis_index("dp") * lax.axis_size("head") + lax.axis_index("head")
        width = norm_ref.shape[1]
        turned = pltpu.roll(norm_ref[...], (width - here * share) % width, axis=1)
        gain_ref[...] = turned[:5, :share]
        shift_ref[...] = turned[8:13, :share]


def finish(source, source_mate, target, target_mate, norms, named, share, inner, devices):
    _, rows, width = source.shape
    half = rows // 2
    row = pl.BlockSpec((1, half, width), lambda step: (step // 2, step % 2, 0))
    mate = pl.BlockSpec((half, width), lambda step: (step % 2, 0))
    sums = [array for array, *_ in named]
    counts = [tuple(rest) for _, *rest in named]
    outs = [
        (shaped((2, rows, width), F32), row),
        (shaped((2, rows, width), F32), row),
    ]
    for shape in ((12, share, width), (2, share, inner), (2, inner // devices, width), (5, share), (5, share)):
        outs.append((shaped(shape, F32), pl.BlockSpec(shape, lambda step, size=len(shape): (0,) * size)))
    return pl.pallas_call(
        functools.partial(finish_kernel, counts),
        grid=(4,),
        out_shape=[shape for shape, _ in outs],
        in_specs=[row, mate, row, mate, whole(norms)] + [whole(array) for array in sums],
        out_specs=[spec for _, spec in outs],
        compiler_params=params(),
        cost_estimate=cost(0, 11 << 20),
        name="finish",
    )(source, source_mate, target, target_mate, norms, *sums)


def place_stages(plan, numbers, stages, start, spots):
    plan.setdefault(start, []).extend((number, None) for number in numbers)
    for index, stage in enumerate(stages):
        plan.setdefault(spots[min(index, len(spots) - 1)], []).extend((number, stage) for number in numbers)


def body(
    source,
    target,
    cotangent,
    short_lengths,
    long_lengths,
    attn,
    ups,
    downs,
    gains,
    shifts,
):
    _, rows, width = source.shape
    inner = ups.shape[2]
    devices = lax.axis_size("dp") * lax.axis_size("head")
    bits = devices.bit_length() - 1
    assert 2 * rows == LONG and rows % SHORT == 0 and devices == 1 << bits
    share = width // devices
    parts = (2,) * bits
    lengths = (short_lengths, long_lengths)
    orders = (
        tuple(range(bits)),
        (0, 2, 1) + tuple(range(3, bits)),
        (0,) + tuple(range(3, bits)) + (1, 2),
    )
    tiles = inner // width

    def square(array):
        return array.reshape(parts + (1, share, width)), None, 0, 1

    def ffn_flows(last, dup, ddown):
        up = dup.reshape((tiles,) + parts + (1, share, width))
        down = ddown.reshape(parts + (tiles, share, width))
        most = tiles - 1
        pieces = (
            [(up, index, 0, 1) for index in range(most)],
            [(down, None, 0, most)],
            [(up, most, 0, 1), (down, None, most, 1)],
        )
        return [Flow(order, 0, last, piece) for order, piece in zip(orders, pieces)]

    def attn_flows(last, *groups):
        pieces = [[square(array) for array in group] for group in groups]
        return [Flow(order, 0, last, piece) for order, piece in zip(orders, pieces)]

    def later(first, last, partial):
        return [
            Flow(order, first, last, [(part, None, 0, part.shape[-3])])
            for order, part in zip(orders, partial)
        ]

    enc_saved, source_mate = attend(source, None, attn, 0, lengths, False, 0)
    r1, u, r2, enc = feed(enc_saved[0], source, attn, ups, downs, gains, shifts)
    self_saved, target_mate = attend(target, None, attn, 4, lengths, True, 1)
    r3, h3 = middle(self_saved[0], target, attn, gains, shifts)
    cross_saved, enc_mate = attend(h3, enc, attn, 8, lengths, False, 2)
    decoded, dr4, do_cross, dup1, ddown1, dw11, norms_a = turn(
        cross_saved[0], r3, cotangent, attn, ups, downs, gains, shifts
    )

    plan = {}
    place_stages(plan, (0, 1, 2), range(2), (0, 0), [(0, 2), (1, 3)])
    (dh3, denc, denc_mate, dw8, dw9, dw10), ffn1 = attend_back(
        do_cross,
        cross_saved,
        enc_mate,
        dr4,
        h3,
        enc,
        attn,
        8,
        ffn_flows(2, dup1, ddown1),
        plan,
        3,
    )

    plan = {}
    mate = Swap(0, (rows, width), denc_mate, kept=False)
    place_stages(plan, (5,), [0], (0, 0), [(1, 0)])
    place_stages(plan, (0, 1, 2), range(2, 4), (0, 0), [(0, 4), (1, 3)])
    place_stages(plan, (3, 4), range(2), (0, 0), [(0, 4), (1, 4)])
    (dr1, do_enc, dup0, ddown0, dw3, norms_c), sums = feed_back(
        denc,
        r2,
        r1,
        u,
        enc_saved[0],
        attn,
        ups,
        downs,
        gains,
        shifts,
        mate,
        later(2, 4, ffn1) + attn_flows(2, [dw8, dw11], [dw9, dw10]) + [mate],
        plan,
        4,
    )
    ffn1, cross = sums[:3], sums[3:]

    plan = {}
    place_stages(plan, (0, 1, 2), range(1), (0, 0), [(1, 1)])
    place_stages(plan, (3, 4), range(2, 3), (0, 0), [(1, 1)])
    place_stages(plan, (5, 6, 7), range(4, bits), (0, 0), [(1, 1)])
    (dr3, do_self, dw7, norms_b), sums = middle_back(
        dh3,
        r3,
        self_saved[0],
        attn,
        gains,
        ffn_flows(1, dup0, ddown0) + later(2, 3, cross) + later(4, bits, ffn1),
        plan,
        5,
    )
    ffn0, cross, ffn1 = sums[:3], sums[3:5], sums[5:]

    plan = {}
    place_stages(plan, (0, 1, 2), range(1, 3), (0, 0), [(1, 0), (1, 3)])
    place_stages(plan, (3, 4), range(3, bits), (0, 0), [(0, 5), (1, 2)])
    place_stages(plan, (5, 6), range(2), (1, 0), [(1, 2), (1, 6)])
    (dx_target, target_back, dw4, dw5, dw6), sums = attend_back(
        do_self,
        self_saved,
        target_mate,
        dr3,
        target,
        None,
        attn,
        4,
        later(1, 3, ffn0) + later(3, bits, cross) + attn_flows(2, [dw3], [dw7]),
        plan,
        6,
    )
    ffn0, cross, outward = sums[:3], sums[3:5], sums[5:]

    plan = {}
    stages = range(bits)
    block = (3, share, COLS // 2)
    own = [Flow(order, 0, bits, [], block) for _ in range(2) for order in orders[:2]]
    source_swap = Swap(0, (rows, width))
    total = Total(bits, [norms_a, norms_b, norms_c])
    place_stages(plan, (8,), [0], (0, 0), [(0, 1)])
    place_stages(plan, (3, 4), range(2, bits), (0, 0), [(0, 2), (1, 0), (1, 1)])
    place_stages(plan, (0, 1, 2), range(3, bits), (0, 0), [(0, 2), (1, 1)])
    place_stages(plan, (5, 6, 7), stages, (0, 0), [(0, 2), (1, 0), (1, 2), (1, 4), (1, 7)])
    place_stages(plan, (9,), stages, (0, 1), [(0, 2), (0, 5), (1, 1), (1, 2), (1, 4)])
    place_stages(plan, (10, 11), stages, (0, 4), [(1, 1), (1, 3), (1, 6), (1, 7), (1, 8)])
    place_stages(plan, (12, 13), stages, (1, 4), [(1, spot) for spot in range(6, 6 + bits)])
    place_stages(plan, (14,), [0], (1, 5), [(1, 6)])
    (dx_source,), sums = attend_back(
        do_enc,
        enc_saved,
        source_mate,
        dr1,
        source,
        None,
        attn,
        0,
        later(3, bits, ffn0)
        + later(2, bits, outward)
        + attn_flows(bits, [dw4], [dw5], [dw6])
        + [Swap(0, (rows, width), target_back), total]
        + own
        + [source_swap],
        plan,
        7,
        (own, source_swap, total),
    )
    ffn0, outward, inward = sums[:3], sums[3:5], sums[5:8]
    target_back, norms, *own_sums, source_back = sums[8:]

    everything = slice(None)
    named = [(array, "attn", places, everything) for array, places in zip(cross, ((8, 11), (9, 10)))]
    named += [
        (array, "attn", (place,), everything)
        for array, place in zip((*outward, *inward), (3, 7, 4, 5, 6))
    ]
    for index, sums in enumerate((ffn0, ffn1)):
        named += [(array, kind, (index,), None) for array, kind in zip(sums, ("up", "down", "both"))]
    for number, array in enumerate(own_sums):
        start = number * (COLS // 2)
        named.append((array, "attn", (0, 1, 2), slice(start, start + COLS // 2)))
    grad_source, grad_target, grad_attn, grad_up, grad_down, grad_gains, grad_shifts = finish(
        dx_source, source_back, dx_target, target_back, norms, named, share, inner, devices
    )
    return decoded, grad_source, grad_target, grad_attn, grad_up, grad_down, grad_gains, grad_shifts


def solution(mesh):
    rows = P(None, AXES, None)
    return jax.shard_map(
        body,
        mesh=mesh,
        in_specs=(rows, rows, rows, P(None, "dp"), P(None, "dp"), P(), P(), P(), P(), P()),
        out_specs=(rows, rows, rows, rows, rows, rows, P(None, AXES), P(None, AXES)),
        check_vma=False,
    )
```

```python
import functools
import math

import jax
import jax.numpy as jnp
from jax import lax
from jax.experimental import pallas as pl
from jax.experimental.pallas import tpu as pltpu
from jax.sharding import PartitionSpec as P

HEADS = 8
SHORT = 256
LONG = 1024

EPSILON = 1e-05
MASKED = -1e30
F32 = jnp.float32
BF16 = jnp.bfloat16
AXES = ("dp", "head")
COLS = 256
CHUNK = 512

NN = (((1,), (0,)), ((), ()))
NT = (((1,), (1,)), ((), ()))
TN = (((0,), (0,)), ((), ()))


def dot(left, right, dims=NN):
    return lax.dot_general(left, right, dims, preferred_element_type=F32)


def params():
    return pltpu.CompilerParams(vmem_limit_bytes=63 << 20)


def cost(flops, moved, powers=0):
    return pl.CostEstimate(flops=int(flops), bytes_accessed=int(moved), transcendentals=int(powers))


def whole(array):
    return pl.BlockSpec(array.shape, lambda *step: (0,) * array.ndim, pipeline_mode=pl.Buffered(1))


def shaped(shape, kind):
    return jax.ShapeDtypeStruct(shape, kind)


def lanes():
    return lax.broadcasted_iota(jnp.int32, (1, 128), 1)


def one_head(which, pair):
    keep = (lanes() < 64) if which == 0 else (lanes() >= 64)
    return jnp.where(keep, pair, jnp.zeros_like(pair))


def join_heads(first, second):
    return jnp.where(lanes() < 64, first, second)


MESH = pl.DeviceIdType.MESH


def partner(bit):
    head_bits = lax.axis_size("head").bit_length() - 1
    data, head = lax.axis_index("dp"), lax.axis_index("head")
    if bit < head_bits:
        step = 1 << bit
        mine = (head // step) % 2
        return mine, (data, head + (1 - 2 * mine) * step)
    step = 1 << (bit - head_bits)
    mine = (data // step) % 2
    return mine, (data + (1 - 2 * mine) * step, head)


class Flow:
    def __init__(self, order, first, last, pieces, block=None):
        self.order, self.first, self.last = order, first, last
        self.bits = order[first:last]
        self.local = block is not None
        self.arrays = []
        self.pieces = []
        total = 0
        for array, lead, start, count in pieces:
            known = [index for index, other in enumerate(self.arrays) if other is array]
            if not known:
                self.arrays.append(array)
            index = known[0] if known else len(self.arrays) - 1
            self.pieces.append((index, lead, start, total, count))
            total += count
        self.block = block or (total,) + pieces[0][0].shape[-2:]

    def shape(self, stage):
        return (2,) * (len(self.order) - stage) + self.block

    def out(self):
        done = self.last == len(self.order)
        return shaped(self.shape(self.last), F32 if done else BF16)

    def scratch(self):
        stages = range(self.first, self.last)
        count = len(self.pieces)
        dma = pltpu.SemaphoreType.DMA
        return (
            ([] if self.local else [pltpu.VMEM(self.shape(self.first + 1), BF16)])
            + [pltpu.VMEM(self.shape(stage + 1), BF16) for stage in stages]
            + [pltpu.VMEM(self.shape(stage + 1), BF16) for stage in stages[:-1]]
            + [dma((len(stages),)), dma((len(stages),))]
            + [dma((count,)) for _ in range(0 if self.local else 3)]
        )

    def bind(self, inputs, out, scratch):
        stages = range(self.first, self.last)
        self.in_refs, self.out_ref = inputs, out
        count = len(stages)
        skip = 0 if self.local else 1
        self.own = scratch[0]
        self.got = dict(zip(stages, scratch[skip : skip + count]))
        self.sum = dict(zip(stages[:-1], scratch[skip + count :]))
        if self.local:
            self.send, self.recv = scratch[-2:]
        else:
            self.send, self.recv, self.local_sem, self.piece_send, self.piece_recv = scratch[-5:]

    def where(self, stage, index):
        left = sorted(self.order[stage:])
        place = len(left) - 1 - left.index(self.order[stage])
        return (slice(None),) * place + (index,)

    def piece_copies(self):
        stage = self.first
        mine, device = partner(self.order[stage])
        left = len(self.order) - stage
        for number, (index, lead, start, total, count) in enumerate(self.pieces):
            prefix = () if lead is None else (lead,)
            target = (slice(None),) * (left - 1) + (slice(total, total + count),)
            ref = self.in_refs[index]

            def part(value):
                at = self.where(stage, value)
                at += (slice(None),) * (left - len(at)) + (slice(start, start + count),)
                return ref.at[prefix + at]

            yield pltpu.make_async_remote_copy(
                src_ref=part(1 - mine),
                dst_ref=self.got[stage].at[target],
                send_sem=self.piece_send.at[number],
                recv_sem=self.piece_recv.at[number],
                device_id=device,
                device_id_type=MESH,
            )
            yield pltpu.make_async_copy(
                part(mine),
                self.own.at[target],
                self.local_sem.at[number],
            )

    def stage_copy(self, stage):
        mine, device = partner(self.order[stage])
        source = self.source if stage == self.first else self.sum[stage - 1]
        return pltpu.make_async_remote_copy(
            src_ref=source.at[self.where(stage, 1 - mine)],
            dst_ref=self.got[stage],
            send_sem=self.send.at[stage - self.first],
            recv_sem=self.recv.at[stage - self.first],
            device_id=device,
            device_id_type=MESH,
        )

    def start(self):
        if self.local:
            self.stage_copy(self.first).start()
        else:
            for copy in self.piece_copies():
                copy.start()

    def step(self, stage):
        mine, _ = partner(self.order[stage])
        if stage > self.first:
            self.stage_copy(stage).wait()
            kept = self.sum[stage - 1].at[self.where(stage, mine)]
        elif self.local:
            self.stage_copy(stage).wait()
            kept = self.source.at[self.where(stage, mine)]
        else:
            for copy in self.piece_copies():
                copy.wait()
            kept = self.own
        got = self.got[stage]
        last = stage == self.last - 1
        target = self.out_ref if last else self.sum[stage]
        kind = F32 if stage == len(self.order) - 1 else BF16
        dims = min(2, len(self.order) - stage - 1)

        def add(index, carry):
            at = tuple((index >> bit) & 1 for bit in range(dims))
            target[at] = kept[at].astype(kind) + got[at].astype(kind)
            return carry

        if dims:
            lax.fori_loop(0, 1 << dims, add, 0)
        else:
            target[...] = kept[...].astype(kind) + got[...].astype(kind)
        if not last:
            self.stage_copy(stage + 1).start()


class Swap:
    def __init__(self, bit, shape, array=None, kept=True):
        self.bits = (bit,)
        self.wide = shape
        self.kept = kept
        self.arrays = [] if array is None else [array]

    def out(self):
        return shaped(self.wide, BF16) if self.kept else None

    def scratch(self):
        return [pltpu.VMEM(self.wide, BF16), pltpu.SemaphoreType.DMA, pltpu.SemaphoreType.DMA]

    def bind(self, inputs, out, scratch):
        self.source = inputs[0] if inputs else None
        self.out_ref = out
        self.got, self.send, self.recv = scratch

    def copy(self):
        return pltpu.make_async_remote_copy(
            src_ref=self.source,
            dst_ref=self.got,
            send_sem=self.send,
            recv_sem=self.recv,
            device_id=partner(self.bits[0])[1],
            device_id_type=MESH,
        )

    def start(self):
        self.copy().start()

    def step(self, stage):
        self.copy().wait()
        if self.kept:
            self.out_ref[...] = self.got[...]


class Total:
    def __init__(self, bits, arrays):
        self.bits = tuple(range(bits))
        self.arrays = []
        self.terms = arrays

    def out(self):
        return shaped(self.terms[0].shape, F32)

    def scratch(self):
        count = len(self.bits)
        whole_shape = (count,) + self.terms[0].shape
        dma = pltpu.SemaphoreType.DMA((count,))
        return [pltpu.VMEM(whole_shape, F32), pltpu.VMEM(whole_shape, F32), dma, dma]

    def bind(self, inputs, out, scratch):
        self.out_ref = out
        self.held, self.got, self.send, self.recv = scratch

    def copy(self, stage):
        return pltpu.make_async_remote_copy(
            src_ref=self.held.at[stage],
            dst_ref=self.got.at[stage],
            send_sem=self.send.at[stage],
            recv_sem=self.recv.at[stage],
            device_id=partner(stage)[1],
            device_id_type=MESH,
        )

    def start(self):
        self.held[0] = functools.reduce(lambda left, right: left + right, [ref[...] for ref in self.refs])
        self.copy(0).start()

    def step(self, stage):
        self.copy(stage).wait()
        total = self.held[stage] + self.got[stage]
        if stage == len(self.bits) - 1:
            self.out_ref[...] = total
        else:
            self.held[stage + 1] = total
            self.copy(stage + 1).start()


def greet(bits):
    ready = pltpu.get_barrier_semaphore()
    for bit in bits:
        _, device = partner(bit)
        pl.semaphore_signal(ready, inc=1, device_id=device, device_id_type=MESH)
    pl.semaphore_wait(ready, len(bits))


def call(kernel, steps, ins, outs, scratch, name, estimate, flows=(), plan=None, collective=None):
    extra_in = [array for flow in flows for array in flow.arrays]
    bits = sorted({bit for flow in flows for bit in flow.bits})
    counts = (len(ins), len(outs), len(scratch))

    def body(*refs):
        refs = list(refs)
        take = lambda count: [refs.pop(0) for _ in range(count)]
        main = take(counts[0])
        inputs = [take(len(flow.arrays)) for flow in flows]
        main += take(counts[1])
        results = [take(1)[0] if flow.out() else None for flow in flows]
        main += take(counts[2])
        for flow, given, result in zip(flows, inputs, results):
            flow.bind(given, result, take(len(flow.scratch())))

        def tick(slot, now=None):
            for (step, place), actions in (plan or {}).items():
                if place == slot:

                    here = pl.program_id(0) == step

                    @pl.when(here if now is None else here & now)
                    def _():
                        if (step, slot) == (0, 0):
                            greet(bits)
                        for number, stage in actions:
                            if stage is None:
                                flows[number].start()
                            else:
                                flows[number].step(stage)

        kernel(tick, *main)

    still = lambda shape: pl.BlockSpec(shape, lambda step: (0,) * len(shape))
    given_out = [flow.out() for flow in flows if flow.out()]
    remote = dict(collective_id=collective, has_side_effects=True) if flows else {}
    result = pl.pallas_call(
        body,
        grid=(steps,),
        out_shape=[shape for shape, _ in outs] + given_out,
        in_specs=[spec for _, spec in ins] + [pl.BlockSpec(memory_space=pl.ANY)] * len(extra_in),
        out_specs=[spec for _, spec in outs] + [still(shape.shape) for shape in given_out],
        scratch_shapes=list(scratch) + [shape for flow in flows for shape in flow.scratch()],
        compiler_params=pltpu.CompilerParams(vmem_limit_bytes=63 << 20, **remote),
        cost_estimate=estimate,
        name=name,
    )(*[array for array, _ in ins], *extra_in)
    return result[: len(outs)], result[len(outs) :]


def scores_bias(own_length, other_length, width, ahead):
    row = lax.broadcasted_iota(jnp.int32, (width, width), 0)
    column = lax.broadcasted_iota(jnp.int32, (width, width), 1)
    own = jnp.where((column < own_length) & (column <= row + ahead), 0.0, MASKED).astype(F32)
    if other_length is None:
        return own
    other = jnp.where(column < other_length, 0.0, MASKED).astype(F32)
    return jnp.concatenate([own, other], axis=1)


def attend_rows(bias, q_ref, k_ref, v_ref, e_ref, o_ref, inv_ref, rows, keys):
    count = bias.shape[1]
    ones = jnp.ones((count, 128), BF16)
    for pair in range(COLS // 128):
        cols = slice(pair * 128, pair * 128 + 128)
        queries = q_ref[rows, cols]
        key_pair = k_ref[keys, cols]
        value_ext = jnp.concatenate([v_ref[keys, cols], ones], axis=1)
        outs, inverses = [], []
        for which in range(2):
            scores = dot(one_head(which, queries), key_pair, NT) + bias
            highest = jnp.max(scores, axis=1, keepdims=True)
            powers = jnp.exp(scores - highest).astype(BF16)
            e_ref[pair * 2 + which, rows, :] = powers
            mixed = dot(powers, value_ext)
            inverse = 1.0 / mixed[:, 128:]
            outs.append(mixed[:, :128] * inverse)
            inverses.append(inverse)
        o_ref[rows, cols] = join_heads(*outs).astype(BF16)
        inv_ref[rows, cols] = join_heads(*inverses)


def attend_kernel(causal, cross, mates, tick, *refs):
    number = len(causal)
    ins = refs[: 2 if cross else number]
    (
        short_ref,
        long_ref,
        wq_ref,
        wk_ref,
        wv_ref,
        o_ref,
        inv_ref,
        q_ref,
        ks_ref,
        vs_ref,
        kl_ref,
        vl_ref,
        es_ref,
        el_ref,
        *scratch,
    ) = refs[len(ins) :]
    rows = ins[0].shape[1]
    scale = 0.125
    step = pl.program_id(0)
    which = step // 2
    place = lax.axis_index("head")
    half = place % 2
    for mate, ref in zip(mates, ins[-len(mates) :]):
        mate.source = ref.at[1]
    tick(0)
    if number == 1:
        xq_ref, xk_ref = ins[0], ins[-1]
    else:
        xq_ref = xk_ref = scratch[0]
        for index in range(number):

            @pl.when(step == 2 * index)
            def _():
                xq_ref[...] = ins[index][...]

    kind = sum([jnp.where(which == index, 1, 0) for index in range(number) if causal[index]], 0)
    ahead = (1 - kind) * LONG
    q_ref[0, 0] = (dot(xq_ref[0], wq_ref[0]) * scale).astype(BF16)
    ks_ref[0] = dot(xk_ref[0], wk_ref[0]).astype(BF16)
    vs_ref[0] = dot(xk_ref[0], wv_ref[0]).astype(BF16)
    slots = rows // SHORT
    for slot in range(slots):
        bias = scores_bias(short_ref[kind, place * slots + slot], None, SHORT, ahead)
        here = slice(slot * SHORT, (slot + 1) * SHORT)
        attend_rows(
            bias,
            q_ref.at[0, 0],
            ks_ref.at[0],
            vs_ref.at[0],
            es_ref.at[0],
            o_ref.at[0, 0],
            inv_ref.at[0, 0],
            here,
            here,
        )
    q_ref[0, 1] = (dot(xq_ref[1], wq_ref[0]) * scale).astype(BF16)
    kl_ref[0, :rows] = dot(xk_ref[1], wk_ref[0]).astype(BF16)
    vl_ref[0, :rows] = dot(xk_ref[1], wv_ref[0]).astype(BF16)
    tick(1)
    if number == 1:
        mate_ref = mates[0].got
    else:
        mate_ref = scratch[1]
        for index in range(number):

            @pl.when(step == 2 * index)
            def _():
                mate_ref[...] = mates[index].got[...]

    kl_ref[0, rows:] = dot(mate_ref[...], wk_ref[0]).astype(BF16)
    vl_ref[0, rows:] = dot(mate_ref[...], wv_ref[0]).astype(BF16)
    everything = slice(None)
    length = long_ref[kind, place // 2]
    other = (length - (1 - half) * rows) * (1 - kind * (1 - half))
    bias = scores_bias(length - half * rows, other, rows, ahead)
    attend_rows(
        bias,
        q_ref.at[0, 1],
        kl_ref.at[0],
        vl_ref.at[0],
        el_ref.at[0],
        o_ref.at[0, 1],
        inv_ref.at[0, 1],
        everything,
        everything,
    )


def attend(xs, causal, cross, weights, base, lengths, collective):
    _, rows, width = xs[0].shape
    number = len(causal)
    heads = width // 64
    place = lambda step: step // 2
    weight = lambda index: (
        weights,
        pl.BlockSpec((1, width, COLS), lambda step: (base + 4 * place(step) + index, 0, step % 2)),
    )
    both = lambda kind: (
        shaped((number, 2, rows, width), kind),
        pl.BlockSpec((1, 2, rows, COLS), lambda step: (place(step), 0, 0, step % 2)),
    )
    cols = lambda count: (
        shaped((number, count, width), BF16),
        pl.BlockSpec((1, count, COLS), lambda step: (place(step), 0, step % 2)),
    )
    powers = lambda count: (
        shaped((number, heads, rows, count), BF16),
        pl.BlockSpec((1, COLS // 64, rows, count), lambda step: (place(step), step % 2, 0, 0)),
    )
    flops = 2 * rows * width * width * 7 + 4 * rows * width * (SHORT + LONG)
    mates = [Swap(0, (rows, width)) for _ in range(number)]
    plan = {(0, 0): [(index, None) for index in range(number)]}
    for index in range(number):
        plan[2 * index, 1] = [(index, 0)]
    return call(
        functools.partial(attend_kernel, causal, cross, mates),
        2 * number,
        [(array, whole(array)) for array in xs]
        + [(array, pl.BlockSpec(memory_space=pltpu.SMEM)) for array in lengths]
        + [weight(0), weight(1), weight(2)],
        [both(BF16), both(F32), both(BF16), cols(rows), cols(rows), cols(LONG), cols(LONG)]
        + [powers(SHORT), powers(LONG)],
        [] if number == 1 else [pltpu.VMEM((2, rows, width), BF16), pltpu.VMEM((rows, width), BF16)],
        "attend",
        cost(flops * 2 * number, number * (22 << 20), number * heads * rows * (SHORT + LONG)),
        mates,
        plan,
        collective,
    )


def attend_back_rows(
    do_ref,
    o_ref,
    inv_ref,
    q_ref,
    k_ref,
    v_ref,
    e_ref,
    dq_ref,
    dk_ref,
    dv_ref,
    rows,
    keys,
    pair,
    scale,
):
    cols = pl.ds(pl.multiple_of(pair * 128, 128), 128)
    grad = do_ref[rows, cols].astype(F32) * inv_ref[rows, cols]
    product = grad * o_ref[rows, cols].astype(F32)
    grad_low = grad.astype(BF16)
    queries = q_ref[rows, cols]
    key_pair = k_ref[keys, cols]
    value_pair = v_ref[keys, cols]
    grad_turned = grad.T.astype(BF16)
    queries_turned = queries.astype(F32).T.astype(BF16)
    grad_q, grad_k, grad_v = [], [], []
    for which in range(2):
        inner = jnp.sum(one_head(which, product), axis=1, keepdims=True)
        grad_probs = dot(one_head(which, grad_low), value_pair, NT)
        powers = e_ref[pair * 2 + which, rows, :]
        grad_scores = (powers.astype(F32) * (grad_probs - inner)).astype(BF16)
        grad_q.append(dot(grad_scores, key_pair))
        head = slice(which * 64, which * 64 + 64)
        grad_v.append(dot(grad_turned[head], powers))
        grad_k.append(dot(queries_turned[head], grad_scores))
    dq_ref[rows, cols] = (join_heads(*grad_q) * scale).astype(BF16)
    dk_ref[keys, cols] = jnp.concatenate(grad_k, axis=0).T.astype(BF16)
    dv_ref[keys, cols] = jnp.concatenate(grad_v, axis=0).T.astype(BF16)


def attend_back_kernel(number, cross, own, swaps, total, after, tick, *refs):
    refs = list(refs)
    take = lambda count: [refs.pop(0) for _ in range(count)]
    if total:
        total.refs = take(len(total.terms))
    do_ref, o_ref, inv_ref, q_ref, ks_ref, vs_ref, kl_ref, vl_ref, es_ref, el_ref, resid_ref, *ins = take(
        11 + (2 if cross else number)
    )
    wq_ref, wk_ref, wv_ref = take(3)
    mates = take(number)
    dx_ref = take(1)[0]
    if cross:
        dy_ref, dmate_ref, dwq_ref, dwk_ref, dwv_ref = take(5)
    dqs, dks, dvs, dql, dkl, dvl, mate_sum, mate_low, resid_sem, *scratch = refs
    step = pl.program_id(0)
    first = step % 2 == 0
    if cross:
        xq_ref, xk_ref, mate_ref = ins[0], ins[1], mates[0]
        dy_ref = dy_ref.at[0]
    else:
        xq_ref = xk_ref = scratch[0]
        mate_ref = scratch[1]
        terms_ref = scratch[2]
        for place, flow in enumerate(own):
            kind, start = OWN_PARTS[place // 2]
            every = (slice(None),) * len(flow.order)
            flow.source = terms_ref.at[(kind, place % 2) + every + (slice(start, start + flow.block[0]),)]
        for index in range(number):
            swaps[index].source = mate_low.at[index]

            @pl.when(step == 2 * (number - 1 - index))
            def _():
                xq_ref[...] = ins[index][...]
                mate_ref[...] = mates[index][...]

        dy_ref = dx_ref.at[0]
    dx_ref = dx_ref.at[0]
    rows = xq_ref.shape[1]
    load = pltpu.make_async_copy(resid_ref.at[number - 1 - step // 2], dx_ref, resid_sem)

    @pl.when(first)
    def _():
        load.start()

    scale = 0.125
    everything = slice(None)
    tick(0)
    pairs = COLS // 128

    def long_pair(pair, carry):
        attend_back_rows(
            do_ref.at[0, 1],
            o_ref.at[0, 1],
            inv_ref.at[0, 1],
            q_ref.at[0, 1],
            kl_ref.at[0],
            vl_ref.at[0],
            el_ref.at[0],
            dql,
            dkl,
            dvl,
            everything,
            everything,
            pair,
            scale,
        )
        for index in range(pairs):
            tick(1 + index, pair == index)
        return carry

    def short_slot(slot, carry):
        here = pl.ds(pl.multiple_of(slot * SHORT, SHORT), SHORT)
        for pair in range(pairs):
            attend_back_rows(
                do_ref.at[0, 0],
                o_ref.at[0, 0],
                inv_ref.at[0, 0],
                q_ref.at[0, 0],
                ks_ref.at[0],
                vs_ref.at[0],
                es_ref.at[0],
                dqs,
                dks,
                dvs,
                here,
                here,
                pair,
                scale,
            )
        return carry

    lax.fori_loop(0, pairs, long_pair, 0)
    lax.fori_loop(0, rows // SHORT, short_slot, 0)
    tick(3)
    wq, wk, wv = wq_ref[0], wk_ref[0], wv_ref[0]
    front = slice(0, rows)
    other = slice(rows, 2 * rows)
    dwq = dot(xq_ref[0], dqs[...], TN) + dot(xq_ref[1], dql[...], TN)
    short, long, mate = xk_ref[0], xk_ref[1], mate_ref[...]
    dwk = dot(short, dks[...], TN) + dot(long, dkl[front], TN) + dot(mate, dkl[other], TN)
    dwv = dot(short, dvs[...], TN) + dot(long, dvl[front], TN) + dot(mate, dvl[other], TN)
    if cross:
        dwq_ref[...] = dwq.astype(BF16)
        dwk_ref[...] = dwk.astype(BF16)
        dwv_ref[...] = dwv.astype(BF16)
    else:
        flow = own[0]
        _, share, columns = flow.block
        for index, total_w in enumerate((dwq, dwk, dwv)):
            low = total_w.astype(BF16)
            for device in range(low.shape[0] // share):
                at = tuple((device >> bit) & 1 for bit in reversed(range(len(flow.order))))
                for color in range(2):
                    terms_ref[(1 - step // 2, color) + at + (step % 2 * 3 + index,)] = low[
                        device * share : (device + 1) * share, color * columns : (color + 1) * columns
                    ]

    tick(4)

    @pl.when(first)
    def _():
        load.wait()
        if cross:
            dy_ref[...] = jnp.zeros_like(dy_ref)
        mate_sum[...] = jnp.zeros_like(mate_sum)

    mate_sum[...] += dot(dkl[other], wk, NT) + dot(dvl[other], wv, NT)
    if cross:

        @pl.when(jnp.logical_not(first))
        def _():
            dmate_ref[...] = mate_sum[...].astype(BF16)

    else:
        for index in range(number):

            @pl.when(step == 2 * (number - 1 - index) + 1)
            def _():
                mate_low[index] = mate_sum[...].astype(BF16)

    tick(5)
    dx_ref[0] += dot(dqs[...], wq, NT)
    dx_ref[1] += dot(dql[...], wq, NT)
    dy_ref[0] += dot(dks[...], wk, NT) + dot(dvs[...], wv, NT)
    dy_ref[1] += dot(dkl[front], wk, NT) + dot(dvl[front], wv, NT)
    for slot in range(6, 6 + after):
        tick(slot)


def attend_back(grad, saved, mates, resid, xs, cross, weights, base, flows, plan, collective, last=None):
    _, rows, width = xs[0].shape
    number = 1 if cross else len(xs)
    place = lambda step: number - 1 - step // 2
    weight = lambda index: (
        weights,
        pl.BlockSpec((1, width, COLS), lambda step: (base + 4 * place(step) + index, 0, step % 2)),
    )
    both = pl.BlockSpec((1, 2, rows, COLS), lambda step: (place(step), 0, 0, step % 2))
    cols = lambda count: pl.BlockSpec((1, count, COLS), lambda step: (place(step), 0, step % 2))
    powers = lambda count: pl.BlockSpec((1, COLS // 64, rows, count), lambda step: (place(step), step % 2, 0, 0))
    deep = pl.BlockSpec((1, 2, rows, width), lambda step: (place(step), 0, 0, 0))
    flops = 2 * rows * width * width * 14 + 8 * rows * width * (SHORT + LONG)
    specs = [both] * 4 + [cols(rows)] * 2 + [cols(LONG)] * 2 + [powers(SHORT), powers(LONG)]
    o, inverse, *rest = saved
    own, swaps, total = last or ((), (), None)
    data = (shaped((number, 2, rows, width), F32), deep)
    outs = [data]
    scratch = (
        [pltpu.VMEM((rows, COLS), BF16)] * 4
        + [pltpu.VMEM((LONG, COLS), BF16)] * 2
        + [pltpu.VMEM((rows, width), F32), pltpu.VMEM((number, rows, width), BF16)]
        + [pltpu.SemaphoreType.DMA]
    )
    if cross:
        outs += [data, (shaped((rows, width), BF16), pl.BlockSpec((rows, width), lambda step: (0, 0)))]
        outs += [(shaped((width, width), BF16), pl.BlockSpec((width, COLS), lambda step: (0, step)))] * 3
    else:
        scratch += [pltpu.VMEM((2, rows, width), BF16), pltpu.VMEM((rows, width), BF16)]
        _, share, columns = own[0].block
        scratch += [pltpu.VMEM((number, 2) + own[0].shape(0)[:-3] + (6, share, columns), BF16)]
    after = 1 + max([spot for _, spot in plan] + [5]) - 6
    norms = total.terms if total else []
    return call(
        functools.partial(attend_back_kernel, number, cross, own, swaps, total, after),
        2 * number,
        [(array, whole(array)) for array in norms]
        + list(zip((grad, o, inverse, *rest), specs))
        + [(resid, pl.BlockSpec(memory_space=pl.ANY))]
        + [(array, whole(array)) for array in xs]
        + [weight(0), weight(1), weight(2)]
        + [(array, whole(array)) for array in mates],
        outs,
        scratch,
        "attend_back",
        cost(flops * 2 * number, number * (28 << 20)),
        flows,
        plan,
        collective,
    )


BLOCK = 512
WIDE = 1024
ANY = pl.BlockSpec(memory_space=pl.ANY)


def norm_parts(resid):
    average = jnp.mean(resid, axis=-1, keepdims=True)
    centered = resid - average
    variance = jnp.mean(centered * centered, axis=-1, keepdims=True)
    spread = lax.rsqrt(variance + EPSILON)
    return centered * spread, spread


def norm_back(normal, spread, gain, grad):
    scaled = grad * gain
    first = jnp.mean(scaled, axis=-1, keepdims=True)
    second = jnp.mean(scaled * normal, axis=-1, keepdims=True)
    return (scaled - first - normal * second) * spread


def add_norm_grads(ref, place, grad, normal):
    ref[place : place + 1, :] += jnp.sum(grad * normal, axis=0, keepdims=True)
    ref[8 + place : 9 + place, :] += jnp.sum(grad, axis=0, keepdims=True)


def logistic(value):
    return 1.0 / (1.0 + jnp.exp(-value))


def each_block(count, work, size=BLOCK):
    def step(index, carry):
        work(pl.ds(pl.multiple_of(index * size, size), size))
        return carry

    lax.fori_loop(0, count // size, step, 0)


def each_chunk(count, work):
    def step(index, carry):
        work(index)
        return carry

    lax.fori_loop(0, count, step, 0)


class Loads:
    def __init__(self, pairs, sems):
        self.copies = [
            pltpu.make_async_copy(source, target, sems.at[index])
            for index, (source, target) in enumerate(pairs)
        ]

    def start(self):
        for copy in self.copies:
            copy.start()

    def wait(self, *places):
        for place in places:
            self.copies[place].wait()


def chunk_loads(up_ref, down_ref, up_s, down_s, sems):
    def copies(chunk):
        part = pl.ds(pl.multiple_of(chunk * CHUNK, CHUNK), CHUNK)
        return (
            pltpu.make_async_copy(up_ref.at[:, part], up_s.at[chunk], sems.at[0, chunk]),
            pltpu.make_async_copy(down_ref.at[part], down_s.at[chunk], sems.at[1, chunk]),
        )

    return copies


def feed_chunks(copies, low_s, total_s, up_s, down_s, u_s, a_s, out=None):
    count = low_s.shape[0]

    def chunk_work(chunk):
        for copy in copies(chunk):
            copy.wait()

        def block_work(rows):
            upward = dot(low_s[rows, :], up_s[chunk])
            u_s[chunk, rows, :] = upward
            active = (upward * logistic(upward)).astype(BF16)
            if a_s is not None:
                a_s[chunk, rows, :] = active
            total_s[rows, :] += dot(active, down_s[chunk])

        each_block(count, block_work, WIDE)
        if out is not None:
            out(chunk)

    each_chunk(up_s.shape[0], chunk_work)


def feed_back_chunks(tick, wait, low_s, hidden_s, total_s, up_s, down_s, u_s, a_s, du_s, write):
    count = low_s.shape[0]
    chunks = up_s.shape[0]

    def chunk_work(chunk):
        wait(chunk)
        store = a_s is None
        active_ref = du_s.at[1] if store else a_s.at[chunk]

        def block_work(rows):
            upward = u_s[chunk, rows, :]
            gate = logistic(upward)
            if store:
                active_ref[rows, :] = (upward * gate).astype(BF16)
            grad_active = dot(low_s[rows, :], down_s[chunk], NT)
            grad_up = (grad_active * gate * (1.0 + upward * (1.0 - gate))).astype(BF16)
            du_s[0, rows, :] = grad_up
            total_s[rows, :] += dot(grad_up, up_s[chunk], NT)

        each_block(count, block_work, WIDE)
        write(chunk, dot(hidden_s[...], du_s[0], TN), dot(active_ref[...], low_s[...], TN))
        for index in range(chunks):
            tick(2 + index, chunk == index)

    each_chunk(chunks, chunk_work)


def feed_kernel(
    tick,
    os_ref,
    x_ref,
    z_ref,
    wm_ref,
    wo_ref,
    up_ref,
    down_ref,
    gain_ref,
    shift_ref,
    u_ref,
    r1_ref,
    r2_ref,
    enc_ref,
    r3_ref,
    h3_ref,
    *scratch,
):
    up_s, down_s, u_s, low_s, sems, out_sems = scratch
    copies = chunk_loads(up_ref.at[0], down_ref.at[0], up_s, down_s, sems)
    chunks = up_s.shape[0]
    for chunk in range(chunks):
        for copy in copies(chunk):
            copy.start()
    count = low_s.shape[0]

    def first(rows):
        resid = x_ref[rows, :].astype(F32) + dot(os_ref[0, rows, :], wo_ref[0])
        r1_ref[rows, :] = resid
        normal, _ = norm_parts(resid)
        hidden = normal * gain_ref[0:1] + shift_ref[0:1]
        r2_ref[rows, :] = hidden
        low_s[rows, :] = hidden.astype(BF16)
        resid = z_ref[rows, :].astype(F32) + dot(os_ref[1, rows, :], wm_ref[0])
        r3_ref[rows, :] = resid
        normal, _ = norm_parts(resid)
        h3_ref[rows, :] = (normal * gain_ref[2:3] + shift_ref[2:3]).astype(BF16)

    each_block(count, first)
    keep = lambda chunk: pltpu.make_async_copy(u_s.at[chunk], u_ref.at[chunk], out_sems.at[chunk])
    feed_chunks(copies, low_s, r2_ref, up_s, down_s, u_s, None, lambda chunk: keep(chunk).start())

    def last(rows):
        normal, _ = norm_parts(r2_ref[rows, :])
        enc_ref[rows, :] = (normal * gain_ref[1:2] + shift_ref[1:2]).astype(BF16)

    each_block(count, last)
    for chunk in range(chunks):
        keep(chunk).wait()


def picked(array, index):
    return array, pl.BlockSpec((1,) + array.shape[1:], lambda step: (index, 0, 0))


def flat(array):
    return array.reshape((-1,) + array.shape[2:])


def full(array):
    return array, whole(array)


def new(kind, *shape):
    return shaped(shape, kind), pl.BlockSpec(shape, lambda step: (0,) * len(shape))


def weight_scratch(width, chunks):
    return [
        pltpu.VMEM((chunks, width, CHUNK), BF16),
        pltpu.VMEM((chunks, CHUNK, width), BF16),
    ]


def feed(o, x, z, attn, ups, downs, gains, shifts):
    shape = x.shape
    o, x, z = o.reshape((2, -1, shape[-1])), flat(x), flat(z)
    count, width = x.shape
    inner = ups.shape[2]
    chunks = inner // CHUNK
    results, _ = call(
        feed_kernel,
        1,
        [full(o), full(x), full(z), picked(attn, 7), picked(attn, 3)]
        + [(ups, ANY), (downs, ANY), full(gains), full(shifts)],
        [
            (shaped((chunks, count, CHUNK), F32), ANY),
            new(F32, count, width),
            new(F32, count, width),
            new(BF16, count, width),
            new(F32, count, width),
            new(BF16, count, width),
        ],
        weight_scratch(width, chunks)
        + [
            pltpu.VMEM((chunks, count, CHUNK), F32),
            pltpu.VMEM((count, width), BF16),
            pltpu.SemaphoreType.DMA((2, chunks)),
            pltpu.SemaphoreType.DMA((chunks,)),
        ],
        "feed",
        cost(2 * count * width * (2 * width + 2 * inner), 28 << 20, 2 * count * inner),
    )
    u, r1, r2, enc, r3, h3 = results
    return u, r1, r2, enc.reshape(shape), r3, h3.reshape(shape)


def turn_kernel(
    tick,
    o_ref,
    r3_ref,
    wo_ref,
    cot_ref,
    up_ref,
    down_ref,
    gain_ref,
    shift_ref,
    out_ref,
    dr_ref,
    do_ref,
    dup_ref,
    ddown_ref,
    dwo_ref,
    norm_ref,
    *scratch,
):
    up_s, down_s, u_s, a_s, low_s, hidden_s, du_s, cot_s, total_s, normal_s, spread_s, sems, cot_sem = scratch
    copies = chunk_loads(up_ref.at[1], down_ref.at[1], up_s, down_s, sems)
    chunks = up_s.shape[0]
    for chunk in range(chunks):
        for copy in copies(chunk):
            copy.start()
    load = pltpu.make_async_copy(cot_ref, cot_s, cot_sem)
    load.start()
    count = low_s.shape[0]
    norm_ref[...] = jnp.zeros_like(norm_ref)

    def first(rows):
        normal3, _ = norm_parts(r3_ref[rows, :])
        resid4 = normal3 * gain_ref[2:3] + shift_ref[2:3] + dot(o_ref[rows, :], wo_ref[0])
        normal4, spread4 = norm_parts(resid4)
        hidden = normal4 * gain_ref[3:4] + shift_ref[3:4]
        normal_s[rows, :] = normal4
        spread_s[rows, :] = spread4
        total_s[rows, :] = hidden
        hidden_s[rows, :] = hidden.astype(BF16)

    each_block(count, first)
    feed_chunks(copies, hidden_s, total_s, up_s, down_s, u_s, a_s)
    load.wait()

    def top(rows):
        normal5, spread5 = norm_parts(total_s[rows, :])
        out_ref[rows, :] = (normal5 * gain_ref[4:5] + shift_ref[4:5]).astype(BF16)
        grad = cot_s[rows, :].astype(F32)
        add_norm_grads(norm_ref, 4, grad, normal5)
        grad = norm_back(normal5, spread5, gain_ref[4:5], grad)
        total_s[rows, :] = grad
        low_s[rows, :] = grad.astype(BF16)

    each_block(count, top)

    def write(chunk, dup, ddown):
        dup_ref[chunk] = dup.astype(BF16)
        ddown_ref[chunk] = ddown.astype(BF16)

    feed_back_chunks(
        tick, lambda chunk: None, low_s, hidden_s, total_s, up_s, down_s, u_s, a_s, du_s, write
    )

    def bottom(rows):
        grad = total_s[rows, :]
        normal4 = normal_s[rows, :]
        add_norm_grads(norm_ref, 3, grad, normal4)
        grad = norm_back(normal4, spread_s[rows, :], gain_ref[3:4], grad)
        dr_ref[rows, :] = grad
        low = grad.astype(BF16)
        low_s[rows, :] = low
        do_ref[rows, :] = dot(low, wo_ref[0], NT).astype(BF16)

    each_block(count, bottom)
    dwo_ref[...] = dot(o_ref[...], low_s[...], TN).astype(BF16)


def turn(o, r3, cot, attn, ups, downs, gains, shifts):
    rows = cot.shape[1]
    o, cot = flat(flat(o)), flat(cot)
    count, width = r3.shape
    inner = ups.shape[2]
    chunks = inner // CHUNK
    wide = pltpu.VMEM((count, width), BF16)
    results, _ = call(
        turn_kernel,
        1,
        [full(o), full(r3), picked(attn, 11), (cot, ANY), (ups, ANY), (downs, ANY), full(gains), full(shifts)],
        [
            new(BF16, count, width),
            new(F32, count, width),
            new(BF16, count, width),
            new(BF16, chunks, width, CHUNK),
            new(BF16, chunks, CHUNK, width),
            new(BF16, width, width),
            new(F32, 16, width),
        ],
        weight_scratch(width, chunks)
        + [
            pltpu.VMEM((chunks, count, CHUNK), F32),
            pltpu.VMEM((chunks, count, CHUNK), BF16),
            wide,
            wide,
            pltpu.VMEM((1, count, CHUNK), BF16),
            wide,
            pltpu.VMEM((count, width), F32),
            pltpu.VMEM((count, width), F32),
            pltpu.VMEM((count, 1), F32),
            pltpu.SemaphoreType.DMA((2, chunks)),
            pltpu.SemaphoreType.DMA,
        ],
        "turn",
        cost(6 * count * width * (width + 2 * inner), 20 << 20, 4 * count * inner),
    )
    out, dr, do, dup, ddown, dwo, norms = results
    pair = lambda array: array.reshape((2, rows) + array.shape[1:])
    return pair(out), pair(dr)[None], pair(do)[None], dup, ddown.reshape(inner, width), dwo, norms


def feed_back_kernel(
    mate,
    tick,
    gradm_ref,
    r3_ref,
    wm_ref,
    wo_ref,
    grad_ref,
    r2_ref,
    r1_ref,
    os_ref,
    u_ref,
    up_ref,
    down_ref,
    gain_ref,
    shift_ref,
    dr_ref,
    do_ref,
    dup_ref,
    ddown_ref,
    dwo_ref,
    dwm_ref,
    norm_ref,
    *scratch,
):
    (
        up_s,
        down_s,
        u_s,
        low_s,
        hidden_s,
        du_s,
        total_s,
        normal_s,
        spread_s,
        grad_s,
        r2_s,
        r1_s,
        os_s,
        sems,
        u_sems,
        in_sems,
    ) = scratch
    copies = chunk_loads(up_ref.at[0], down_ref.at[0], up_s, down_s, sems)
    chunks = up_s.shape[0]
    keep = lambda chunk: pltpu.make_async_copy(u_ref.at[chunk], u_s.at[chunk], u_sems.at[chunk])
    late = Loads([(os_ref, os_s), (grad_ref, grad_s), (r2_ref, r2_s), (r1_ref, r1_s)], in_sems)
    late.start()
    for chunk in range(chunks):
        keep(chunk).start()
        for copy in copies(chunk):
            copy.start()
    tick(0)
    count = low_s.shape[0]
    half = count // 2
    norm_ref[...] = jnp.zeros_like(norm_ref)

    def middle(rows):
        grad = gradm_ref[rows, :]
        normal, spread = norm_parts(r3_ref[rows, :])
        add_norm_grads(norm_ref, 2, grad, normal)
        grad = norm_back(normal, spread, gain_ref[2:3], grad)
        dr_ref[1, rows, :] = grad
        low = grad.astype(BF16)
        low_s[rows, :] = low
        do_ref[1, rows, :] = dot(low, wm_ref[0], NT).astype(BF16)

    each_block(count, middle)
    late.wait(0)
    dwm_ref[...] = dot(os_s[1], low_s[...], TN).astype(BF16)
    tick(1)

    def first(rows, grad):
        normal2, spread2 = norm_parts(r2_s[rows, :])
        add_norm_grads(norm_ref, 1, grad, normal2)
        grad = norm_back(normal2, spread2, gain_ref[1:2], grad)
        total_s[rows, :] = grad
        low_s[rows, :] = grad.astype(BF16)
        normal1, spread1 = norm_parts(r1_s[rows, :])
        normal_s[rows, :] = normal1
        spread_s[rows, :] = spread1
        hidden_s[rows, :] = (normal1 * gain_ref[0:1] + shift_ref[0:1]).astype(BF16)

    late.wait(1, 2, 3)
    each_block(half, lambda rows: first(rows, grad_s[rows, :]))

    def long(index, carry):
        start = pl.multiple_of(index * BLOCK, BLOCK)
        rows = pl.ds(pl.multiple_of(start + half, BLOCK), BLOCK)
        first(rows, grad_s[rows, :] + mate.got[pl.ds(start, BLOCK), :].astype(F32))
        return carry

    lax.fori_loop(0, half // BLOCK, long, 0)

    def write(chunk, dup, ddown):
        dup_ref[chunk] = dup.astype(BF16)
        ddown_ref[chunk] = ddown.astype(BF16)

    def wait(chunk):
        keep(chunk).wait()
        for copy in copies(chunk):
            copy.wait()

    feed_back_chunks(tick, wait, low_s, hidden_s, total_s, up_s, down_s, u_s, None, du_s, write)

    def bottom(rows):
        grad = total_s[rows, :]
        normal1 = normal_s[rows, :]
        add_norm_grads(norm_ref, 0, grad, normal1)
        grad = norm_back(normal1, spread_s[rows, :], gain_ref[0:1], grad)
        dr_ref[0, rows, :] = grad
        low = grad.astype(BF16)
        low_s[rows, :] = low
        do_ref[0, rows, :] = dot(low, wo_ref[0], NT).astype(BF16)

    each_block(count, bottom)
    dwo_ref[...] = dot(os_s[0], low_s[...], TN).astype(BF16)
    tick(2 + chunks)


def feed_back(gradm, r3, grad, r2, r1, u, o, attn, ups, downs, gains, shifts, mate, flows, plan, collective):
    gradm, grad = flat(flat(gradm)), flat(flat(grad))
    o = o.reshape((2,) + grad.shape)
    count, width = r1.shape
    inner = ups.shape[2]
    chunks = inner // CHUNK
    wide = pltpu.VMEM((count, width), BF16)
    deep = pltpu.VMEM((count, width), F32)
    results, sums = call(
        functools.partial(feed_back_kernel, mate),
        1,
        [full(gradm), full(r3), picked(attn, 7), picked(attn, 3)]
        + [(array, ANY) for array in (grad, r2, r1, o, u, ups, downs)]
        + [full(gains), full(shifts)],
        [
            new(F32, 2, count, width),
            new(BF16, 2, count, width),
            new(BF16, chunks, width, CHUNK),
            new(BF16, chunks, CHUNK, width),
            new(BF16, width, width),
            new(BF16, width, width),
            new(F32, 16, width),
        ],
        weight_scratch(width, chunks)
        + [
            pltpu.VMEM((chunks, count, CHUNK), F32),
            wide,
            wide,
            pltpu.VMEM((2, count, CHUNK), BF16),
            deep,
            deep,
            pltpu.VMEM((count, 1), F32),
            deep,
            deep,
            deep,
            pltpu.VMEM((2, count, width), BF16),
            pltpu.SemaphoreType.DMA((2, chunks)),
            pltpu.SemaphoreType.DMA((chunks,)),
            pltpu.SemaphoreType.DMA((4,)),
        ],
        "feed_back",
        cost(4 * count * width * (2 * width + 2 * inner), 36 << 20, 2 * count * inner),
        flows,
        plan,
        collective,
    )
    dr, do, dup, ddown, dwo, dwm, norms = results
    halves = lambda array: array.reshape((2, 2, count // 2, width))
    return (halves(dr), halves(do), dup, ddown.reshape(inner, width), dwo, dwm, norms), sums


def finish_kernel(counts, part_ref, src_mate_ref, tgt_mate_ref, norm_ref, *refs):
    sums, outs = refs[: -7], refs[-7:]
    gs_ref, gt_ref, attn_ref, up_ref, down_ref, gain_ref, shift_ref = outs
    long = pl.program_id(0) >= pl.num_programs(0) // 2
    for index, mate_ref, out_ref in ((0, src_mate_ref, gs_ref), (1, tgt_mate_ref, gt_ref)):

        @pl.when(long)
        def _():
            out_ref[...] = part_ref[index] + mate_ref[...].astype(F32)[None]

        @pl.when(jnp.logical_not(long))
        def _():
            out_ref[...] = part_ref[index]

    @pl.when(pl.program_id(0) == 0)
    def _():
        for ref, (kind, index, cols) in zip(sums, counts):
            share = ref.shape[-2]
            if kind == "attn":
                for number, place in enumerate(index):
                    attn_ref[place, :, cols[number]] = ref[number]
                continue
            tiles = up_ref.shape[2] // CHUNK
            index, place = index
            for number in range(ref.shape[0]):
                tile = tiles - 1 if kind == "both" else number
                if place is not None and number == tiles - 1:
                    attn_ref[place, :, :] = ref[number]
                elif kind == "up" or (kind == "both" and number == 0):
                    up_ref[index, :, tile * CHUNK : (tile + 1) * CHUNK] = ref[number]
                else:
                    down_ref[index, tile * share : (tile + 1) * share, :] = ref[number]
        share = gain_ref.shape[1]
        here = lax.axis_index("dp") * lax.axis_size("head") + lax.axis_index("head")
        width = norm_ref.shape[1]
        turned = pltpu.roll(norm_ref[...], (width - here * share) % width, axis=1)
        gain_ref[...] = turned[:5, :share]
        shift_ref[...] = turned[8:13, :share]


def finish(data, source_mate, target_mate, norms, named, share, inner, devices):
    _, _, rows, width = data.shape
    half = rows // 2
    row = pl.BlockSpec((1, half, width), lambda step: (step // 2, step % 2, 0))
    mate = pl.BlockSpec((half, width), lambda step: (step % 2, 0))
    sums = [array for array, *_ in named]
    counts = [tuple(rest) for _, *rest in named]
    outs = [
        (shaped((2, rows, width), F32), row),
        (shaped((2, rows, width), F32), row),
    ]
    for shape in ((12, share, width), (2, share, inner), (2, inner // devices, width), (5, share), (5, share)):
        outs.append((shaped(shape, F32), pl.BlockSpec(shape, lambda step, size=len(shape): (0,) * size)))
    return pl.pallas_call(
        functools.partial(finish_kernel, counts),
        grid=(4,),
        out_shape=[shape for shape, _ in outs],
        in_specs=[pl.BlockSpec((2, 1, half, width), lambda step: (0, step // 2, step % 2, 0)), mate, mate, whole(norms)] + [whole(array) for array in sums],
        out_specs=[spec for _, spec in outs],
        compiler_params=params(),
        cost_estimate=cost(0, 11 << 20),
        name="finish",
    )(data, source_mate, target_mate, norms, *sums)


CROSS_FFN = [(0, 2), (1, 2)]
FEED_FFN = [(0, 2), (0, 4), (0, 6)]
FEED_CROSS = [(0, 2), (0, 5), (0, 6)]
LAST_FFN = [(0, 2), (1, 4), (2, 4), (3, 1), (3, 6)]
LAST_CROSS = [(0, 2), (1, 4)]
LAST_NORMS = [(0, 2), (1, 1), (1, 4), (2, 1), (2, 4), (3, 1)]
LAST_OWN = [
    [(1, 4), (2, 1), (2, 4), (3, 1), (3, 4), (3, 6)],
    [(2, 4), (3, 1), (3, 4), (3, 6), (3, 7), (3, 8)],
    [(3, 4), (3, 6), (3, 7), (3, 8), (3, 9), (3, 10)],
]
OWN_PARTS = [(1, 0), (0, 0), (0, 3)]


def place_stages(plan, numbers, stages, start, spots):
    plan.setdefault(start, []).extend((number, None) for number in numbers)
    for index, stage in enumerate(stages):
        plan.setdefault(spots[min(index, len(spots) - 1)], []).extend((number, stage) for number in numbers)


def body(
    source,
    target,
    cotangent,
    short_lengths,
    long_lengths,
    attn,
    ups,
    downs,
    gains,
    shifts,
):
    _, rows, width = source.shape
    inner = ups.shape[2]
    devices = lax.axis_size("dp") * lax.axis_size("head")
    bits = devices.bit_length() - 1
    assert 2 * rows == LONG and rows % SHORT == 0 and devices == 1 << bits
    share = width // devices
    parts = (2,) * bits
    lengths = (short_lengths, long_lengths)
    orders = (
        tuple(range(bits)),
        (0, 2, 1) + tuple(range(3, bits)),
        (0,) + tuple(range(3, bits)) + (1, 2),
    )
    tiles = inner // width

    def square(array):
        return array.reshape(parts + (1, share, width)), None, 0, 1

    def ffn_flows(last, dup, ddown, extra=((), ())):
        up = dup.reshape((tiles,) + parts + (1, share, width))
        down = ddown.reshape(parts + (tiles, share, width))
        most = tiles - 1
        pieces = (
            [(up, index, 0, 1) for index in range(most)] + [square(array) for array in extra[0]],
            [(down, None, 0, most)] + [square(array) for array in extra[1]],
            [(up, most, 0, 1), (down, None, most, 1)],
        )
        return [Flow(order, 0, last, piece) for order, piece in zip(orders, pieces)]

    def attn_flows(last, *groups):
        pieces = [[square(array) for array in group] for group in groups]
        return [Flow(order, 0, last, piece) for order, piece in zip(orders, pieces)]

    def later(first, last, partial):
        return [
            Flow(order, first, last, [(part, None, 0, part.shape[-3])])
            for order, part in zip(orders, partial)
        ]

    self_saved, mates = attend((source, target), (False, True), False, attn, 0, lengths, 0)
    u, r1, r2, enc, r3, h3 = feed(self_saved[0], source, target, attn, ups, downs, gains, shifts)
    cross_saved, enc_mates = attend((h3, enc), (False,), True, attn, 8, lengths, 1)
    decoded, dr4, do_cross, dup1, ddown1, dw11, norms_a = turn(
        cross_saved[0], r3, cotangent, attn, ups, downs, gains, shifts
    )

    plan = {}
    place_stages(plan, (0, 1, 2), range(2), (0, 0), CROSS_FFN)
    (dh3, denc, denc_mate, dw8, dw9, dw10), ffn1 = attend_back(
        do_cross,
        cross_saved,
        enc_mates,
        dr4,
        (h3, enc),
        True,
        attn,
        8,
        ffn_flows(2, dup1, ddown1),
        plan,
        2,
    )

    plan = {}
    mate = Swap(0, (rows, width), denc_mate, kept=False)
    place_stages(plan, (5,), [0], (0, 0), [(0, 1)])
    place_stages(plan, (0, 1, 2), range(2, bits), (0, 0), FEED_FFN)
    place_stages(plan, (3, 4), range(3), (0, 0), FEED_CROSS)
    (dr, do, dup0, ddown0, dw3, dw7, norms_b), sums = feed_back(
        dh3,
        r3,
        denc,
        r2,
        r1,
        u,
        self_saved[0],
        attn,
        ups,
        downs,
        gains,
        shifts,
        mate,
        later(2, bits, ffn1) + attn_flows(3, [dw8, dw11], [dw9, dw10]) + [mate],
        plan,
        3,
    )
    ffn1, cross = sums[:3], sums[3:]

    plan = {}
    stages = range(bits)
    own = [
        Flow(order, 0, bits, [], (count, share, COLS // 2)) for count in (6, 3, 3) for order in orders[:2]
    ]
    swaps = [Swap(0, (rows, width)) for _ in range(2)]
    total = Total(bits, [norms_a, norms_b])
    place_stages(plan, (3, 4), range(3, bits), (0, 0), LAST_CROSS)
    place_stages(plan, (0, 1, 2), stages, (0, 0), LAST_FFN)
    place_stages(plan, (5,), stages, LAST_NORMS[0], LAST_NORMS[1:])
    for index, spots in enumerate(LAST_OWN):
        place_stages(plan, (6 + 2 * index, 7 + 2 * index), stages, spots[0], spots[1:])
    place_stages(plan, (13,), [0], (1, 5), [(2, 1)])
    place_stages(plan, (12,), [0], (3, 5), [(3, 7)])
    (data,), sums = attend_back(
        do,
        self_saved,
        mates,
        dr,
        (source, target),
        False,
        attn,
        0,
        ffn_flows(bits, dup0, ddown0, ([dw3], [dw7]))
        + later(3, bits, cross)
        + [total]
        + own
        + swaps,
        plan,
        4,
        (own, swaps, total),
    )
    ffn0, cross = sums[:3], sums[3:5]
    norms, *own_sums, source_back, target_back = sums[5:]

    everything = slice(None)
    named = [(array, "attn", places, (everything,) * 2) for array, places in zip(cross, ((8, 11), (9, 10)))]
    for index, sums in enumerate((ffn0, ffn1)):
        squares = (3, 7, None) if index == 0 else (None,) * 3
        named += [
            (array, kind, (index, place), None) for array, kind, place in zip(sums, ("up", "down", "both"), squares)
        ]
    for number, array in enumerate(own_sums):
        kind, first = OWN_PARTS[number // 2]
        places, cols = [], []
        for index in range(first, first + array.shape[0]):
            start = index // 3 * COLS + number % 2 * (COLS // 2)
            places.append(4 * kind + index % 3)
            cols.append(slice(start, start + COLS // 2))
        named.append((array, "attn", tuple(places), tuple(cols)))
    grad_source, grad_target, grad_attn, grad_up, grad_down, grad_gains, grad_shifts = finish(
        data, source_back, target_back, norms, named, share, inner, devices
    )
    return decoded, grad_source, grad_target, grad_attn, grad_up, grad_down, grad_gains, grad_shifts


def solution(mesh):
    rows = P(None, AXES, None)
    return jax.shard_map(
        body,
        mesh=mesh,
        in_specs=(rows, rows, rows, P(None, "dp"), P(None, "dp"), P(), P(), P(), P(), P()),
        out_specs=(rows, rows, rows, rows, rows, rows, P(None, AXES), P(None, AXES)),
        check_vma=False,
    )
```

```python
import functools
import math

import jax
import jax.numpy as jnp
from jax import lax
from jax.experimental import pallas as pl
from jax.experimental.pallas import tpu as pltpu
from jax.sharding import PartitionSpec as P

HEADS = 8
SHORT = 256
LONG = 1024

EPSILON = 1e-05
MASKED = -1e30
F32 = jnp.float32
BF16 = jnp.bfloat16
AXES = ("dp", "head")
COLS = 256
CHUNK = 512

NN = (((1,), (0,)), ((), ()))
NT = (((1,), (1,)), ((), ()))
TN = (((0,), (0,)), ((), ()))


def dot(left, right, dims=NN):
    return lax.dot_general(left, right, dims, preferred_element_type=F32)


def params():
    return pltpu.CompilerParams(vmem_limit_bytes=63 << 20)


def cost(flops, moved, powers=0):
    return pl.CostEstimate(flops=int(flops), bytes_accessed=int(moved), transcendentals=int(powers))


def whole(array):
    return pl.BlockSpec(array.shape, lambda *step: (0,) * array.ndim, pipeline_mode=pl.Buffered(1))


def shaped(shape, kind):
    return jax.ShapeDtypeStruct(shape, kind)


def lanes():
    return lax.broadcasted_iota(jnp.int32, (1, 128), 1)


def one_head(which, pair):
    keep = (lanes() < 64) if which == 0 else (lanes() >= 64)
    return jnp.where(keep, pair, jnp.zeros_like(pair))


def join_heads(first, second):
    return jnp.where(lanes() < 64, first, second)


MESH = pl.DeviceIdType.MESH


def partner(bit):
    head_bits = lax.axis_size("head").bit_length() - 1
    data, head = lax.axis_index("dp"), lax.axis_index("head")
    if bit < head_bits:
        step = 1 << bit
        mine = (head // step) % 2
        return mine, (data, head + (1 - 2 * mine) * step)
    step = 1 << (bit - head_bits)
    mine = (data // step) % 2
    return mine, (data + (1 - 2 * mine) * step, head)


class Flow:
    def __init__(self, order, first, last, pieces, block=None):
        self.order, self.first, self.last = order, first, last
        self.bits = order[first:last]
        self.local = block is not None
        self.arrays = []
        self.pieces = []
        total = 0
        for array, lead, start, count in pieces:
            known = [index for index, other in enumerate(self.arrays) if other is array]
            if not known:
                self.arrays.append(array)
            index = known[0] if known else len(self.arrays) - 1
            self.pieces.append((index, lead, start, total, count))
            total += count
        self.block = block or (total,) + pieces[0][0].shape[-2:]

    def shape(self, stage):
        return (2,) * (len(self.order) - stage) + self.block

    def out(self):
        done = self.last == len(self.order)
        return shaped(self.shape(self.last), F32 if done else BF16)

    def scratch(self):
        stages = range(self.first, self.last)
        count = len(self.pieces)
        dma = pltpu.SemaphoreType.DMA
        return (
            ([] if self.local else [pltpu.VMEM(self.shape(self.first + 1), BF16)])
            + [pltpu.VMEM(self.shape(stage + 1), BF16) for stage in stages]
            + [pltpu.VMEM(self.shape(stage + 1), BF16) for stage in stages[:-1]]
            + [dma((len(stages),)), dma((len(stages),))]
            + [dma((count,)) for _ in range(0 if self.local else 3)]
        )

    def bind(self, inputs, out, scratch):
        stages = range(self.first, self.last)
        self.in_refs, self.out_ref = inputs, out
        count = len(stages)
        skip = 0 if self.local else 1
        self.own = scratch[0]
        self.got = dict(zip(stages, scratch[skip : skip + count]))
        self.sum = dict(zip(stages[:-1], scratch[skip + count :]))
        if self.local:
            self.send, self.recv = scratch[-2:]
        else:
            self.send, self.recv, self.local_sem, self.piece_send, self.piece_recv = scratch[-5:]

    def where(self, stage, index):
        left = sorted(self.order[stage:])
        place = len(left) - 1 - left.index(self.order[stage])
        return (slice(None),) * place + (index,)

    def piece_copies(self):
        stage = self.first
        mine, device = partner(self.order[stage])
        left = len(self.order) - stage
        for number, (index, lead, start, total, count) in enumerate(self.pieces):
            prefix = () if lead is None else (lead,)
            target = (slice(None),) * (left - 1) + (slice(total, total + count),)
            ref = self.in_refs[index]

            def part(value):
                at = self.where(stage, value)
                at += (slice(None),) * (left - len(at)) + (slice(start, start + count),)
                return ref.at[prefix + at]

            yield pltpu.make_async_remote_copy(
                src_ref=part(1 - mine),
                dst_ref=self.got[stage].at[target],
                send_sem=self.piece_send.at[number],
                recv_sem=self.piece_recv.at[number],
                device_id=device,
                device_id_type=MESH,
            )
            yield pltpu.make_async_copy(
                part(mine),
                self.own.at[target],
                self.local_sem.at[number],
            )

    def stage_copy(self, stage):
        mine, device = partner(self.order[stage])
        source = self.source if stage == self.first else self.sum[stage - 1]
        return pltpu.make_async_remote_copy(
            src_ref=source.at[self.where(stage, 1 - mine)],
            dst_ref=self.got[stage],
            send_sem=self.send.at[stage - self.first],
            recv_sem=self.recv.at[stage - self.first],
            device_id=device,
            device_id_type=MESH,
        )

    def start(self):
        if self.local:
            self.stage_copy(self.first).start()
        else:
            for copy in self.piece_copies():
                copy.start()

    def step(self, stage):
        mine, _ = partner(self.order[stage])
        if stage > self.first:
            self.stage_copy(stage).wait()
            kept = self.sum[stage - 1].at[self.where(stage, mine)]
        elif self.local:
            self.stage_copy(stage).wait()
            kept = self.source.at[self.where(stage, mine)]
        else:
            for copy in self.piece_copies():
                copy.wait()
            kept = self.own
        got = self.got[stage]
        last = stage == self.last - 1
        target = self.out_ref if last else self.sum[stage]
        kind = F32 if stage == len(self.order) - 1 else BF16
        dims = min(2, len(self.order) - stage - 1)

        def add(index, carry):
            at = tuple((index >> bit) & 1 for bit in range(dims))
            target[at] = kept[at].astype(kind) + got[at].astype(kind)
            return carry

        if dims:
            lax.fori_loop(0, 1 << dims, add, 0)
        else:
            target[...] = kept[...].astype(kind) + got[...].astype(kind)
        if not last:
            self.stage_copy(stage + 1).start()


class Swap:
    def __init__(self, bit, shape, array=None, kept=True):
        self.bits = (bit,)
        self.wide = shape
        self.kept = kept
        self.arrays = [] if array is None else [array]

    def out(self):
        return shaped(self.wide, BF16) if self.kept else None

    def scratch(self):
        return [pltpu.VMEM(self.wide, BF16), pltpu.SemaphoreType.DMA, pltpu.SemaphoreType.DMA]

    def bind(self, inputs, out, scratch):
        self.source = inputs[0] if inputs else None
        self.out_ref = out
        self.got, self.send, self.recv = scratch

    def copy(self):
        return pltpu.make_async_remote_copy(
            src_ref=self.source,
            dst_ref=self.got,
            send_sem=self.send,
            recv_sem=self.recv,
            device_id=partner(self.bits[0])[1],
            device_id_type=MESH,
        )

    def start(self):
        self.copy().start()

    def step(self, stage):
        self.copy().wait()
        if self.kept:
            self.out_ref[...] = self.got[...]


class Total:
    def __init__(self, bits, arrays):
        self.bits = tuple(range(bits))
        self.arrays = []
        self.terms = arrays

    def out(self):
        return shaped(self.terms[0].shape, F32)

    def scratch(self):
        count = len(self.bits)
        whole_shape = (count,) + self.terms[0].shape
        dma = pltpu.SemaphoreType.DMA((count,))
        return [pltpu.VMEM(whole_shape, F32), pltpu.VMEM(whole_shape, F32), dma, dma]

    def bind(self, inputs, out, scratch):
        self.out_ref = out
        self.held, self.got, self.send, self.recv = scratch

    def copy(self, stage):
        return pltpu.make_async_remote_copy(
            src_ref=self.held.at[stage],
            dst_ref=self.got.at[stage],
            send_sem=self.send.at[stage],
            recv_sem=self.recv.at[stage],
            device_id=partner(stage)[1],
            device_id_type=MESH,
        )

    def start(self):
        self.held[0] = functools.reduce(lambda left, right: left + right, [ref[...] for ref in self.refs])
        self.copy(0).start()

    def step(self, stage):
        self.copy(stage).wait()
        total = self.held[stage] + self.got[stage]
        if stage == len(self.bits) - 1:
            self.out_ref[...] = total
        else:
            self.held[stage + 1] = total
            self.copy(stage + 1).start()


def greet(bits):
    ready = pltpu.get_barrier_semaphore()
    for bit in bits:
        _, device = partner(bit)
        pl.semaphore_signal(ready, inc=1, device_id=device, device_id_type=MESH)
    pl.semaphore_wait(ready, len(bits))


def call(kernel, steps, ins, outs, scratch, name, estimate, flows=(), plan=None, collective=None):
    extra_in = [array for flow in flows for array in flow.arrays]
    bits = sorted({bit for flow in flows for bit in flow.bits})
    counts = (len(ins), len(outs), len(scratch))

    def body(*refs):
        refs = list(refs)
        take = lambda count: [refs.pop(0) for _ in range(count)]
        main = take(counts[0])
        inputs = [take(len(flow.arrays)) for flow in flows]
        main += take(counts[1])
        results = [take(1)[0] if flow.out() else None for flow in flows]
        main += take(counts[2])
        for flow, given, result in zip(flows, inputs, results):
            flow.bind(given, result, take(len(flow.scratch())))

        def tick(slot, now=None):
            for (step, place), actions in (plan or {}).items():
                if place == slot:

                    here = pl.program_id(0) == step

                    @pl.when(here if now is None else here & now)
                    def _():
                        if (step, slot) == (0, 0):
                            greet(bits)
                        for number, stage in actions:
                            if stage is None:
                                flows[number].start()
                            else:
                                flows[number].step(stage)

        kernel(tick, *main)

    still = lambda shape: pl.BlockSpec(shape, lambda step: (0,) * len(shape))
    given_out = [flow.out() for flow in flows if flow.out()]
    remote = dict(collective_id=collective, has_side_effects=True) if flows else {}
    result = pl.pallas_call(
        body,
        grid=(steps,),
        out_shape=[shape for shape, _ in outs] + given_out,
        in_specs=[spec for _, spec in ins] + [pl.BlockSpec(memory_space=pl.ANY)] * len(extra_in),
        out_specs=[spec for _, spec in outs] + [still(shape.shape) for shape in given_out],
        scratch_shapes=list(scratch) + [shape for flow in flows for shape in flow.scratch()],
        compiler_params=pltpu.CompilerParams(vmem_limit_bytes=63 << 20, **remote),
        cost_estimate=estimate,
        name=name,
    )(*[array for array, _ in ins], *extra_in)
    return result[: len(outs)], result[len(outs) :]


def scores_bias(own_length, other_length, width, ahead):
    row = lax.broadcasted_iota(jnp.int32, (width, width), 0)
    column = lax.broadcasted_iota(jnp.int32, (width, width), 1)
    own = jnp.where((column < own_length) & (column <= row + ahead), 0.0, MASKED).astype(F32)
    if other_length is None:
        return own
    other = jnp.where(column < other_length, 0.0, MASKED).astype(F32)
    return jnp.concatenate([own, other], axis=1)


def attend_rows(bias, q_ref, k_ref, v_ref, e_ref, o_ref, inv_ref, rows, keys):
    count = bias.shape[1]
    ones = jnp.ones((count, 128), BF16)
    for pair in range(COLS // 128):
        cols = slice(pair * 128, pair * 128 + 128)
        queries = q_ref[rows, cols]
        key_pair = k_ref[keys, cols]
        value_ext = jnp.concatenate([v_ref[keys, cols], ones], axis=1)
        outs, inverses = [], []
        for which in range(2):
            scores = dot(one_head(which, queries), key_pair, NT) + bias
            highest = jnp.max(scores, axis=1, keepdims=True)
            powers = jnp.exp(scores - highest).astype(BF16)
            e_ref[pair * 2 + which, rows, :] = powers
            mixed = dot(powers, value_ext)
            inverse = 1.0 / mixed[:, 128:]
            outs.append(mixed[:, :128] * inverse)
            inverses.append(inverse)
        o_ref[rows, cols] = join_heads(*outs).astype(BF16)
        inv_ref[rows, cols] = join_heads(*inverses)


def attend_kernel(causal, cross, mates, tick, *refs):
    number = len(causal)
    ins = refs[: 2 if cross else number]
    (
        short_ref,
        long_ref,
        wq_ref,
        wk_ref,
        wv_ref,
        o_ref,
        inv_ref,
        q_ref,
        ks_ref,
        vs_ref,
        kl_ref,
        vl_ref,
        es_ref,
        el_ref,
        *scratch,
    ) = refs[len(ins) :]
    rows = ins[0].shape[1]
    scale = 0.125
    step = pl.program_id(0)
    which = step // 2
    place = lax.axis_index("head")
    half = place % 2
    for mate, ref in zip(mates, ins[-len(mates) :]):
        mate.source = ref.at[1]
    tick(0)
    if number == 1:
        xq_ref, xk_ref = ins[0], ins[-1]
    else:
        xq_ref = xk_ref = scratch[0]
        for index in range(number):

            @pl.when(step == 2 * index)
            def _():
                xq_ref[...] = ins[index][...]

    kind = sum([jnp.where(which == index, 1, 0) for index in range(number) if causal[index]], 0)
    ahead = (1 - kind) * LONG
    q_ref[0, 0] = (dot(xq_ref[0], wq_ref[0]) * scale).astype(BF16)
    ks_ref[0] = dot(xk_ref[0], wk_ref[0]).astype(BF16)
    vs_ref[0] = dot(xk_ref[0], wv_ref[0]).astype(BF16)
    slots = rows // SHORT
    for slot in range(slots):
        bias = scores_bias(short_ref[kind, place * slots + slot], None, SHORT, ahead)
        here = slice(slot * SHORT, (slot + 1) * SHORT)
        attend_rows(
            bias,
            q_ref.at[0, 0],
            ks_ref.at[0],
            vs_ref.at[0],
            es_ref.at[0],
            o_ref.at[0, 0],
            inv_ref.at[0, 0],
            here,
            here,
        )
    q_ref[0, 1] = (dot(xq_ref[1], wq_ref[0]) * scale).astype(BF16)
    kl_ref[0, :rows] = dot(xk_ref[1], wk_ref[0]).astype(BF16)
    vl_ref[0, :rows] = dot(xk_ref[1], wv_ref[0]).astype(BF16)
    tick(1)
    if number == 1:
        mate_ref = mates[0].got
    else:
        mate_ref = scratch[1]
        for index in range(number):

            @pl.when(step == 2 * index)
            def _():
                mate_ref[...] = mates[index].got[...]

    kl_ref[0, rows:] = dot(mate_ref[...], wk_ref[0]).astype(BF16)
    vl_ref[0, rows:] = dot(mate_ref[...], wv_ref[0]).astype(BF16)
    everything = slice(None)
    length = long_ref[kind, place // 2]
    other = (length - (1 - half) * rows) * (1 - kind * (1 - half))
    bias = scores_bias(length - half * rows, other, rows, ahead)
    attend_rows(
        bias,
        q_ref.at[0, 1],
        kl_ref.at[0],
        vl_ref.at[0],
        el_ref.at[0],
        o_ref.at[0, 1],
        inv_ref.at[0, 1],
        everything,
        everything,
    )


def attend(xs, causal, cross, weights, base, lengths, collective):
    _, rows, width = xs[0].shape
    number = len(causal)
    heads = width // 64
    place = lambda step: step // 2
    weight = lambda index: (
        weights,
        pl.BlockSpec((1, width, COLS), lambda step: (base + 4 * place(step) + index, 0, step % 2)),
    )
    both = lambda kind: (
        shaped((number, 2, rows, width), kind),
        pl.BlockSpec((1, 2, rows, COLS), lambda step: (place(step), 0, 0, step % 2)),
    )
    cols = lambda count: (
        shaped((number, count, width), BF16),
        pl.BlockSpec((1, count, COLS), lambda step: (place(step), 0, step % 2)),
    )
    powers = lambda count: (
        shaped((number, heads, rows, count), BF16),
        pl.BlockSpec((1, COLS // 64, rows, count), lambda step: (place(step), step % 2, 0, 0)),
    )
    flops = 2 * rows * width * width * 7 + 4 * rows * width * (SHORT + LONG)
    mates = [Swap(0, (rows, width)) for _ in range(number)]
    plan = {(0, 0): [(index, None) for index in range(number)]}
    for index in range(number):
        plan[2 * index, 1] = [(index, 0)]
    return call(
        functools.partial(attend_kernel, causal, cross, mates),
        2 * number,
        [(array, whole(array)) for array in xs]
        + [(array, pl.BlockSpec(memory_space=pltpu.SMEM)) for array in lengths]
        + [weight(0), weight(1), weight(2)],
        [both(BF16), both(F32), both(BF16), cols(rows), cols(rows), cols(LONG), cols(LONG)]
        + [powers(SHORT), powers(LONG)],
        [] if number == 1 else [pltpu.VMEM((2, rows, width), BF16), pltpu.VMEM((rows, width), BF16)],
        "attend",
        cost(flops * 2 * number, number * (22 << 20), number * heads * rows * (SHORT + LONG)),
        mates,
        plan,
        collective,
    )


def attend_back_rows(
    do_ref,
    o_ref,
    inv_ref,
    q_ref,
    k_ref,
    v_ref,
    e_ref,
    dq_ref,
    dk_ref,
    dv_ref,
    rows,
    keys,
    pair,
    scale,
):
    cols = pl.ds(pl.multiple_of(pair * 128, 128), 128)
    grad = do_ref[rows, cols].astype(F32) * inv_ref[rows, cols]
    product = grad * o_ref[rows, cols].astype(F32)
    grad_low = grad.astype(BF16)
    queries = q_ref[rows, cols]
    key_pair = k_ref[keys, cols]
    value_pair = v_ref[keys, cols]
    grad_turned = grad.T.astype(BF16)
    queries_turned = queries.astype(F32).T.astype(BF16)
    grad_q, grad_k, grad_v = [], [], []
    for which in range(2):
        inner = jnp.sum(one_head(which, product), axis=1, keepdims=True)
        grad_probs = dot(one_head(which, grad_low), value_pair, NT)
        powers = e_ref[pair * 2 + which, rows, :]
        grad_scores = (powers.astype(F32) * (grad_probs - inner)).astype(BF16)
        grad_q.append(dot(grad_scores, key_pair))
        head = slice(which * 64, which * 64 + 64)
        grad_v.append(dot(grad_turned[head], powers))
        grad_k.append(dot(queries_turned[head], grad_scores))
    dq_ref[rows, cols] = (join_heads(*grad_q) * scale).astype(BF16)
    dk_ref[keys, cols] = jnp.concatenate(grad_k, axis=0).T.astype(BF16)
    dv_ref[keys, cols] = jnp.concatenate(grad_v, axis=0).T.astype(BF16)


def attend_back_kernel(number, cross, own, swaps, total, after, tick, *refs):
    refs = list(refs)
    take = lambda count: [refs.pop(0) for _ in range(count)]
    if total:
        total.refs = take(len(total.terms))
    do_ref, o_ref, inv_ref, q_ref, ks_ref, vs_ref, kl_ref, vl_ref, es_ref, el_ref, resid_ref, *ins = take(
        11 + (2 if cross else number)
    )
    wq_ref, wk_ref, wv_ref = take(3)
    mates = take(number)
    dx_ref = take(1)[0]
    if cross:
        dy_ref, dmate_ref, dwq_ref, dwk_ref, dwv_ref = take(5)
    dqs, dks, dvs, dql, dkl, dvl, mate_sum, mate_low, resid_sem, *scratch = refs
    step = pl.program_id(0)
    first = step % 2 == 0
    if cross:
        xq_ref, xk_ref, mate_ref = ins[0], ins[1], mates[0]
        dy_ref = dy_ref.at[0]
    else:
        xq_ref = xk_ref = scratch[0]
        mate_ref = scratch[1]
        terms_ref = scratch[2]
        for place, flow in enumerate(own):
            kind, start = OWN_PARTS[place // 2]
            every = (slice(None),) * len(flow.order)
            flow.source = terms_ref.at[(kind, place % 2) + every + (slice(start, start + flow.block[0]),)]
        for index in range(number):
            swaps[index].source = mate_low.at[index]

            @pl.when(step == 2 * (number - 1 - index))
            def _():
                xq_ref[...] = ins[index][...]
                mate_ref[...] = mates[index][...]

        dy_ref = dx_ref.at[0]
    dx_ref = dx_ref.at[0]
    rows = xq_ref.shape[1]
    load = pltpu.make_async_copy(resid_ref.at[number - 1 - step // 2], dx_ref, resid_sem)

    @pl.when(first)
    def _():
        load.start()

    scale = 0.125
    everything = slice(None)
    tick(0)
    pairs = COLS // 128

    def long_pair(pair, carry):
        attend_back_rows(
            do_ref.at[0, 1],
            o_ref.at[0, 1],
            inv_ref.at[0, 1],
            q_ref.at[0, 1],
            kl_ref.at[0],
            vl_ref.at[0],
            el_ref.at[0],
            dql,
            dkl,
            dvl,
            everything,
            everything,
            pair,
            scale,
        )
        for index in range(pairs):
            tick(1 + index, pair == index)
        return carry

    def short_slot(slot, carry):
        here = pl.ds(pl.multiple_of(slot * SHORT, SHORT), SHORT)
        for pair in range(pairs):
            attend_back_rows(
                do_ref.at[0, 0],
                o_ref.at[0, 0],
                inv_ref.at[0, 0],
                q_ref.at[0, 0],
                ks_ref.at[0],
                vs_ref.at[0],
                es_ref.at[0],
                dqs,
                dks,
                dvs,
                here,
                here,
                pair,
                scale,
            )
        return carry

    lax.fori_loop(0, pairs, long_pair, 0)
    lax.fori_loop(0, rows // SHORT, short_slot, 0)
    tick(3)
    wq, wk, wv = wq_ref[0], wk_ref[0], wv_ref[0]
    front = slice(0, rows)
    other = slice(rows, 2 * rows)
    dwq = dot(xq_ref[0], dqs[...], TN) + dot(xq_ref[1], dql[...], TN)
    short, long, mate = xk_ref[0], xk_ref[1], mate_ref[...]
    dwk = dot(short, dks[...], TN) + dot(long, dkl[front], TN) + dot(mate, dkl[other], TN)
    dwv = dot(short, dvs[...], TN) + dot(long, dvl[front], TN) + dot(mate, dvl[other], TN)
    if cross:
        dwq_ref[...] = dwq.astype(BF16)
        dwk_ref[...] = dwk.astype(BF16)
        dwv_ref[...] = dwv.astype(BF16)
    else:
        flow = own[0]
        _, share, columns = flow.block
        for index, total_w in enumerate((dwq, dwk, dwv)):
            low = total_w.astype(BF16)
            for device in range(low.shape[0] // share):
                at = tuple((device >> bit) & 1 for bit in reversed(range(len(flow.order))))
                for color in range(2):
                    terms_ref[(1 - step // 2, color) + at + (step % 2 * 3 + index,)] = low[
                        device * share : (device + 1) * share, color * columns : (color + 1) * columns
                    ]

    tick(4)

    @pl.when(first)
    def _():
        load.wait()
        if cross:
            dy_ref[...] = jnp.zeros_like(dy_ref)
        mate_sum[...] = jnp.zeros_like(mate_sum)

    mate_sum[...] += dot(dkl[other], wk, NT) + dot(dvl[other], wv, NT)
    if cross:

        @pl.when(jnp.logical_not(first))
        def _():
            dmate_ref[...] = mate_sum[...].astype(BF16)

    else:
        for index in range(number):

            @pl.when(step == 2 * (number - 1 - index) + 1)
            def _():
                mate_low[index] = mate_sum[...].astype(BF16)

    tick(5)
    dx_ref[0] += dot(dqs[...], wq, NT)
    dx_ref[1] += dot(dql[...], wq, NT)
    dy_ref[0] += dot(dks[...], wk, NT) + dot(dvs[...], wv, NT)
    dy_ref[1] += dot(dkl[front], wk, NT) + dot(dvl[front], wv, NT)
    for slot in range(6, 6 + after):
        tick(slot)


def attend_back(grad, saved, mates, resid, xs, cross, weights, base, flows, plan, collective, last=None):
    _, rows, width = xs[0].shape
    number = 1 if cross else len(xs)
    place = lambda step: number - 1 - step // 2
    weight = lambda index: (
        weights,
        pl.BlockSpec((1, width, COLS), lambda step: (base + 4 * place(step) + index, 0, step % 2)),
    )
    both = pl.BlockSpec((1, 2, rows, COLS), lambda step: (place(step), 0, 0, step % 2))
    cols = lambda count: pl.BlockSpec((1, count, COLS), lambda step: (place(step), 0, step % 2))
    powers = lambda count: pl.BlockSpec((1, COLS // 64, rows, count), lambda step: (place(step), step % 2, 0, 0))
    deep = pl.BlockSpec((1, 2, rows, width), lambda step: (place(step), 0, 0, 0))
    flops = 2 * rows * width * width * 14 + 8 * rows * width * (SHORT + LONG)
    specs = [both] * 4 + [cols(rows)] * 2 + [cols(LONG)] * 2 + [powers(SHORT), powers(LONG)]
    o, inverse, *rest = saved
    own, swaps, total = last or ((), (), None)
    data = (shaped((number, 2, rows, width), F32), deep)
    outs = [data]
    scratch = (
        [pltpu.VMEM((rows, COLS), BF16)] * 4
        + [pltpu.VMEM((LONG, COLS), BF16)] * 2
        + [pltpu.VMEM((rows, width), F32), pltpu.VMEM((number, rows, width), BF16)]
        + [pltpu.SemaphoreType.DMA]
    )
    if cross:
        outs += [data, (shaped((rows, width), BF16), pl.BlockSpec((rows, width), lambda step: (0, 0)))]
        outs += [(shaped((width, width), BF16), pl.BlockSpec((width, COLS), lambda step: (0, step)))] * 3
    else:
        scratch += [pltpu.VMEM((2, rows, width), BF16), pltpu.VMEM((rows, width), BF16)]
        _, share, columns = own[0].block
        scratch += [pltpu.VMEM((number, 2) + own[0].shape(0)[:-3] + (6, share, columns), BF16)]
    after = 1 + max([spot for _, spot in plan] + [5]) - 6
    norms = total.terms if total else []
    return call(
        functools.partial(attend_back_kernel, number, cross, own, swaps, total, after),
        2 * number,
        [(array, whole(array)) for array in norms]
        + list(zip((grad, o, inverse, *rest), specs))
        + [(resid, pl.BlockSpec(memory_space=pl.ANY))]
        + [(array, whole(array)) for array in xs]
        + [weight(0), weight(1), weight(2)]
        + [(array, whole(array)) for array in mates],
        outs,
        scratch,
        "attend_back",
        cost(flops * 2 * number, number * (28 << 20)),
        flows,
        plan,
        collective,
    )


BLOCK = 512
WIDE = 1024
ANY = pl.BlockSpec(memory_space=pl.ANY)


def norm_parts(resid):
    average = jnp.mean(resid, axis=-1, keepdims=True)
    centered = resid - average
    variance = jnp.mean(centered * centered, axis=-1, keepdims=True)
    spread = lax.rsqrt(variance + EPSILON)
    return centered * spread, spread


def norm_back(normal, spread, gain, grad):
    scaled = grad * gain
    first = jnp.mean(scaled, axis=-1, keepdims=True)
    second = jnp.mean(scaled * normal, axis=-1, keepdims=True)
    return (scaled - first - normal * second) * spread


def add_norm_grads(ref, place, grad, normal):
    ref[place : place + 1, :] += jnp.sum(grad * normal, axis=0, keepdims=True)
    ref[8 + place : 9 + place, :] += jnp.sum(grad, axis=0, keepdims=True)


def logistic(value):
    return 1.0 / (1.0 + jnp.exp(-value))


def each_block(count, work, size=BLOCK):
    def step(index, carry):
        work(pl.ds(pl.multiple_of(index * size, size), size))
        return carry

    lax.fori_loop(0, count // size, step, 0)


def each_chunk(count, work):
    def step(index, carry):
        work(index)
        return carry

    lax.fori_loop(0, count, step, 0)


class Loads:
    def __init__(self, pairs, sems):
        self.copies = [
            pltpu.make_async_copy(source, target, sems.at[index])
            for index, (source, target) in enumerate(pairs)
        ]

    def start(self):
        for copy in self.copies:
            copy.start()

    def wait(self, *places):
        for place in places:
            self.copies[place].wait()


def chunk_loads(up_ref, down_ref, up_s, down_s, sems):
    def copies(chunk):
        part = pl.ds(pl.multiple_of(chunk * CHUNK, CHUNK), CHUNK)
        return (
            pltpu.make_async_copy(up_ref.at[:, part], up_s.at[chunk], sems.at[0, chunk]),
            pltpu.make_async_copy(down_ref.at[part], down_s.at[chunk], sems.at[1, chunk]),
        )

    return copies


def feed_chunks(copies, low_s, total_s, up_s, down_s, u_s, a_s, out=None):
    count = low_s.shape[0]

    def chunk_work(chunk):
        for copy in copies(chunk):
            copy.wait()

        def block_work(rows):
            upward = dot(low_s[rows, :], up_s[chunk])
            u_s[chunk, rows, :] = upward
            active = (upward * logistic(upward)).astype(BF16)
            if a_s is not None:
                a_s[chunk, rows, :] = active
            total_s[rows, :] += dot(active, down_s[chunk])

        each_block(count, block_work, WIDE)
        if out is not None:
            out(chunk)

    each_chunk(up_s.shape[0], chunk_work)


def feed_back_chunks(tick, wait, low_s, hidden_s, total_s, up_s, down_s, u_s, a_s, du_s, write):
    count = low_s.shape[0]
    chunks = up_s.shape[0]

    def chunk_work(chunk):
        wait(chunk)
        store = a_s is None
        active_ref = du_s.at[1] if store else a_s.at[chunk]

        def block_work(rows):
            upward = u_s[chunk, rows, :]
            gate = logistic(upward)
            if store:
                active_ref[rows, :] = (upward * gate).astype(BF16)
            grad_active = dot(low_s[rows, :], down_s[chunk], NT)
            grad_up = (grad_active * gate * (1.0 + upward * (1.0 - gate))).astype(BF16)
            du_s[0, rows, :] = grad_up
            total_s[rows, :] += dot(grad_up, up_s[chunk], NT)

        each_block(count, block_work, WIDE)
        write(chunk, dot(hidden_s[...], du_s[0], TN), dot(active_ref[...], low_s[...], TN))
        for index in range(chunks):
            tick(2 + index, chunk == index)

    each_chunk(chunks, chunk_work)


def feed_kernel(
    tick,
    os_ref,
    x_ref,
    z_ref,
    wm_ref,
    wo_ref,
    up_ref,
    down_ref,
    gain_ref,
    shift_ref,
    u_ref,
    r1_ref,
    r2_ref,
    enc_ref,
    r3_ref,
    h3_ref,
    *scratch,
):
    up_s, down_s, u_s, low_s, sems, out_sems = scratch
    copies = chunk_loads(up_ref.at[0], down_ref.at[0], up_s, down_s, sems)
    chunks = up_s.shape[0]
    for chunk in range(chunks):
        for copy in copies(chunk):
            copy.start()
    count = low_s.shape[0]

    def first(rows):
        resid = x_ref[rows, :].astype(F32) + dot(os_ref[0, rows, :], wo_ref[0])
        r1_ref[rows, :] = resid
        normal, _ = norm_parts(resid)
        hidden = normal * gain_ref[0:1] + shift_ref[0:1]
        r2_ref[rows, :] = hidden
        low_s[rows, :] = hidden.astype(BF16)
        resid = z_ref[rows, :].astype(F32) + dot(os_ref[1, rows, :], wm_ref[0])
        r3_ref[rows, :] = resid
        normal, _ = norm_parts(resid)
        h3_ref[rows, :] = (normal * gain_ref[2:3] + shift_ref[2:3]).astype(BF16)

    each_block(count, first)
    keep = lambda chunk: pltpu.make_async_copy(u_s.at[chunk], u_ref.at[chunk], out_sems.at[chunk])
    feed_chunks(copies, low_s, r2_ref, up_s, down_s, u_s, None, lambda chunk: keep(chunk).start())

    def last(rows):
        normal, _ = norm_parts(r2_ref[rows, :])
        enc_ref[rows, :] = (normal * gain_ref[1:2] + shift_ref[1:2]).astype(BF16)

    each_block(count, last)
    for chunk in range(chunks):
        keep(chunk).wait()


def picked(array, index):
    return array, pl.BlockSpec((1,) + array.shape[1:], lambda step: (index, 0, 0))


def flat(array):
    return array.reshape((-1,) + array.shape[2:])


def full(array):
    return array, whole(array)


def new(kind, *shape):
    return shaped(shape, kind), pl.BlockSpec(shape, lambda step: (0,) * len(shape))


def weight_scratch(width, chunks):
    return [
        pltpu.VMEM((chunks, width, CHUNK), BF16),
        pltpu.VMEM((chunks, CHUNK, width), BF16),
    ]


def feed(o, x, z, attn, ups, downs, gains, shifts):
    shape = x.shape
    o, x, z = o.reshape((2, -1, shape[-1])), flat(x), flat(z)
    count, width = x.shape
    inner = ups.shape[2]
    chunks = inner // CHUNK
    results, _ = call(
        feed_kernel,
        1,
        [full(o), full(x), full(z), picked(attn, 7), picked(attn, 3)]
        + [(ups, ANY), (downs, ANY), full(gains), full(shifts)],
        [
            (shaped((chunks, count, CHUNK), F32), ANY),
            new(F32, count, width),
            new(F32, count, width),
            new(BF16, count, width),
            new(F32, count, width),
            new(BF16, count, width),
        ],
        weight_scratch(width, chunks)
        + [
            pltpu.VMEM((chunks, count, CHUNK), F32),
            pltpu.VMEM((count, width), BF16),
            pltpu.SemaphoreType.DMA((2, chunks)),
            pltpu.SemaphoreType.DMA((chunks,)),
        ],
        "feed",
        cost(2 * count * width * (2 * width + 2 * inner), 28 << 20, 2 * count * inner),
    )
    u, r1, r2, enc, r3, h3 = results
    return u, r1, r2, enc.reshape(shape), r3, h3.reshape(shape)


def turn_kernel(
    tick,
    o_ref,
    r3_ref,
    wo_ref,
    cot_ref,
    up_ref,
    down_ref,
    gain_ref,
    shift_ref,
    out_ref,
    dr_ref,
    do_ref,
    dup_ref,
    ddown_ref,
    dwo_ref,
    norm_ref,
    *scratch,
):
    up_s, down_s, u_s, a_s, low_s, hidden_s, du_s, cot_s, total_s, normal_s, spread_s, sems, cot_sem = scratch
    copies = chunk_loads(up_ref.at[1], down_ref.at[1], up_s, down_s, sems)
    chunks = up_s.shape[0]
    for chunk in range(chunks):
        for copy in copies(chunk):
            copy.start()
    load = pltpu.make_async_copy(cot_ref, cot_s, cot_sem)
    load.start()
    count = low_s.shape[0]
    norm_ref[...] = jnp.zeros_like(norm_ref)

    def first(rows):
        normal3, _ = norm_parts(r3_ref[rows, :])
        resid4 = normal3 * gain_ref[2:3] + shift_ref[2:3] + dot(o_ref[rows, :], wo_ref[0])
        normal4, spread4 = norm_parts(resid4)
        hidden = normal4 * gain_ref[3:4] + shift_ref[3:4]
        normal_s[rows, :] = normal4
        spread_s[rows, :] = spread4
        total_s[rows, :] = hidden
        hidden_s[rows, :] = hidden.astype(BF16)

    each_block(count, first)
    feed_chunks(copies, hidden_s, total_s, up_s, down_s, u_s, a_s)
    load.wait()

    def top(rows):
        normal5, spread5 = norm_parts(total_s[rows, :])
        out_ref[rows, :] = (normal5 * gain_ref[4:5] + shift_ref[4:5]).astype(BF16)
        grad = cot_s[rows, :].astype(F32)
        add_norm_grads(norm_ref, 4, grad, normal5)
        grad = norm_back(normal5, spread5, gain_ref[4:5], grad)
        total_s[rows, :] = grad
        low_s[rows, :] = grad.astype(BF16)

    each_block(count, top)

    def write(chunk, dup, ddown):
        dup_ref[chunk] = dup.astype(BF16)
        ddown_ref[chunk] = ddown.astype(BF16)

    feed_back_chunks(
        tick, lambda chunk: None, low_s, hidden_s, total_s, up_s, down_s, u_s, a_s, du_s, write
    )

    def bottom(rows):
        grad = total_s[rows, :]
        normal4 = normal_s[rows, :]
        add_norm_grads(norm_ref, 3, grad, normal4)
        grad = norm_back(normal4, spread_s[rows, :], gain_ref[3:4], grad)
        dr_ref[rows, :] = grad
        low = grad.astype(BF16)
        low_s[rows, :] = low
        do_ref[rows, :] = dot(low, wo_ref[0], NT).astype(BF16)

    each_block(count, bottom)
    dwo_ref[...] = dot(o_ref[...], low_s[...], TN).astype(BF16)


def turn(o, r3, cot, attn, ups, downs, gains, shifts):
    rows = cot.shape[1]
    o, cot = flat(flat(o)), flat(cot)
    count, width = r3.shape
    inner = ups.shape[2]
    chunks = inner // CHUNK
    wide = pltpu.VMEM((count, width), BF16)
    results, _ = call(
        turn_kernel,
        1,
        [full(o), full(r3), picked(attn, 11), (cot, ANY), (ups, ANY), (downs, ANY), full(gains), full(shifts)],
        [
            new(BF16, count, width),
            new(F32, count, width),
            new(BF16, count, width),
            new(BF16, chunks, width, CHUNK),
            new(BF16, chunks, CHUNK, width),
            new(BF16, width, width),
            new(F32, 16, width),
        ],
        weight_scratch(width, chunks)
        + [
            pltpu.VMEM((chunks, count, CHUNK), F32),
            pltpu.VMEM((chunks, count, CHUNK), BF16),
            wide,
            wide,
            pltpu.VMEM((1, count, CHUNK), BF16),
            wide,
            pltpu.VMEM((count, width), F32),
            pltpu.VMEM((count, width), F32),
            pltpu.VMEM((count, 1), F32),
            pltpu.SemaphoreType.DMA((2, chunks)),
            pltpu.SemaphoreType.DMA,
        ],
        "turn",
        cost(6 * count * width * (width + 2 * inner), 20 << 20, 4 * count * inner),
    )
    out, dr, do, dup, ddown, dwo, norms = results
    pair = lambda array: array.reshape((2, rows) + array.shape[1:])
    return pair(out), pair(dr)[None], pair(do)[None], dup, ddown.reshape(inner, width), dwo, norms


def feed_back_kernel(
    mate,
    tick,
    gradm_ref,
    r3_ref,
    wm_ref,
    wo_ref,
    grad_ref,
    r2_ref,
    r1_ref,
    os_ref,
    u_ref,
    up_ref,
    down_ref,
    gain_ref,
    shift_ref,
    dr_ref,
    do_ref,
    dup_ref,
    ddown_ref,
    dwo_ref,
    dwm_ref,
    norm_ref,
    *scratch,
):
    (
        up_s,
        down_s,
        u_s,
        low_s,
        hidden_s,
        du_s,
        total_s,
        normal_s,
        spread_s,
        grad_s,
        r2_s,
        r1_s,
        os_s,
        sems,
        u_sems,
        in_sems,
    ) = scratch
    copies = chunk_loads(up_ref.at[0], down_ref.at[0], up_s, down_s, sems)
    chunks = up_s.shape[0]
    keep = lambda chunk: pltpu.make_async_copy(u_ref.at[chunk], u_s.at[chunk], u_sems.at[chunk])
    late = Loads([(os_ref, os_s), (grad_ref, grad_s), (r2_ref, r2_s), (r1_ref, r1_s)], in_sems)
    late.start()
    for chunk in range(chunks):
        keep(chunk).start()
        for copy in copies(chunk):
            copy.start()
    tick(0)
    count = low_s.shape[0]
    half = count // 2
    norm_ref[...] = jnp.zeros_like(norm_ref)

    def middle(rows):
        grad = gradm_ref[rows, :]
        normal, spread = norm_parts(r3_ref[rows, :])
        add_norm_grads(norm_ref, 2, grad, normal)
        grad = norm_back(normal, spread, gain_ref[2:3], grad)
        dr_ref[1, rows, :] = grad
        low = grad.astype(BF16)
        low_s[rows, :] = low
        do_ref[1, rows, :] = dot(low, wm_ref[0], NT).astype(BF16)

    each_block(count, middle)
    late.wait(0)
    dwm_ref[...] = dot(os_s[1], low_s[...], TN).astype(BF16)
    tick(1)

    def first(rows, grad):
        normal2, spread2 = norm_parts(r2_s[rows, :])
        add_norm_grads(norm_ref, 1, grad, normal2)
        grad = norm_back(normal2, spread2, gain_ref[1:2], grad)
        total_s[rows, :] = grad
        low_s[rows, :] = grad.astype(BF16)
        normal1, spread1 = norm_parts(r1_s[rows, :])
        normal_s[rows, :] = normal1
        spread_s[rows, :] = spread1
        hidden_s[rows, :] = (normal1 * gain_ref[0:1] + shift_ref[0:1]).astype(BF16)

    late.wait(1, 2, 3)
    each_block(half, lambda rows: first(rows, grad_s[rows, :]))

    def long(index, carry):
        start = pl.multiple_of(index * BLOCK, BLOCK)
        rows = pl.ds(pl.multiple_of(start + half, BLOCK), BLOCK)
        first(rows, grad_s[rows, :] + mate.got[pl.ds(start, BLOCK), :].astype(F32))
        return carry

    lax.fori_loop(0, half // BLOCK, long, 0)

    def write(chunk, dup, ddown):
        dup_ref[chunk] = dup.astype(BF16)
        ddown_ref[chunk] = ddown.astype(BF16)

    def wait(chunk):
        keep(chunk).wait()
        for copy in copies(chunk):
            copy.wait()

    feed_back_chunks(tick, wait, low_s, hidden_s, total_s, up_s, down_s, u_s, None, du_s, write)

    def bottom(rows):
        grad = total_s[rows, :]
        normal1 = normal_s[rows, :]
        add_norm_grads(norm_ref, 0, grad, normal1)
        grad = norm_back(normal1, spread_s[rows, :], gain_ref[0:1], grad)
        dr_ref[0, rows, :] = grad
        low = grad.astype(BF16)
        low_s[rows, :] = low
        do_ref[0, rows, :] = dot(low, wo_ref[0], NT).astype(BF16)

    each_block(count, bottom)
    dwo_ref[...] = dot(os_s[0], low_s[...], TN).astype(BF16)
    tick(2 + chunks)


def feed_back(gradm, r3, grad, r2, r1, u, o, attn, ups, downs, gains, shifts, mate, flows, plan, collective):
    gradm, grad = flat(flat(gradm)), flat(flat(grad))
    o = o.reshape((2,) + grad.shape)
    count, width = r1.shape
    inner = ups.shape[2]
    chunks = inner // CHUNK
    wide = pltpu.VMEM((count, width), BF16)
    deep = pltpu.VMEM((count, width), F32)
    results, sums = call(
        functools.partial(feed_back_kernel, mate),
        1,
        [full(gradm), full(r3), picked(attn, 7), picked(attn, 3)]
        + [(array, ANY) for array in (grad, r2, r1, o, u, ups, downs)]
        + [full(gains), full(shifts)],
        [
            new(F32, 2, count, width),
            new(BF16, 2, count, width),
            new(BF16, chunks, width, CHUNK),
            new(BF16, chunks, CHUNK, width),
            new(BF16, width, width),
            new(BF16, width, width),
            new(F32, 16, width),
        ],
        weight_scratch(width, chunks)
        + [
            pltpu.VMEM((chunks, count, CHUNK), F32),
            wide,
            wide,
            pltpu.VMEM((2, count, CHUNK), BF16),
            deep,
            deep,
            pltpu.VMEM((count, 1), F32),
            deep,
            deep,
            deep,
            pltpu.VMEM((2, count, width), BF16),
            pltpu.SemaphoreType.DMA((2, chunks)),
            pltpu.SemaphoreType.DMA((chunks,)),
            pltpu.SemaphoreType.DMA((4,)),
        ],
        "feed_back",
        cost(4 * count * width * (2 * width + 2 * inner), 36 << 20, 2 * count * inner),
        flows,
        plan,
        collective,
    )
    dr, do, dup, ddown, dwo, dwm, norms = results
    halves = lambda array: array.reshape((2, 2, count // 2, width))
    return (halves(dr), halves(do), dup, ddown.reshape(inner, width), dwo, dwm, norms), sums


def finish_kernel(counts, part_ref, src_mate_ref, tgt_mate_ref, norm_ref, *refs):
    sums, outs = refs[: -7], refs[-7:]
    gs_ref, gt_ref, attn_ref, up_ref, down_ref, gain_ref, shift_ref = outs
    long = pl.program_id(0) >= pl.num_programs(0) // 2
    for index, mate_ref, out_ref in ((0, src_mate_ref, gs_ref), (1, tgt_mate_ref, gt_ref)):

        @pl.when(long)
        def _():
            out_ref[...] = part_ref[index] + mate_ref[...].astype(F32)[None]

        @pl.when(jnp.logical_not(long))
        def _():
            out_ref[...] = part_ref[index]

    @pl.when(pl.program_id(0) == 0)
    def _():
        for ref, (kind, index, cols) in zip(sums, counts):
            share = ref.shape[-2]
            if kind == "attn":
                for number, place in enumerate(index):
                    attn_ref[place, :, cols[number]] = ref[number]
                continue
            tiles = up_ref.shape[2] // CHUNK
            index, place = index
            for number in range(ref.shape[0]):
                tile = tiles - 1 if kind == "both" else number
                if place is not None and number == tiles - 1:
                    attn_ref[place, :, :] = ref[number]
                elif kind == "up" or (kind == "both" and number == 0):
                    up_ref[index, :, tile * CHUNK : (tile + 1) * CHUNK] = ref[number]
                else:
                    down_ref[index, tile * share : (tile + 1) * share, :] = ref[number]
        share = gain_ref.shape[1]
        here = lax.axis_index("dp") * lax.axis_size("head") + lax.axis_index("head")
        width = norm_ref.shape[1]
        turned = pltpu.roll(norm_ref[...], (width - here * share) % width, axis=1)
        gain_ref[...] = turned[:5, :share]
        shift_ref[...] = turned[8:13, :share]


def finish(data, source_mate, target_mate, norms, named, share, inner, devices):
    _, _, rows, width = data.shape
    half = rows // 2
    row = pl.BlockSpec((1, half, width), lambda step: (step // 2, step % 2, 0))
    mate = pl.BlockSpec((half, width), lambda step: (step % 2, 0))
    sums = [array for array, *_ in named]
    counts = [tuple(rest) for _, *rest in named]
    outs = [
        (shaped((2, rows, width), F32), row),
        (shaped((2, rows, width), F32), row),
    ]
    for shape in ((12, share, width), (2, share, inner), (2, inner // devices, width), (5, share), (5, share)):
        outs.append((shaped(shape, F32), pl.BlockSpec(shape, lambda step, size=len(shape): (0,) * size)))
    return pl.pallas_call(
        functools.partial(finish_kernel, counts),
        grid=(4,),
        out_shape=[shape for shape, _ in outs],
        in_specs=[pl.BlockSpec((2, 1, half, width), lambda step: (0, step // 2, step % 2, 0)), mate, mate, whole(norms)] + [whole(array) for array in sums],
        out_specs=[spec for _, spec in outs],
        compiler_params=params(),
        cost_estimate=cost(0, 11 << 20),
        name="finish",
    )(data, source_mate, target_mate, norms, *sums)


CROSS_FFN = [(0, 2), (1, 2)]
FEED_FFN = [(0, 2), (0, 4), (0, 6)]
FEED_CROSS = [(0, 2), (0, 5), (0, 6)]
LAST_FFN = [(0, 3), (1, 5), (2, 5), (3, 3), (3, 9)]
LAST_CROSS = [(0, 4), (2, 0)]
LAST_NORMS = [(0, 2), (1, 2), (2, 0), (2, 4), (3, 1), (3, 7)]
LAST_OWN = [
    [(1, 4), (2, 2), (2, 5), (3, 3), (3, 6), (3, 8)],
    [(2, 4), (3, 2), (3, 4), (3, 7), (3, 8), (3, 9)],
    [(3, 4), (3, 6), (3, 7), (3, 8), (3, 9), (3, 10)],
]
OWN_PARTS = [(1, 0), (0, 0), (0, 3)]


def place_stages(plan, numbers, stages, start, spots):
    plan.setdefault(start, []).extend((number, None) for number in numbers)
    for index, stage in enumerate(stages):
        plan.setdefault(spots[min(index, len(spots) - 1)], []).extend((number, stage) for number in numbers)


def body(
    source,
    target,
    cotangent,
    short_lengths,
    long_lengths,
    attn,
    ups,
    downs,
    gains,
    shifts,
):
    _, rows, width = source.shape
    inner = ups.shape[2]
    devices = lax.axis_size("dp") * lax.axis_size("head")
    bits = devices.bit_length() - 1
    assert 2 * rows == LONG and rows % SHORT == 0 and devices == 1 << bits
    share = width // devices
    parts = (2,) * bits
    lengths = (short_lengths, long_lengths)
    orders = (
        tuple(range(bits)),
        (0, 2, 1) + tuple(range(3, bits)),
        (0,) + tuple(range(3, bits)) + (1, 2),
    )
    tiles = inner // width

    def square(array):
        return array.reshape(parts + (1, share, width)), None, 0, 1

    def ffn_flows(last, dup, ddown, extra=((), ())):
        up = dup.reshape((tiles,) + parts + (1, share, width))
        down = ddown.reshape(parts + (tiles, share, width))
        most = tiles - 1
        pieces = (
            [(up, index, 0, 1) for index in range(most)] + [square(array) for array in extra[0]],
            [(down, None, 0, most)] + [square(array) for array in extra[1]],
            [(up, most, 0, 1), (down, None, most, 1)],
        )
        return [Flow(order, 0, last, piece) for order, piece in zip(orders, pieces)]

    def attn_flows(last, *groups):
        pieces = [[square(array) for array in group] for group in groups]
        return [Flow(order, 0, last, piece) for order, piece in zip(orders, pieces)]

    def later(first, last, partial):
        return [
            Flow(order, first, last, [(part, None, 0, part.shape[-3])])
            for order, part in zip(orders, partial)
        ]

    self_saved, mates = attend((source, target), (False, True), False, attn, 0, lengths, 0)
    u, r1, r2, enc, r3, h3 = feed(self_saved[0], source, target, attn, ups, downs, gains, shifts)
    cross_saved, enc_mates = attend((h3, enc), (False,), True, attn, 8, lengths, 1)
    decoded, dr4, do_cross, dup1, ddown1, dw11, norms_a = turn(
        cross_saved[0], r3, cotangent, attn, ups, downs, gains, shifts
    )

    plan = {}
    place_stages(plan, (0, 1, 2), range(2), (0, 0), CROSS_FFN)
    (dh3, denc, denc_mate, dw8, dw9, dw10), ffn1 = attend_back(
        do_cross,
        cross_saved,
        enc_mates,
        dr4,
        (h3, enc),
        True,
        attn,
        8,
        ffn_flows(2, dup1, ddown1),
        plan,
        2,
    )

    plan = {}
    mate = Swap(0, (rows, width), denc_mate, kept=False)
    place_stages(plan, (5,), [0], (0, 0), [(0, 1)])
    place_stages(plan, (0, 1, 2), range(2, bits), (0, 0), FEED_FFN)
    place_stages(plan, (3, 4), range(3), (0, 0), FEED_CROSS)
    (dr, do, dup0, ddown0, dw3, dw7, norms_b), sums = feed_back(
        dh3,
        r3,
        denc,
        r2,
        r1,
        u,
        self_saved[0],
        attn,
        ups,
        downs,
        gains,
        shifts,
        mate,
        later(2, bits, ffn1) + attn_flows(3, [dw8, dw11], [dw9, dw10]) + [mate],
        plan,
        3,
    )
    ffn1, cross = sums[:3], sums[3:]

    plan = {}
    stages = range(bits)
    own = [
        Flow(order, 0, bits, [], (count, share, COLS // 2)) for count in (6, 3, 3) for order in orders[:2]
    ]
    swaps = [Swap(0, (rows, width)) for _ in range(2)]
    total = Total(bits, [norms_a, norms_b])
    for index in reversed(range(3)):
        spots = LAST_OWN[index]
        place_stages(plan, (6 + 2 * index, 7 + 2 * index), stages, spots[0], spots[1:])
    place_stages(plan, (0, 1, 2), stages, (0, 0), LAST_FFN)
    place_stages(plan, (3, 4), range(3, bits), (0, 0), LAST_CROSS)
    place_stages(plan, (5,), stages, LAST_NORMS[0], LAST_NORMS[1:])
    place_stages(plan, (13,), [0], (1, 5), [(3, 1)])
    place_stages(plan, (12,), [0], (3, 5), [(3, 9)])
    (data,), sums = attend_back(
        do,
        self_saved,
        mates,
        dr,
        (source, target),
        False,
        attn,
        0,
        ffn_flows(bits, dup0, ddown0, ([dw3], [dw7]))
        + later(3, bits, cross)
        + [total]
        + own
        + swaps,
        plan,
        4,
        (own, swaps, total),
    )
    ffn0, cross = sums[:3], sums[3:5]
    norms, *own_sums, source_back, target_back = sums[5:]

    everything = slice(None)
    named = [(array, "attn", places, (everything,) * 2) for array, places in zip(cross, ((8, 11), (9, 10)))]
    for index, sums in enumerate((ffn0, ffn1)):
        squares = (3, 7, None) if index == 0 else (None,) * 3
        named += [
            (array, kind, (index, place), None) for array, kind, place in zip(sums, ("up", "down", "both"), squares)
        ]
    for number, array in enumerate(own_sums):
        kind, first = OWN_PARTS[number // 2]
        places, cols = [], []
        for index in range(first, first + array.shape[0]):
            start = index // 3 * COLS + number % 2 * (COLS // 2)
            places.append(4 * kind + index % 3)
            cols.append(slice(start, start + COLS // 2))
        named.append((array, "attn", tuple(places), tuple(cols)))
    grad_source, grad_target, grad_attn, grad_up, grad_down, grad_gains, grad_shifts = finish(
        data, source_back, target_back, norms, named, share, inner, devices
    )
    return decoded, grad_source, grad_target, grad_attn, grad_up, grad_down, grad_gains, grad_shifts


def solution(mesh):
    rows = P(None, AXES, None)
    return jax.shard_map(
        body,
        mesh=mesh,
        in_specs=(rows, rows, rows, P(None, "dp"), P(None, "dp"), P(), P(), P(), P(), P()),
        out_specs=(rows, rows, rows, rows, rows, rows, P(None, AXES), P(None, AXES)),
        check_vma=False,
    )
```

```python
import functools
import math

import jax
import jax.numpy as jnp
from jax import lax
from jax.experimental import pallas as pl
from jax.experimental.pallas import tpu as pltpu
from jax.sharding import PartitionSpec as P

HEADS = 8
SHORT = 256
LONG = 1024

EPSILON = 1e-05
MASKED = -1e30
F32 = jnp.float32
BF16 = jnp.bfloat16
AXES = ("dp", "head")
COLS = 256
CHUNK = 512

NN = (((1,), (0,)), ((), ()))
NT = (((1,), (1,)), ((), ()))
TN = (((0,), (0,)), ((), ()))


def dot(left, right, dims=NN):
    return lax.dot_general(left, right, dims, preferred_element_type=F32)


def params():
    return pltpu.CompilerParams(vmem_limit_bytes=63 << 20)


def cost(flops, moved, powers=0):
    return pl.CostEstimate(flops=int(flops), bytes_accessed=int(moved), transcendentals=int(powers))


def whole(array):
    return pl.BlockSpec(array.shape, lambda *step: (0,) * array.ndim, pipeline_mode=pl.Buffered(1))


def shaped(shape, kind):
    return jax.ShapeDtypeStruct(shape, kind)


def lanes():
    return lax.broadcasted_iota(jnp.int32, (1, 128), 1)


def one_head(which, pair):
    keep = (lanes() < 64) if which == 0 else (lanes() >= 64)
    return jnp.where(keep, pair, jnp.zeros_like(pair))


def join_heads(first, second):
    return jnp.where(lanes() < 64, first, second)


MESH = pl.DeviceIdType.MESH


def partner(bit):
    head_bits = lax.axis_size("head").bit_length() - 1
    data, head = lax.axis_index("dp"), lax.axis_index("head")
    if bit < head_bits:
        step = 1 << bit
        mine = (head // step) % 2
        return mine, (data, head + (1 - 2 * mine) * step)
    step = 1 << (bit - head_bits)
    mine = (data // step) % 2
    return mine, (data + (1 - 2 * mine) * step, head)


class Flow:
    def __init__(self, order, first, last, pieces, block=None):
        self.order, self.first, self.last = order, first, last
        self.bits = order[first:last]
        self.local = block is not None
        self.arrays = []
        self.pieces = []
        total = 0
        for array, lead, start, count in pieces:
            known = [index for index, other in enumerate(self.arrays) if other is array]
            if not known:
                self.arrays.append(array)
            index = known[0] if known else len(self.arrays) - 1
            self.pieces.append((index, lead, start, total, count))
            total += count
        self.block = block or (total,) + pieces[0][0].shape[-2:]

    def shape(self, stage):
        return (2,) * (len(self.order) - stage) + self.block

    def out(self):
        done = self.last == len(self.order)
        return shaped(self.shape(self.last), F32 if done else BF16)

    def scratch(self):
        stages = range(self.first, self.last)
        count = len(self.pieces)
        dma = pltpu.SemaphoreType.DMA
        return (
            ([] if self.local else [pltpu.VMEM(self.shape(self.first + 1), BF16)])
            + [pltpu.VMEM(self.shape(stage + 1), BF16) for stage in stages]
            + [pltpu.VMEM(self.shape(stage + 1), BF16) for stage in stages[:-1]]
            + [dma((len(stages),)), dma((len(stages),))]
            + [dma((count,)) for _ in range(0 if self.local else 3)]
        )

    def bind(self, inputs, out, scratch):
        stages = range(self.first, self.last)
        self.in_refs, self.out_ref = inputs, out
        count = len(stages)
        skip = 0 if self.local else 1
        self.own = scratch[0]
        self.got = dict(zip(stages, scratch[skip : skip + count]))
        self.sum = dict(zip(stages[:-1], scratch[skip + count :]))
        if self.local:
            self.send, self.recv = scratch[-2:]
        else:
            self.send, self.recv, self.local_sem, self.piece_send, self.piece_recv = scratch[-5:]

    def where(self, stage, index):
        left = sorted(self.order[stage:])
        place = len(left) - 1 - left.index(self.order[stage])
        return (slice(None),) * place + (index,)

    def piece_copies(self):
        stage = self.first
        mine, device = partner(self.order[stage])
        left = len(self.order) - stage
        for number, (index, lead, start, total, count) in enumerate(self.pieces):
            prefix = () if lead is None else (lead,)
            target = (slice(None),) * (left - 1) + (slice(total, total + count),)
            ref = self.in_refs[index]

            def part(value):
                at = self.where(stage, value)
                at += (slice(None),) * (left - len(at)) + (slice(start, start + count),)
                return ref.at[prefix + at]

            yield pltpu.make_async_remote_copy(
                src_ref=part(1 - mine),
                dst_ref=self.got[stage].at[target],
                send_sem=self.piece_send.at[number],
                recv_sem=self.piece_recv.at[number],
                device_id=device,
                device_id_type=MESH,
            )
            yield pltpu.make_async_copy(
                part(mine),
                self.own.at[target],
                self.local_sem.at[number],
            )

    def stage_copy(self, stage):
        mine, device = partner(self.order[stage])
        source = self.source if stage == self.first else self.sum[stage - 1]
        return pltpu.make_async_remote_copy(
            src_ref=source.at[self.where(stage, 1 - mine)],
            dst_ref=self.got[stage],
            send_sem=self.send.at[stage - self.first],
            recv_sem=self.recv.at[stage - self.first],
            device_id=device,
            device_id_type=MESH,
        )

    def start(self):
        if self.local:
            self.stage_copy(self.first).start()
        else:
            for copy in self.piece_copies():
                copy.start()

    def step(self, stage):
        mine, _ = partner(self.order[stage])
        if stage > self.first:
            self.stage_copy(stage).wait()
            kept = self.sum[stage - 1].at[self.where(stage, mine)]
        elif self.local:
            self.stage_copy(stage).wait()
            kept = self.source.at[self.where(stage, mine)]
        else:
            for copy in self.piece_copies():
                copy.wait()
            kept = self.own
        got = self.got[stage]
        last = stage == self.last - 1
        target = self.out_ref if last else self.sum[stage]
        kind = F32 if stage == len(self.order) - 1 else BF16
        dims = min(2, len(self.order) - stage - 1)

        def add(index, carry):
            at = tuple((index >> bit) & 1 for bit in range(dims))
            target[at] = kept[at].astype(kind) + got[at].astype(kind)
            return carry

        if dims:
            lax.fori_loop(0, 1 << dims, add, 0)
        else:
            target[...] = kept[...].astype(kind) + got[...].astype(kind)
        if not last:
            self.stage_copy(stage + 1).start()


class Swap:
    def __init__(self, bit, shape, array=None, kept=True):
        self.bits = (bit,)
        self.wide = shape
        self.kept = kept
        self.arrays = [] if array is None else [array]

    def out(self):
        return shaped(self.wide, BF16) if self.kept else None

    def scratch(self):
        return [pltpu.VMEM(self.wide, BF16), pltpu.SemaphoreType.DMA, pltpu.SemaphoreType.DMA]

    def bind(self, inputs, out, scratch):
        self.source = inputs[0] if inputs else None
        self.out_ref = out
        self.got, self.send, self.recv = scratch

    def copy(self):
        return pltpu.make_async_remote_copy(
            src_ref=self.source,
            dst_ref=self.got,
            send_sem=self.send,
            recv_sem=self.recv,
            device_id=partner(self.bits[0])[1],
            device_id_type=MESH,
        )

    def start(self):
        self.copy().start()

    def step(self, stage):
        self.copy().wait()
        if self.kept:
            self.out_ref[...] = self.got[...]


class Total:
    def __init__(self, bits, arrays):
        self.bits = tuple(range(bits))
        self.arrays = []
        self.terms = arrays

    def out(self):
        return shaped(self.terms[0].shape, F32)

    def scratch(self):
        count = len(self.bits)
        whole_shape = (count,) + self.terms[0].shape
        dma = pltpu.SemaphoreType.DMA((count,))
        return [pltpu.VMEM(whole_shape, F32), pltpu.VMEM(whole_shape, F32), dma, dma]

    def bind(self, inputs, out, scratch):
        self.out_ref = out
        self.held, self.got, self.send, self.recv = scratch

    def copy(self, stage):
        return pltpu.make_async_remote_copy(
            src_ref=self.held.at[stage],
            dst_ref=self.got.at[stage],
            send_sem=self.send.at[stage],
            recv_sem=self.recv.at[stage],
            device_id=partner(stage)[1],
            device_id_type=MESH,
        )

    def start(self):
        self.held[0] = functools.reduce(lambda left, right: left + right, [ref[...] for ref in self.refs])
        self.copy(0).start()

    def step(self, stage):
        self.copy(stage).wait()
        total = self.held[stage] + self.got[stage]
        if stage == len(self.bits) - 1:
            self.out_ref[...] = total
        else:
            self.held[stage + 1] = total
            self.copy(stage + 1).start()


def greet(bits):
    ready = pltpu.get_barrier_semaphore()
    for bit in bits:
        _, device = partner(bit)
        pl.semaphore_signal(ready, inc=1, device_id=device, device_id_type=MESH)
    pl.semaphore_wait(ready, len(bits))


def call(kernel, steps, ins, outs, scratch, name, estimate, flows=(), plan=None, collective=None):
    extra_in = [array for flow in flows for array in flow.arrays]
    bits = sorted({bit for flow in flows for bit in flow.bits})
    counts = (len(ins), len(outs), len(scratch))

    def body(*refs):
        refs = list(refs)
        take = lambda count: [refs.pop(0) for _ in range(count)]
        main = take(counts[0])
        inputs = [take(len(flow.arrays)) for flow in flows]
        main += take(counts[1])
        results = [take(1)[0] if flow.out() else None for flow in flows]
        main += take(counts[2])
        for flow, given, result in zip(flows, inputs, results):
            flow.bind(given, result, take(len(flow.scratch())))

        def tick(slot, now=None):
            for (step, place), actions in (plan or {}).items():
                if place == slot:

                    here = pl.program_id(0) == step

                    @pl.when(here if now is None else here & now)
                    def _():
                        if (step, slot) == (0, 0):
                            greet(bits)
                        for number, stage in actions:
                            if stage is None:
                                flows[number].start()
                            else:
                                flows[number].step(stage)

        kernel(tick, *main)

    still = lambda shape: pl.BlockSpec(shape, lambda step: (0,) * len(shape))
    given_out = [flow.out() for flow in flows if flow.out()]
    remote = dict(collective_id=collective, has_side_effects=True) if flows else {}
    result = pl.pallas_call(
        body,
        grid=(steps,),
        out_shape=[shape for shape, _ in outs] + given_out,
        in_specs=[spec for _, spec in ins] + [pl.BlockSpec(memory_space=pl.ANY)] * len(extra_in),
        out_specs=[spec for _, spec in outs] + [still(shape.shape) for shape in given_out],
        scratch_shapes=list(scratch) + [shape for flow in flows for shape in flow.scratch()],
        compiler_params=pltpu.CompilerParams(vmem_limit_bytes=63 << 20, **remote),
        cost_estimate=estimate,
        name=name,
    )(*[array for array, _ in ins], *extra_in)
    return result[: len(outs)], result[len(outs) :]


def scores_bias(own_length, other_length, width, ahead):
    row = lax.broadcasted_iota(jnp.int32, (width, width), 0)
    column = lax.broadcasted_iota(jnp.int32, (width, width), 1)
    own = jnp.where((column < own_length) & (column <= row + ahead), 0.0, MASKED).astype(F32)
    if other_length is None:
        return own
    other = jnp.where(column < other_length, 0.0, MASKED).astype(F32)
    return jnp.concatenate([own, other], axis=1)


def attend_rows(bias, q_ref, k_ref, v_ref, e_ref, o_ref, inv_ref, rows, keys):
    count = bias.shape[1]
    ones = jnp.ones((count, 128), BF16)
    for pair in range(COLS // 128):
        cols = slice(pair * 128, pair * 128 + 128)
        queries = q_ref[rows, cols]
        key_pair = k_ref[keys, cols]
        value_ext = jnp.concatenate([v_ref[keys, cols], ones], axis=1)
        outs, inverses = [], []
        for which in range(2):
            scores = dot(one_head(which, queries), key_pair, NT) + bias
            highest = jnp.max(scores, axis=1, keepdims=True)
            powers = jnp.exp(scores - highest).astype(BF16)
            e_ref[pair * 2 + which, rows, :] = powers
            mixed = dot(powers, value_ext)
            inverse = 1.0 / mixed[:, 128:]
            outs.append(mixed[:, :128] * inverse)
            inverses.append(inverse)
        o_ref[rows, cols] = join_heads(*outs).astype(BF16)
        inv_ref[rows, cols] = join_heads(*inverses)


def attend_kernel(causal, cross, mates, tick, *refs):
    number = len(causal)
    ins = refs[: 2 if cross else number]
    (
        short_ref,
        long_ref,
        wq_ref,
        wk_ref,
        wv_ref,
        o_ref,
        inv_ref,
        q_ref,
        ks_ref,
        vs_ref,
        kl_ref,
        vl_ref,
        es_ref,
        el_ref,
        *scratch,
    ) = refs[len(ins) :]
    rows = ins[0].shape[1]
    scale = 0.125
    step = pl.program_id(0)
    which = step // 2
    place = lax.axis_index("head")
    half = place % 2
    for mate, ref in zip(mates, ins[-len(mates) :]):
        mate.source = ref.at[1]
    tick(0)
    if number == 1:
        xq_ref, xk_ref = ins[0], ins[-1]
    else:
        xq_ref = xk_ref = scratch[0]
        for index in range(number):

            @pl.when(step == 2 * index)
            def _():
                xq_ref[...] = ins[index][...]

    kind = sum([jnp.where(which == index, 1, 0) for index in range(number) if causal[index]], 0)
    ahead = (1 - kind) * LONG
    q_ref[0, 0] = (dot(xq_ref[0], wq_ref[0]) * scale).astype(BF16)
    ks_ref[0] = dot(xk_ref[0], wk_ref[0]).astype(BF16)
    vs_ref[0] = dot(xk_ref[0], wv_ref[0]).astype(BF16)
    slots = rows // SHORT
    for slot in range(slots):
        bias = scores_bias(short_ref[kind, place * slots + slot], None, SHORT, ahead)
        here = slice(slot * SHORT, (slot + 1) * SHORT)
        attend_rows(
            bias,
            q_ref.at[0, 0],
            ks_ref.at[0],
            vs_ref.at[0],
            es_ref.at[0],
            o_ref.at[0, 0],
            inv_ref.at[0, 0],
            here,
            here,
        )
    q_ref[0, 1] = (dot(xq_ref[1], wq_ref[0]) * scale).astype(BF16)
    kl_ref[0, :rows] = dot(xk_ref[1], wk_ref[0]).astype(BF16)
    vl_ref[0, :rows] = dot(xk_ref[1], wv_ref[0]).astype(BF16)
    tick(1)
    if number == 1:
        mate_ref = mates[0].got
    else:
        mate_ref = scratch[1]
        for index in range(number):

            @pl.when(step == 2 * index)
            def _():
                mate_ref[...] = mates[index].got[...]

    kl_ref[0, rows:] = dot(mate_ref[...], wk_ref[0]).astype(BF16)
    vl_ref[0, rows:] = dot(mate_ref[...], wv_ref[0]).astype(BF16)
    everything = slice(None)
    length = long_ref[kind, place // 2]
    other = (length - (1 - half) * rows) * (1 - kind * (1 - half))
    bias = scores_bias(length - half * rows, other, rows, ahead)
    attend_rows(
        bias,
        q_ref.at[0, 1],
        kl_ref.at[0],
        vl_ref.at[0],
        el_ref.at[0],
        o_ref.at[0, 1],
        inv_ref.at[0, 1],
        everything,
        everything,
    )


def attend(xs, causal, cross, weights, base, lengths, collective):
    _, rows, width = xs[0].shape
    number = len(causal)
    heads = width // 64
    place = lambda step: step // 2
    weight = lambda index: (
        weights,
        pl.BlockSpec((1, width, COLS), lambda step: (base + 4 * place(step) + index, 0, step % 2)),
    )
    both = lambda kind: (
        shaped((number, 2, rows, width), kind),
        pl.BlockSpec((1, 2, rows, COLS), lambda step: (place(step), 0, 0, step % 2)),
    )
    cols = lambda count: (
        shaped((number, count, width), BF16),
        pl.BlockSpec((1, count, COLS), lambda step: (place(step), 0, step % 2)),
    )
    powers = lambda count: (
        shaped((number, heads, rows, count), BF16),
        pl.BlockSpec((1, COLS // 64, rows, count), lambda step: (place(step), step % 2, 0, 0)),
    )
    flops = 2 * rows * width * width * 7 + 4 * rows * width * (SHORT + LONG)
    mates = [Swap(0, (rows, width)) for _ in range(number)]
    plan = {(0, 0): [(index, None) for index in range(number)]}
    for index in range(number):
        plan[2 * index, 1] = [(index, 0)]
    return call(
        functools.partial(attend_kernel, causal, cross, mates),
        2 * number,
        [(array, whole(array)) for array in xs]
        + [(array, pl.BlockSpec(memory_space=pltpu.SMEM)) for array in lengths]
        + [weight(0), weight(1), weight(2)],
        [both(BF16), both(F32), both(BF16), cols(rows), cols(rows), cols(LONG), cols(LONG)]
        + [powers(SHORT), powers(LONG)],
        [] if number == 1 else [pltpu.VMEM((2, rows, width), BF16), pltpu.VMEM((rows, width), BF16)],
        "attend",
        cost(flops * 2 * number, number * (22 << 20), number * heads * rows * (SHORT + LONG)),
        mates,
        plan,
        collective,
    )


def attend_back_rows(
    do_ref,
    o_ref,
    inv_ref,
    q_ref,
    k_ref,
    v_ref,
    e_ref,
    dq_ref,
    dk_ref,
    dv_ref,
    rows,
    keys,
    pair,
    scale,
):
    cols = pl.ds(pl.multiple_of(pair * 128, 128), 128)
    grad = do_ref[rows, cols].astype(F32) * inv_ref[rows, cols]
    product = grad * o_ref[rows, cols].astype(F32)
    grad_low = grad.astype(BF16)
    queries = q_ref[rows, cols]
    key_pair = k_ref[keys, cols]
    value_pair = v_ref[keys, cols]
    grad_turned = grad.T.astype(BF16)
    queries_turned = queries.astype(F32).T.astype(BF16)
    grad_q, grad_k, grad_v = [], [], []
    for which in range(2):
        inner = jnp.sum(one_head(which, product), axis=1, keepdims=True)
        grad_probs = dot(one_head(which, grad_low), value_pair, NT)
        powers = e_ref[pair * 2 + which, rows, :]
        grad_scores = (powers.astype(F32) * (grad_probs - inner)).astype(BF16)
        grad_q.append(dot(grad_scores, key_pair))
        head = slice(which * 64, which * 64 + 64)
        grad_v.append(dot(grad_turned[head], powers))
        grad_k.append(dot(queries_turned[head], grad_scores))
    dq_ref[rows, cols] = (join_heads(*grad_q) * scale).astype(BF16)
    dk_ref[keys, cols] = jnp.concatenate(grad_k, axis=0).T.astype(BF16)
    dv_ref[keys, cols] = jnp.concatenate(grad_v, axis=0).T.astype(BF16)


def attend_back_kernel(number, cross, own, swaps, total, after, tick, *refs):
    refs = list(refs)
    take = lambda count: [refs.pop(0) for _ in range(count)]
    if total:
        total.refs = take(len(total.terms))
    do_ref, o_ref, inv_ref, q_ref, ks_ref, vs_ref, kl_ref, vl_ref, es_ref, el_ref, resid_ref, *ins = take(
        11 + (2 if cross else number)
    )
    wq_ref, wk_ref, wv_ref = take(3)
    mates = take(number)
    dx_ref = take(1)[0]
    if cross:
        dy_ref, dmate_ref, dwq_ref, dwk_ref, dwv_ref = take(5)
    dqs, dks, dvs, dql, dkl, dvl, mate_sum, mate_low, resid_sem, *scratch = refs
    step = pl.program_id(0)
    first = step % 2 == 0
    if cross:
        xq_ref, xk_ref, mate_ref = ins[0], ins[1], mates[0]
        dy_ref = dy_ref.at[0]
    else:
        xq_ref = xk_ref = scratch[0]
        mate_ref = scratch[1]
        terms_ref = scratch[2]
        for place, flow in enumerate(own):
            kind, start = OWN_PARTS[place // 2]
            every = (slice(None),) * len(flow.order)
            flow.source = terms_ref.at[(kind, place % 2) + every + (slice(start, start + flow.block[0]),)]
        for index in range(number):
            swaps[index].source = mate_low.at[index]

            @pl.when(step == 2 * (number - 1 - index))
            def _():
                xq_ref[...] = ins[index][...]
                mate_ref[...] = mates[index][...]

        dy_ref = dx_ref.at[0]
    dx_ref = dx_ref.at[0]
    rows = xq_ref.shape[1]
    load = pltpu.make_async_copy(resid_ref.at[number - 1 - step // 2], dx_ref, resid_sem)

    @pl.when(first)
    def _():
        load.start()

    scale = 0.125
    everything = slice(None)
    tick(0)
    pairs = COLS // 128

    def long_pair(pair, carry):
        attend_back_rows(
            do_ref.at[0, 1],
            o_ref.at[0, 1],
            inv_ref.at[0, 1],
            q_ref.at[0, 1],
            kl_ref.at[0],
            vl_ref.at[0],
            el_ref.at[0],
            dql,
            dkl,
            dvl,
            everything,
            everything,
            pair,
            scale,
        )
        for index in range(pairs):
            tick(1 + index, pair == index)
        return carry

    def short_slot(slot, carry):
        here = pl.ds(pl.multiple_of(slot * SHORT, SHORT), SHORT)
        for pair in range(pairs):
            attend_back_rows(
                do_ref.at[0, 0],
                o_ref.at[0, 0],
                inv_ref.at[0, 0],
                q_ref.at[0, 0],
                ks_ref.at[0],
                vs_ref.at[0],
                es_ref.at[0],
                dqs,
                dks,
                dvs,
                here,
                here,
                pair,
                scale,
            )
        return carry

    lax.fori_loop(0, pairs, long_pair, 0)
    lax.fori_loop(0, rows // SHORT, short_slot, 0)
    tick(3)
    wq, wk, wv = wq_ref[0], wk_ref[0], wv_ref[0]
    front = slice(0, rows)
    other = slice(rows, 2 * rows)
    dwq = dot(xq_ref[0], dqs[...], TN) + dot(xq_ref[1], dql[...], TN)
    short, long, mate = xk_ref[0], xk_ref[1], mate_ref[...]
    dwk = dot(short, dks[...], TN) + dot(long, dkl[front], TN) + dot(mate, dkl[other], TN)
    dwv = dot(short, dvs[...], TN) + dot(long, dvl[front], TN) + dot(mate, dvl[other], TN)
    if cross:
        dwq_ref[...] = dwq.astype(BF16)
        dwk_ref[...] = dwk.astype(BF16)
        dwv_ref[...] = dwv.astype(BF16)
    else:
        flow = own[0]
        _, share, columns = flow.block
        for index, total_w in enumerate((dwq, dwk, dwv)):
            low = total_w.astype(BF16)
            for device in range(low.shape[0] // share):
                at = tuple((device >> bit) & 1 for bit in reversed(range(len(flow.order))))
                for color in range(2):
                    terms_ref[(1 - step // 2, color) + at + (step % 2 * 3 + index,)] = low[
                        device * share : (device + 1) * share, color * columns : (color + 1) * columns
                    ]

    tick(4)

    @pl.when(first)
    def _():
        load.wait()
        if cross:
            dy_ref[...] = jnp.zeros_like(dy_ref)
        mate_sum[...] = jnp.zeros_like(mate_sum)

    mate_sum[...] += dot(dkl[other], wk, NT) + dot(dvl[other], wv, NT)
    if cross:

        @pl.when(jnp.logical_not(first))
        def _():
            dmate_ref[...] = mate_sum[...].astype(BF16)

    else:
        for index in range(number):

            @pl.when(step == 2 * (number - 1 - index) + 1)
            def _():
                mate_low[index] = mate_sum[...].astype(BF16)

    tick(5)
    dx_ref[0] += dot(dqs[...], wq, NT)
    dx_ref[1] += dot(dql[...], wq, NT)
    dy_ref[0] += dot(dks[...], wk, NT) + dot(dvs[...], wv, NT)
    dy_ref[1] += dot(dkl[front], wk, NT) + dot(dvl[front], wv, NT)
    for slot in range(6, 6 + after):
        tick(slot)


def attend_back(grad, saved, mates, resid, xs, cross, weights, base, flows, plan, collective, last=None):
    _, rows, width = xs[0].shape
    number = 1 if cross else len(xs)
    place = lambda step: number - 1 - step // 2
    weight = lambda index: (
        weights,
        pl.BlockSpec((1, width, COLS), lambda step: (base + 4 * place(step) + index, 0, step % 2)),
    )
    both = pl.BlockSpec((1, 2, rows, COLS), lambda step: (place(step), 0, 0, step % 2))
    cols = lambda count: pl.BlockSpec((1, count, COLS), lambda step: (place(step), 0, step % 2))
    powers = lambda count: pl.BlockSpec((1, COLS // 64, rows, count), lambda step: (place(step), step % 2, 0, 0))
    deep = pl.BlockSpec((1, 2, rows, width), lambda step: (place(step), 0, 0, 0))
    flops = 2 * rows * width * width * 14 + 8 * rows * width * (SHORT + LONG)
    specs = [both] * 4 + [cols(rows)] * 2 + [cols(LONG)] * 2 + [powers(SHORT), powers(LONG)]
    o, inverse, *rest = saved
    own, swaps, total = last or ((), (), None)
    data = (shaped((number, 2, rows, width), F32), deep)
    outs = [data]
    scratch = (
        [pltpu.VMEM((rows, COLS), BF16)] * 4
        + [pltpu.VMEM((LONG, COLS), BF16)] * 2
        + [pltpu.VMEM((rows, width), F32), pltpu.VMEM((number, rows, width), BF16)]
        + [pltpu.SemaphoreType.DMA]
    )
    if cross:
        outs += [data, (shaped((rows, width), BF16), pl.BlockSpec((rows, width), lambda step: (0, 0)))]
        outs += [(shaped((width, width), BF16), pl.BlockSpec((width, COLS), lambda step: (0, step)))] * 3
    else:
        scratch += [pltpu.VMEM((2, rows, width), BF16), pltpu.VMEM((rows, width), BF16)]
        _, share, columns = own[0].block
        scratch += [pltpu.VMEM((number, 2) + own[0].shape(0)[:-3] + (6, share, columns), BF16)]
    after = 1 + max([spot for _, spot in plan] + [5]) - 6
    norms = total.terms if total else []
    return call(
        functools.partial(attend_back_kernel, number, cross, own, swaps, total, after),
        2 * number,
        [(array, whole(array)) for array in norms]
        + list(zip((grad, o, inverse, *rest), specs))
        + [(resid, pl.BlockSpec(memory_space=pl.ANY))]
        + [(array, whole(array)) for array in xs]
        + [weight(0), weight(1), weight(2)]
        + [(array, whole(array)) for array in mates],
        outs,
        scratch,
        "attend_back",
        cost(flops * 2 * number, number * (28 << 20)),
        flows,
        plan,
        collective,
    )


BLOCK = 512
WIDE = 1024
ANY = pl.BlockSpec(memory_space=pl.ANY)


def norm_parts(resid):
    average = jnp.mean(resid, axis=-1, keepdims=True)
    centered = resid - average
    variance = jnp.mean(centered * centered, axis=-1, keepdims=True)
    spread = lax.rsqrt(variance + EPSILON)
    return centered * spread, spread


def norm_back(normal, spread, gain, grad):
    scaled = grad * gain
    first = jnp.mean(scaled, axis=-1, keepdims=True)
    second = jnp.mean(scaled * normal, axis=-1, keepdims=True)
    return (scaled - first - normal * second) * spread


def add_norm_grads(ref, place, grad, normal):
    ref[place : place + 1, :] += jnp.sum(grad * normal, axis=0, keepdims=True)
    ref[8 + place : 9 + place, :] += jnp.sum(grad, axis=0, keepdims=True)


def logistic(value):
    return 1.0 / (1.0 + jnp.exp(-value))


def each_block(count, work, size=BLOCK):
    def step(index, carry):
        work(pl.ds(pl.multiple_of(index * size, size), size))
        return carry

    lax.fori_loop(0, count // size, step, 0)


def each_chunk(count, work):
    def step(index, carry):
        work(index)
        return carry

    lax.fori_loop(0, count, step, 0)


class Loads:
    def __init__(self, pairs, sems):
        self.copies = [
            pltpu.make_async_copy(source, target, sems.at[index])
            for index, (source, target) in enumerate(pairs)
        ]

    def start(self):
        for copy in self.copies:
            copy.start()

    def wait(self, *places):
        for place in places:
            self.copies[place].wait()


def chunk_loads(up_ref, down_ref, up_s, down_s, sems):
    def copies(chunk):
        part = pl.ds(pl.multiple_of(chunk * CHUNK, CHUNK), CHUNK)
        return (
            pltpu.make_async_copy(up_ref.at[:, part], up_s.at[chunk], sems.at[0, chunk]),
            pltpu.make_async_copy(down_ref.at[part], down_s.at[chunk], sems.at[1, chunk]),
        )

    return copies


def feed_chunks(copies, low_s, total_s, up_s, down_s, u_s, a_s, out=None):
    count = low_s.shape[0]

    def chunk_work(chunk):
        for copy in copies(chunk):
            copy.wait()

        def block_work(rows):
            upward = dot(low_s[rows, :], up_s[chunk])
            u_s[chunk, rows, :] = upward
            active = (upward * logistic(upward)).astype(BF16)
            if a_s is not None:
                a_s[chunk, rows, :] = active
            total_s[rows, :] += dot(active, down_s[chunk])

        each_block(count, block_work, WIDE)
        if out is not None:
            out(chunk)

    each_chunk(up_s.shape[0], chunk_work)


def feed_back_chunks(tick, wait, low_s, hidden_s, total_s, up_s, down_s, u_s, a_s, du_s, write):
    count = low_s.shape[0]
    chunks = up_s.shape[0]

    def chunk_work(chunk):
        wait(chunk)
        store = a_s is None
        active_ref = du_s.at[1] if store else a_s.at[chunk]

        def block_work(rows):
            upward = u_s[chunk, rows, :]
            gate = logistic(upward)
            if store:
                active_ref[rows, :] = (upward * gate).astype(BF16)
            grad_active = dot(low_s[rows, :], down_s[chunk], NT)
            grad_up = (grad_active * gate * (1.0 + upward * (1.0 - gate))).astype(BF16)
            du_s[0, rows, :] = grad_up
            total_s[rows, :] += dot(grad_up, up_s[chunk], NT)

        each_block(count, block_work, WIDE)
        write(chunk, dot(hidden_s[...], du_s[0], TN), dot(active_ref[...], low_s[...], TN))
        for index in range(chunks):
            tick(2 + index, chunk == index)

    each_chunk(chunks, chunk_work)


def feed_kernel(
    tick,
    os_ref,
    x_ref,
    z_ref,
    wm_ref,
    wo_ref,
    up_ref,
    down_ref,
    gain_ref,
    shift_ref,
    u_ref,
    r1_ref,
    r2_ref,
    enc_ref,
    r3_ref,
    h3_ref,
    *scratch,
):
    up_s, down_s, u_s, low_s, sems, out_sems = scratch
    copies = chunk_loads(up_ref.at[0], down_ref.at[0], up_s, down_s, sems)
    chunks = up_s.shape[0]
    for chunk in range(chunks):
        for copy in copies(chunk):
            copy.start()
    count = low_s.shape[0]

    def first(rows):
        resid = x_ref[rows, :].astype(F32) + dot(os_ref[0, rows, :], wo_ref[0])
        r1_ref[rows, :] = resid
        normal, _ = norm_parts(resid)
        hidden = normal * gain_ref[0:1] + shift_ref[0:1]
        r2_ref[rows, :] = hidden
        low_s[rows, :] = hidden.astype(BF16)
        resid = z_ref[rows, :].astype(F32) + dot(os_ref[1, rows, :], wm_ref[0])
        r3_ref[rows, :] = resid
        normal, _ = norm_parts(resid)
        h3_ref[rows, :] = (normal * gain_ref[2:3] + shift_ref[2:3]).astype(BF16)

    each_block(count, first)
    keep = lambda chunk: pltpu.make_async_copy(u_s.at[chunk], u_ref.at[chunk], out_sems.at[chunk])
    feed_chunks(copies, low_s, r2_ref, up_s, down_s, u_s, None, lambda chunk: keep(chunk).start())

    def last(rows):
        normal, _ = norm_parts(r2_ref[rows, :])
        enc_ref[rows, :] = (normal * gain_ref[1:2] + shift_ref[1:2]).astype(BF16)

    each_block(count, last)
    for chunk in range(chunks):
        keep(chunk).wait()


def picked(array, index):
    return array, pl.BlockSpec((1,) + array.shape[1:], lambda step: (index, 0, 0))


def flat(array):
    return array.reshape((-1,) + array.shape[2:])


def full(array):
    return array, whole(array)


def new(kind, *shape):
    return shaped(shape, kind), pl.BlockSpec(shape, lambda step: (0,) * len(shape))


def weight_scratch(width, chunks):
    return [
        pltpu.VMEM((chunks, width, CHUNK), BF16),
        pltpu.VMEM((chunks, CHUNK, width), BF16),
    ]


def feed(o, x, z, attn, ups, downs, gains, shifts):
    shape = x.shape
    o, x, z = o.reshape((2, -1, shape[-1])), flat(x), flat(z)
    count, width = x.shape
    inner = ups.shape[2]
    chunks = inner // CHUNK
    results, _ = call(
        feed_kernel,
        1,
        [full(o), full(x), full(z), picked(attn, 7), picked(attn, 3)]
        + [(ups, ANY), (downs, ANY), full(gains), full(shifts)],
        [
            (shaped((chunks, count, CHUNK), F32), ANY),
            new(F32, count, width),
            new(F32, count, width),
            new(BF16, count, width),
            new(F32, count, width),
            new(BF16, count, width),
        ],
        weight_scratch(width, chunks)
        + [
            pltpu.VMEM((chunks, count, CHUNK), F32),
            pltpu.VMEM((count, width), BF16),
            pltpu.SemaphoreType.DMA((2, chunks)),
            pltpu.SemaphoreType.DMA((chunks,)),
        ],
        "feed",
        cost(2 * count * width * (2 * width + 2 * inner), 28 << 20, 2 * count * inner),
    )
    u, r1, r2, enc, r3, h3 = results
    return u, r1, r2, enc.reshape(shape), r3, h3.reshape(shape)


def turn_kernel(
    tick,
    o_ref,
    r3_ref,
    wo_ref,
    cot_ref,
    up_ref,
    down_ref,
    gain_ref,
    shift_ref,
    out_ref,
    dr_ref,
    do_ref,
    dup_ref,
    ddown_ref,
    dwo_ref,
    norm_ref,
    *scratch,
):
    up_s, down_s, u_s, a_s, low_s, hidden_s, du_s, cot_s, total_s, normal_s, spread_s, sems, cot_sem = scratch
    copies = chunk_loads(up_ref.at[1], down_ref.at[1], up_s, down_s, sems)
    chunks = up_s.shape[0]
    for chunk in range(chunks):
        for copy in copies(chunk):
            copy.start()
    load = pltpu.make_async_copy(cot_ref, cot_s, cot_sem)
    load.start()
    count = low_s.shape[0]
    norm_ref[...] = jnp.zeros_like(norm_ref)

    def first(rows):
        normal3, _ = norm_parts(r3_ref[rows, :])
        resid4 = normal3 * gain_ref[2:3] + shift_ref[2:3] + dot(o_ref[rows, :], wo_ref[0])
        normal4, spread4 = norm_parts(resid4)
        hidden = normal4 * gain_ref[3:4] + shift_ref[3:4]
        normal_s[rows, :] = normal4
        spread_s[rows, :] = spread4
        total_s[rows, :] = hidden
        hidden_s[rows, :] = hidden.astype(BF16)

    each_block(count, first)
    feed_chunks(copies, hidden_s, total_s, up_s, down_s, u_s, a_s)
    load.wait()

    def top(rows):
        normal5, spread5 = norm_parts(total_s[rows, :])
        out_ref[rows, :] = (normal5 * gain_ref[4:5] + shift_ref[4:5]).astype(BF16)
        grad = cot_s[rows, :].astype(F32)
        add_norm_grads(norm_ref, 4, grad, normal5)
        grad = norm_back(normal5, spread5, gain_ref[4:5], grad)
        total_s[rows, :] = grad
        low_s[rows, :] = grad.astype(BF16)

    each_block(count, top)

    def write(chunk, dup, ddown):
        dup_ref[chunk] = dup.astype(BF16)
        ddown_ref[chunk] = ddown.astype(BF16)

    feed_back_chunks(
        tick, lambda chunk: None, low_s, hidden_s, total_s, up_s, down_s, u_s, a_s, du_s, write
    )

    def bottom(rows):
        grad = total_s[rows, :]
        normal4 = normal_s[rows, :]
        add_norm_grads(norm_ref, 3, grad, normal4)
        grad = norm_back(normal4, spread_s[rows, :], gain_ref[3:4], grad)
        dr_ref[rows, :] = grad
        low = grad.astype(BF16)
        low_s[rows, :] = low
        do_ref[rows, :] = dot(low, wo_ref[0], NT).astype(BF16)

    each_block(count, bottom)
    dwo_ref[...] = dot(o_ref[...], low_s[...], TN).astype(BF16)


def turn(o, r3, cot, attn, ups, downs, gains, shifts):
    rows = cot.shape[1]
    o, cot = flat(flat(o)), flat(cot)
    count, width = r3.shape
    inner = ups.shape[2]
    chunks = inner // CHUNK
    wide = pltpu.VMEM((count, width), BF16)
    results, _ = call(
        turn_kernel,
        1,
        [full(o), full(r3), picked(attn, 11), (cot, ANY), (ups, ANY), (downs, ANY), full(gains), full(shifts)],
        [
            new(BF16, count, width),
            new(F32, count, width),
            new(BF16, count, width),
            new(BF16, chunks, width, CHUNK),
            new(BF16, chunks, CHUNK, width),
            new(BF16, width, width),
            new(F32, 16, width),
        ],
        weight_scratch(width, chunks)
        + [
            pltpu.VMEM((chunks, count, CHUNK), F32),
            pltpu.VMEM((chunks, count, CHUNK), BF16),
            wide,
            wide,
            pltpu.VMEM((1, count, CHUNK), BF16),
            wide,
            pltpu.VMEM((count, width), F32),
            pltpu.VMEM((count, width), F32),
            pltpu.VMEM((count, 1), F32),
            pltpu.SemaphoreType.DMA((2, chunks)),
            pltpu.SemaphoreType.DMA,
        ],
        "turn",
        cost(6 * count * width * (width + 2 * inner), 20 << 20, 4 * count * inner),
    )
    out, dr, do, dup, ddown, dwo, norms = results
    pair = lambda array: array.reshape((2, rows) + array.shape[1:])
    return pair(out), pair(dr)[None], pair(do)[None], dup, ddown.reshape(inner, width), dwo, norms


def feed_back_kernel(
    mate,
    tick,
    gradm_ref,
    r3_ref,
    wm_ref,
    wo_ref,
    grad_ref,
    r2_ref,
    r1_ref,
    os_ref,
    u_ref,
    up_ref,
    down_ref,
    gain_ref,
    shift_ref,
    dr_ref,
    do_ref,
    dup_ref,
    ddown_ref,
    dwo_ref,
    dwm_ref,
    norm_ref,
    *scratch,
):
    (
        up_s,
        down_s,
        u_s,
        low_s,
        hidden_s,
        du_s,
        total_s,
        normal_s,
        spread_s,
        grad_s,
        r2_s,
        r1_s,
        os_s,
        sems,
        u_sems,
        in_sems,
    ) = scratch
    copies = chunk_loads(up_ref.at[0], down_ref.at[0], up_s, down_s, sems)
    chunks = up_s.shape[0]
    keep = lambda chunk: pltpu.make_async_copy(u_ref.at[chunk], u_s.at[chunk], u_sems.at[chunk])
    late = Loads([(os_ref, os_s), (grad_ref, grad_s), (r2_ref, r2_s), (r1_ref, r1_s)], in_sems)
    late.start()
    for chunk in range(chunks):
        keep(chunk).start()
        for copy in copies(chunk):
            copy.start()
    tick(0)
    count = low_s.shape[0]
    half = count // 2
    norm_ref[...] = jnp.zeros_like(norm_ref)

    def middle(rows):
        grad = gradm_ref[rows, :]
        normal, spread = norm_parts(r3_ref[rows, :])
        add_norm_grads(norm_ref, 2, grad, normal)
        grad = norm_back(normal, spread, gain_ref[2:3], grad)
        dr_ref[1, rows, :] = grad
        low = grad.astype(BF16)
        low_s[rows, :] = low
        do_ref[1, rows, :] = dot(low, wm_ref[0], NT).astype(BF16)

    each_block(count, middle)
    late.wait(0)
    dwm_ref[...] = dot(os_s[1], low_s[...], TN).astype(BF16)
    tick(1)

    def first(rows, grad):
        normal2, spread2 = norm_parts(r2_s[rows, :])
        add_norm_grads(norm_ref, 1, grad, normal2)
        grad = norm_back(normal2, spread2, gain_ref[1:2], grad)
        total_s[rows, :] = grad
        low_s[rows, :] = grad.astype(BF16)
        normal1, spread1 = norm_parts(r1_s[rows, :])
        normal_s[rows, :] = normal1
        spread_s[rows, :] = spread1
        hidden_s[rows, :] = (normal1 * gain_ref[0:1] + shift_ref[0:1]).astype(BF16)

    late.wait(1, 2, 3)
    each_block(half, lambda rows: first(rows, grad_s[rows, :]))

    def long(index, carry):
        start = pl.multiple_of(index * BLOCK, BLOCK)
        rows = pl.ds(pl.multiple_of(start + half, BLOCK), BLOCK)
        first(rows, grad_s[rows, :] + mate.got[pl.ds(start, BLOCK), :].astype(F32))
        return carry

    lax.fori_loop(0, half // BLOCK, long, 0)

    def write(chunk, dup, ddown):
        dup_ref[chunk] = dup.astype(BF16)
        ddown_ref[chunk] = ddown.astype(BF16)

    def wait(chunk):
        keep(chunk).wait()
        for copy in copies(chunk):
            copy.wait()

    feed_back_chunks(tick, wait, low_s, hidden_s, total_s, up_s, down_s, u_s, None, du_s, write)

    def bottom(rows):
        grad = total_s[rows, :]
        normal1 = normal_s[rows, :]
        add_norm_grads(norm_ref, 0, grad, normal1)
        grad = norm_back(normal1, spread_s[rows, :], gain_ref[0:1], grad)
        dr_ref[0, rows, :] = grad
        low = grad.astype(BF16)
        low_s[rows, :] = low
        do_ref[0, rows, :] = dot(low, wo_ref[0], NT).astype(BF16)

    each_block(count, bottom)
    dwo_ref[...] = dot(os_s[0], low_s[...], TN).astype(BF16)
    tick(2 + chunks)


def feed_back(gradm, r3, grad, r2, r1, u, o, attn, ups, downs, gains, shifts, mate, flows, plan, collective):
    gradm, grad = flat(flat(gradm)), flat(flat(grad))
    o = o.reshape((2,) + grad.shape)
    count, width = r1.shape
    inner = ups.shape[2]
    chunks = inner // CHUNK
    wide = pltpu.VMEM((count, width), BF16)
    deep = pltpu.VMEM((count, width), F32)
    results, sums = call(
        functools.partial(feed_back_kernel, mate),
        1,
        [full(gradm), full(r3), picked(attn, 7), picked(attn, 3)]
        + [(array, ANY) for array in (grad, r2, r1, o, u, ups, downs)]
        + [full(gains), full(shifts)],
        [
            new(F32, 2, count, width),
            new(BF16, 2, count, width),
            new(BF16, chunks, width, CHUNK),
            new(BF16, chunks, CHUNK, width),
            new(BF16, width, width),
            new(BF16, width, width),
            new(F32, 16, width),
        ],
        weight_scratch(width, chunks)
        + [
            pltpu.VMEM((chunks, count, CHUNK), F32),
            wide,
            wide,
            pltpu.VMEM((2, count, CHUNK), BF16),
            deep,
            deep,
            pltpu.VMEM((count, 1), F32),
            deep,
            deep,
            deep,
            pltpu.VMEM((2, count, width), BF16),
            pltpu.SemaphoreType.DMA((2, chunks)),
            pltpu.SemaphoreType.DMA((chunks,)),
            pltpu.SemaphoreType.DMA((4,)),
        ],
        "feed_back",
        cost(4 * count * width * (2 * width + 2 * inner), 36 << 20, 2 * count * inner),
        flows,
        plan,
        collective,
    )
    dr, do, dup, ddown, dwo, dwm, norms = results
    halves = lambda array: array.reshape((2, 2, count // 2, width))
    return (halves(dr), halves(do), dup, ddown.reshape(inner, width), dwo, dwm, norms), sums


def finish_kernel(counts, part_ref, src_mate_ref, tgt_mate_ref, norm_ref, *refs):
    sums, outs = refs[: -7], refs[-7:]
    gs_ref, gt_ref, attn_ref, up_ref, down_ref, gain_ref, shift_ref = outs
    long = pl.program_id(0) >= pl.num_programs(0) // 2
    for index, mate_ref, out_ref in ((0, src_mate_ref, gs_ref), (1, tgt_mate_ref, gt_ref)):

        @pl.when(long)
        def _():
            out_ref[...] = part_ref[index] + mate_ref[...].astype(F32)[None]

        @pl.when(jnp.logical_not(long))
        def _():
            out_ref[...] = part_ref[index]

    @pl.when(pl.program_id(0) == 0)
    def _():
        for ref, (kind, index, cols) in zip(sums, counts):
            share = ref.shape[-2]
            if kind == "attn":
                for number, place in enumerate(index):
                    attn_ref[place, :, cols[number]] = ref[number]
                continue
            tiles = up_ref.shape[2] // CHUNK
            index, place = index
            for number in range(ref.shape[0]):
                tile = tiles - 1 if kind == "both" else number
                if place is not None and number == tiles - 1:
                    attn_ref[place, :, :] = ref[number]
                elif kind == "up" or (kind == "both" and number == 0):
                    up_ref[index, :, tile * CHUNK : (tile + 1) * CHUNK] = ref[number]
                else:
                    down_ref[index, tile * share : (tile + 1) * share, :] = ref[number]
        share = gain_ref.shape[1]
        here = lax.axis_index("dp") * lax.axis_size("head") + lax.axis_index("head")
        width = norm_ref.shape[1]
        turned = pltpu.roll(norm_ref[...], (width - here * share) % width, axis=1)
        gain_ref[...] = turned[:5, :share]
        shift_ref[...] = turned[8:13, :share]


def finish(data, source_mate, target_mate, norms, named, share, inner, devices):
    _, _, rows, width = data.shape
    pieces = 1
    part = rows // pieces
    row = pl.BlockSpec((1, part, width), lambda step: (step // pieces, step % pieces, 0))
    mate = pl.BlockSpec((part, width), lambda step: (step % pieces, 0))
    sums = [array for array, *_ in named]
    counts = [tuple(rest) for _, *rest in named]
    outs = [
        (shaped((2, rows, width), F32), row),
        (shaped((2, rows, width), F32), row),
    ]
    for shape in ((12, share, width), (2, share, inner), (2, inner // devices, width), (5, share), (5, share)):
        outs.append((shaped(shape, F32), pl.BlockSpec(shape, lambda step, size=len(shape): (0,) * size)))
    return pl.pallas_call(
        functools.partial(finish_kernel, counts),
        grid=(2 * pieces,),
        out_shape=[shape for shape, _ in outs],
        in_specs=[pl.BlockSpec((2, 1, part, width), lambda step: (0, step // pieces, step % pieces, 0)), mate, mate, whole(norms)] + [whole(array) for array in sums],
        out_specs=[spec for _, spec in outs],
        compiler_params=params(),
        cost_estimate=cost(0, 11 << 20),
        name="finish",
    )(data, source_mate, target_mate, norms, *sums)


CROSS_FFN = [(0, 2), (1, 2)]
FEED_FFN = [(0, 3), (0, 6)]
FEED_CROSS = [(0, 3), (0, 6)]
LAST_FFN = [(0, 3), (1, 5), (2, 5), (3, 3), (3, 9)]
LAST_CROSS = [(0, 4), (2, 0), (3, 3)]
LAST_FFN1 = [(1, 4)]
LAST_NORMS = [(0, 2), (2, 0), (3, 1), (3, 7), (3, 8), (3, 9)]
LAST_OWN = [
    [(1, 4), (2, 2), (2, 5), (3, 3), (3, 6), (3, 8)],
    [(2, 4), (3, 2), (3, 4), (3, 7), (3, 8), (3, 9)],
    [(3, 4), (3, 6), (3, 7), (3, 8), (3, 9), (3, 10)],
]
OWN_PARTS = [(1, 0), (0, 0), (0, 3)]


def place_stages(plan, numbers, stages, start, spots):
    plan.setdefault(start, []).extend((number, None) for number in numbers)
    for index, stage in enumerate(stages):
        plan.setdefault(spots[min(index, len(spots) - 1)], []).extend((number, stage) for number in numbers)


def body(
    source,
    target,
    cotangent,
    short_lengths,
    long_lengths,
    attn,
    ups,
    downs,
    gains,
    shifts,
):
    _, rows, width = source.shape
    inner = ups.shape[2]
    devices = lax.axis_size("dp") * lax.axis_size("head")
    bits = devices.bit_length() - 1
    assert 2 * rows == LONG and rows % SHORT == 0 and devices == 1 << bits
    share = width // devices
    parts = (2,) * bits
    lengths = (short_lengths, long_lengths)
    orders = (
        tuple(range(bits)),
        (0, 2, 1) + tuple(range(3, bits)),
        (0,) + tuple(range(3, bits)) + (1, 2),
    )
    tiles = inner // width

    def square(array):
        return array.reshape(parts + (1, share, width)), None, 0, 1

    def ffn_flows(last, dup, ddown, extra=((), ())):
        up = dup.reshape((tiles,) + parts + (1, share, width))
        down = ddown.reshape(parts + (tiles, share, width))
        most = tiles - 1
        pieces = (
            [(up, index, 0, 1) for index in range(most)] + [square(array) for array in extra[0]],
            [(down, None, 0, most)] + [square(array) for array in extra[1]],
            [(up, most, 0, 1), (down, None, most, 1)],
        )
        return [Flow(order, 0, last, piece) for order, piece in zip(orders, pieces)]

    def attn_flows(last, *groups):
        pieces = [[square(array) for array in group] for group in groups]
        return [Flow(order, 0, last, piece) for order, piece in zip(orders, pieces)]

    def later(first, last, partial):
        return [
            Flow(order, first, last, [(part, None, 0, part.shape[-3])])
            for order, part in zip(orders, partial)
        ]

    self_saved, mates = attend((source, target), (False, True), False, attn, 0, lengths, 0)
    u, r1, r2, enc, r3, h3 = feed(self_saved[0], source, target, attn, ups, downs, gains, shifts)
    cross_saved, enc_mates = attend((h3, enc), (False,), True, attn, 8, lengths, 1)
    decoded, dr4, do_cross, dup1, ddown1, dw11, norms_a = turn(
        cross_saved[0], r3, cotangent, attn, ups, downs, gains, shifts
    )

    plan = {}
    place_stages(plan, (0, 1, 2), range(2), (0, 0), CROSS_FFN)
    (dh3, denc, denc_mate, dw8, dw9, dw10), ffn1 = attend_back(
        do_cross,
        cross_saved,
        enc_mates,
        dr4,
        (h3, enc),
        True,
        attn,
        8,
        ffn_flows(2, dup1, ddown1),
        plan,
        2,
    )

    plan = {}
    mate = Swap(0, (rows, width), denc_mate, kept=False)
    place_stages(plan, (5,), [0], (0, 0), [(0, 1)])
    place_stages(plan, (0, 1, 2), range(2, 4), (0, 0), FEED_FFN)
    place_stages(plan, (3, 4), range(2), (0, 0), FEED_CROSS)
    (dr, do, dup0, ddown0, dw3, dw7, norms_b), sums = feed_back(
        dh3,
        r3,
        denc,
        r2,
        r1,
        u,
        self_saved[0],
        attn,
        ups,
        downs,
        gains,
        shifts,
        mate,
        later(2, 4, ffn1) + attn_flows(2, [dw8, dw11], [dw9, dw10]) + [mate],
        plan,
        3,
    )
    ffn1, cross = sums[:3], sums[3:]

    plan = {}
    stages = range(bits)
    own = [
        Flow(order, 0, bits, [], (count, share, COLS // 2)) for count in (6, 3, 3) for order in orders[:2]
    ]
    swaps = [Swap(0, (rows, width)) for _ in range(2)]
    total = Total(bits, [norms_a, norms_b])
    for index in reversed(range(3)):
        spots = LAST_OWN[index]
        place_stages(plan, (6 + 2 * index, 7 + 2 * index), stages, spots[0], spots[1:])
    place_stages(plan, (0, 1, 2), stages, (0, 0), LAST_FFN)
    place_stages(plan, (3, 4), range(2, bits), (0, 0), LAST_CROSS)
    place_stages(plan, (14, 15, 16), range(4, bits), (0, 0), LAST_FFN1)
    place_stages(plan, (5,), stages, LAST_NORMS[0], LAST_NORMS[1:])
    place_stages(plan, (13,), [0], (1, 5), [(3, 9)])
    place_stages(plan, (12,), [0], (3, 5), [(3, 9)])
    (data,), sums = attend_back(
        do,
        self_saved,
        mates,
        dr,
        (source, target),
        False,
        attn,
        0,
        ffn_flows(bits, dup0, ddown0, ([dw3], [dw7]))
        + later(2, bits, cross)
        + [total]
        + own
        + swaps
        + later(4, bits, ffn1),
        plan,
        4,
        (own, swaps, total),
    )
    ffn0, cross = sums[:3], sums[3:5]
    norms, *own_sums, source_back, target_back = sums[5:-3]
    ffn1 = sums[-3:]

    everything = slice(None)
    named = [(array, "attn", places, (everything,) * 2) for array, places in zip(cross, ((8, 11), (9, 10)))]
    for index, sums in enumerate((ffn0, ffn1)):
        squares = (3, 7, None) if index == 0 else (None,) * 3
        named += [
            (array, kind, (index, place), None) for array, kind, place in zip(sums, ("up", "down", "both"), squares)
        ]
    for number, array in enumerate(own_sums):
        kind, first = OWN_PARTS[number // 2]
        places, cols = [], []
        for index in range(first, first + array.shape[0]):
            start = index // 3 * COLS + number % 2 * (COLS // 2)
            places.append(4 * kind + index % 3)
            cols.append(slice(start, start + COLS // 2))
        named.append((array, "attn", tuple(places), tuple(cols)))
    grad_source, grad_target, grad_attn, grad_up, grad_down, grad_gains, grad_shifts = finish(
        data, source_back, target_back, norms, named, share, inner, devices
    )
    return decoded, grad_source, grad_target, grad_attn, grad_up, grad_down, grad_gains, grad_shifts


def solution(mesh):
    rows = P(None, AXES, None)
    return jax.shard_map(
        body,
        mesh=mesh,
        in_specs=(rows, rows, rows, P(None, "dp"), P(None, "dp"), P(), P(), P(), P(), P()),
        out_specs=(rows, rows, rows, rows, rows, rows, P(None, AXES), P(None, AXES)),
        check_vma=False,
    )
```

```python
import functools
import math

import jax
import jax.numpy as jnp
from jax import lax
from jax.experimental import pallas as pl
from jax.experimental.pallas import tpu as pltpu
from jax.sharding import PartitionSpec as P

HEADS = 8
SHORT = 256
LONG = 1024

EPSILON = 1e-05
MASKED = -1e30
F32 = jnp.float32
BF16 = jnp.bfloat16
AXES = ("dp", "head")
COLS = 256
CHUNK = 512

NN = (((1,), (0,)), ((), ()))
NT = (((1,), (1,)), ((), ()))
TN = (((0,), (0,)), ((), ()))


def dot(left, right, dims=NN):
    return lax.dot_general(left, right, dims, preferred_element_type=F32)


def params():
    return pltpu.CompilerParams(vmem_limit_bytes=63 << 20)


def cost(flops, moved, powers=0):
    return pl.CostEstimate(flops=int(flops), bytes_accessed=int(moved), transcendentals=int(powers))


def whole(array):
    return pl.BlockSpec(array.shape, lambda *step: (0,) * array.ndim, pipeline_mode=pl.Buffered(1))


def shaped(shape, kind):
    return jax.ShapeDtypeStruct(shape, kind)


def lanes():
    return lax.broadcasted_iota(jnp.int32, (1, 128), 1)


def one_head(which, pair):
    keep = (lanes() < 64) if which == 0 else (lanes() >= 64)
    return jnp.where(keep, pair, jnp.zeros_like(pair))


def join_heads(first, second):
    return jnp.where(lanes() < 64, first, second)


MESH = pl.DeviceIdType.MESH


def partner(bit):
    head_bits = lax.axis_size("head").bit_length() - 1
    data, head = lax.axis_index("dp"), lax.axis_index("head")
    if bit < head_bits:
        step = 1 << bit
        mine = (head // step) % 2
        return mine, (data, head + (1 - 2 * mine) * step)
    step = 1 << (bit - head_bits)
    mine = (data // step) % 2
    return mine, (data + (1 - 2 * mine) * step, head)


class Flow:
    def __init__(self, order, first, last, pieces, block=None):
        self.order, self.first, self.last = order, first, last
        self.bits = order[first:last]
        self.local = block is not None
        self.arrays = []
        self.pieces = []
        total = 0
        for array, lead, start, count in pieces:
            known = [index for index, other in enumerate(self.arrays) if other is array]
            if not known:
                self.arrays.append(array)
            index = known[0] if known else len(self.arrays) - 1
            self.pieces.append((index, lead, start, total, count))
            total += count
        self.block = block or (total,) + pieces[0][0].shape[-2:]

    def shape(self, stage):
        return (2,) * (len(self.order) - stage) + self.block

    def out(self):
        done = self.last == len(self.order)
        return shaped(self.shape(self.last), F32 if done else BF16)

    def scratch(self):
        stages = range(self.first, self.last)
        count = len(self.pieces)
        dma = pltpu.SemaphoreType.DMA
        return (
            ([] if self.local else [pltpu.VMEM(self.shape(self.first + 1), BF16)])
            + [pltpu.VMEM(self.shape(stage + 1), BF16) for stage in stages]
            + [pltpu.VMEM(self.shape(stage + 1), BF16) for stage in stages[:-1]]
            + [dma((len(stages),)), dma((len(stages),))]
            + [dma((count,)) for _ in range(0 if self.local else 3)]
        )

    def bind(self, inputs, out, scratch):
        stages = range(self.first, self.last)
        self.in_refs, self.out_ref = inputs, out
        count = len(stages)
        skip = 0 if self.local else 1
        self.own = scratch[0]
        self.got = dict(zip(stages, scratch[skip : skip + count]))
        self.sum = dict(zip(stages[:-1], scratch[skip + count :]))
        if self.local:
            self.send, self.recv = scratch[-2:]
        else:
            self.send, self.recv, self.local_sem, self.piece_send, self.piece_recv = scratch[-5:]

    def where(self, stage, index):
        left = sorted(self.order[stage:])
        place = len(left) - 1 - left.index(self.order[stage])
        return (slice(None),) * place + (index,)

    def piece_copies(self):
        stage = self.first
        mine, device = partner(self.order[stage])
        left = len(self.order) - stage
        for number, (index, lead, start, total, count) in enumerate(self.pieces):
            prefix = () if lead is None else (lead,)
            target = (slice(None),) * (left - 1) + (slice(total, total + count),)
            ref = self.in_refs[index]

            def part(value):
                at = self.where(stage, value)
                at += (slice(None),) * (left - len(at)) + (slice(start, start + count),)
                return ref.at[prefix + at]

            yield pltpu.make_async_remote_copy(
                src_ref=part(1 - mine),
                dst_ref=self.got[stage].at[target],
                send_sem=self.piece_send.at[number],
                recv_sem=self.piece_recv.at[number],
                device_id=device,
                device_id_type=MESH,
            )
            yield pltpu.make_async_copy(
                part(mine),
                self.own.at[target],
                self.local_sem.at[number],
            )

    def stage_copy(self, stage):
        mine, device = partner(self.order[stage])
        source = self.source if stage == self.first else self.sum[stage - 1]
        return pltpu.make_async_remote_copy(
            src_ref=source.at[self.where(stage, 1 - mine)],
            dst_ref=self.got[stage],
            send_sem=self.send.at[stage - self.first],
            recv_sem=self.recv.at[stage - self.first],
            device_id=device,
            device_id_type=MESH,
        )

    def start(self):
        if self.local:
            self.stage_copy(self.first).start()
        else:
            for copy in self.piece_copies():
                copy.start()

    def step(self, stage):
        mine, _ = partner(self.order[stage])
        if stage > self.first:
            self.stage_copy(stage).wait()
            kept = self.sum[stage - 1].at[self.where(stage, mine)]
        elif self.local:
            self.stage_copy(stage).wait()
            kept = self.source.at[self.where(stage, mine)]
        else:
            for copy in self.piece_copies():
                copy.wait()
            kept = self.own
        got = self.got[stage]
        last = stage == self.last - 1
        target = self.out_ref if last else self.sum[stage]
        kind = F32 if stage == len(self.order) - 1 else BF16
        dims = min(2, len(self.order) - stage - 1)

        def add(index, carry):
            at = tuple((index >> bit) & 1 for bit in range(dims))
            target[at] = kept[at].astype(kind) + got[at].astype(kind)
            return carry

        if dims:
            lax.fori_loop(0, 1 << dims, add, 0)
        else:
            target[...] = kept[...].astype(kind) + got[...].astype(kind)
        if not last:
            self.stage_copy(stage + 1).start()


class Swap:
    def __init__(self, bit, shape, array=None, kept=True):
        self.bits = (bit,)
        self.wide = shape
        self.kept = kept
        self.arrays = [] if array is None else [array]

    def out(self):
        return shaped(self.wide, BF16) if self.kept else None

    def scratch(self):
        return [pltpu.VMEM(self.wide, BF16), pltpu.SemaphoreType.DMA, pltpu.SemaphoreType.DMA]

    def bind(self, inputs, out, scratch):
        self.source = inputs[0] if inputs else None
        self.out_ref = out
        self.got, self.send, self.recv = scratch

    def copy(self):
        return pltpu.make_async_remote_copy(
            src_ref=self.source,
            dst_ref=self.got,
            send_sem=self.send,
            recv_sem=self.recv,
            device_id=partner(self.bits[0])[1],
            device_id_type=MESH,
        )

    def start(self):
        self.copy().start()

    def step(self, stage):
        self.copy().wait()
        if self.kept:
            self.out_ref[...] = self.got[...]


class Total:
    def __init__(self, bits, arrays):
        self.bits = tuple(range(bits))
        self.arrays = []
        self.terms = arrays

    def out(self):
        return shaped(self.terms[0].shape, F32)

    def scratch(self):
        count = len(self.bits)
        whole_shape = (count,) + self.terms[0].shape
        dma = pltpu.SemaphoreType.DMA((count,))
        return [pltpu.VMEM(whole_shape, F32), pltpu.VMEM(whole_shape, F32), dma, dma]

    def bind(self, inputs, out, scratch):
        self.out_ref = out
        self.held, self.got, self.send, self.recv = scratch

    def copy(self, stage):
        return pltpu.make_async_remote_copy(
            src_ref=self.held.at[stage],
            dst_ref=self.got.at[stage],
            send_sem=self.send.at[stage],
            recv_sem=self.recv.at[stage],
            device_id=partner(stage)[1],
            device_id_type=MESH,
        )

    def start(self):
        self.held[0] = functools.reduce(lambda left, right: left + right, [ref[...] for ref in self.refs])
        self.copy(0).start()

    def step(self, stage):
        self.copy(stage).wait()
        total = self.held[stage] + self.got[stage]
        if stage == len(self.bits) - 1:
            self.out_ref[...] = total
        else:
            self.held[stage + 1] = total
            self.copy(stage + 1).start()


def greet(bits):
    ready = pltpu.get_barrier_semaphore()
    for bit in bits:
        _, device = partner(bit)
        pl.semaphore_signal(ready, inc=1, device_id=device, device_id_type=MESH)
    pl.semaphore_wait(ready, len(bits))


def call(kernel, steps, ins, outs, scratch, name, estimate, flows=(), plan=None, collective=None):
    extra_in = [array for flow in flows for array in flow.arrays]
    bits = sorted({bit for flow in flows for bit in flow.bits})
    counts = (len(ins), len(outs), len(scratch))

    def body(*refs):
        refs = list(refs)
        take = lambda count: [refs.pop(0) for _ in range(count)]
        main = take(counts[0])
        inputs = [take(len(flow.arrays)) for flow in flows]
        main += take(counts[1])
        results = [take(1)[0] if flow.out() else None for flow in flows]
        main += take(counts[2])
        for flow, given, result in zip(flows, inputs, results):
            flow.bind(given, result, take(len(flow.scratch())))

        def tick(slot, now=None):
            for (step, place), actions in (plan or {}).items():
                if place == slot:

                    here = pl.program_id(0) == step

                    @pl.when(here if now is None else here & now)
                    def _():
                        if (step, slot) == (0, 0):
                            greet(bits)
                        for number, stage in actions:
                            if stage is None:
                                flows[number].start()
                            else:
                                flows[number].step(stage)

        kernel(tick, *main)

    still = lambda shape: pl.BlockSpec(shape, lambda step: (0,) * len(shape))
    given_out = [flow.out() for flow in flows if flow.out()]
    remote = dict(collective_id=collective, has_side_effects=True) if flows else {}
    result = pl.pallas_call(
        body,
        grid=(steps,),
        out_shape=[shape for shape, _ in outs] + given_out,
        in_specs=[spec for _, spec in ins] + [pl.BlockSpec(memory_space=pl.ANY)] * len(extra_in),
        out_specs=[spec for _, spec in outs] + [still(shape.shape) for shape in given_out],
        scratch_shapes=list(scratch) + [shape for flow in flows for shape in flow.scratch()],
        compiler_params=pltpu.CompilerParams(vmem_limit_bytes=63 << 20, **remote),
        cost_estimate=estimate,
        name=name,
    )(*[array for array, _ in ins], *extra_in)
    return result[: len(outs)], result[len(outs) :]


def scores_bias(own_length, other_length, width, ahead):
    row = lax.broadcasted_iota(jnp.int32, (width, width), 0)
    column = lax.broadcasted_iota(jnp.int32, (width, width), 1)
    own = jnp.where((column < own_length) & (column <= row + ahead), 0.0, MASKED).astype(F32)
    if other_length is None:
        return own
    other = jnp.where(column < other_length, 0.0, MASKED).astype(F32)
    return jnp.concatenate([own, other], axis=1)


def attend_rows(bias, q_ref, k_ref, v_ref, e_ref, o_ref, inv_ref, rows, keys):
    count = bias.shape[1]
    ones = jnp.ones((count, 128), BF16)
    for pair in range(COLS // 128):
        cols = slice(pair * 128, pair * 128 + 128)
        queries = q_ref[rows, cols]
        key_pair = k_ref[keys, cols]
        value_ext = jnp.concatenate([v_ref[keys, cols], ones], axis=1)
        outs, inverses = [], []
        for which in range(2):
            scores = dot(one_head(which, queries), key_pair, NT) + bias
            highest = jnp.max(scores, axis=1, keepdims=True)
            powers = jnp.exp(scores - highest).astype(BF16)
            e_ref[pair * 2 + which, rows, :] = powers
            mixed = dot(powers, value_ext)
            inverse = 1.0 / mixed[:, 128:]
            outs.append(mixed[:, :128] * inverse)
            inverses.append(inverse)
        o_ref[rows, cols] = join_heads(*outs).astype(BF16)
        inv_ref[rows, cols] = join_heads(*inverses)


def attend_kernel(causal, cross, mates, tick, *refs):
    number = len(causal)
    ins = refs[: 2 if cross else number]
    (
        short_ref,
        long_ref,
        wq_ref,
        wk_ref,
        wv_ref,
        o_ref,
        inv_ref,
        q_ref,
        ks_ref,
        vs_ref,
        kl_ref,
        vl_ref,
        es_ref,
        el_ref,
        *scratch,
    ) = refs[len(ins) :]
    rows = ins[0].shape[1]
    scale = 0.125
    step = pl.program_id(0)
    which = step // 2
    place = lax.axis_index("head")
    half = place % 2
    for mate, ref in zip(mates, ins[-len(mates) :]):
        mate.source = ref.at[1]
    tick(0)
    if number == 1:
        xq_ref, xk_ref = ins[0], ins[-1]
    else:
        xq_ref = xk_ref = scratch[0]
        for index in range(number):

            @pl.when(step == 2 * index)
            def _():
                xq_ref[...] = ins[index][...]

    kind = sum([jnp.where(which == index, 1, 0) for index in range(number) if causal[index]], 0)
    ahead = (1 - kind) * LONG
    q_ref[0, 0] = (dot(xq_ref[0], wq_ref[0]) * scale).astype(BF16)
    ks_ref[0] = dot(xk_ref[0], wk_ref[0]).astype(BF16)
    vs_ref[0] = dot(xk_ref[0], wv_ref[0]).astype(BF16)
    slots = rows // SHORT
    for slot in range(slots):
        bias = scores_bias(short_ref[kind, place * slots + slot], None, SHORT, ahead)
        here = slice(slot * SHORT, (slot + 1) * SHORT)
        attend_rows(
            bias,
            q_ref.at[0, 0],
            ks_ref.at[0],
            vs_ref.at[0],
            es_ref.at[0],
            o_ref.at[0, 0],
            inv_ref.at[0, 0],
            here,
            here,
        )
    q_ref[0, 1] = (dot(xq_ref[1], wq_ref[0]) * scale).astype(BF16)
    kl_ref[0, :rows] = dot(xk_ref[1], wk_ref[0]).astype(BF16)
    vl_ref[0, :rows] = dot(xk_ref[1], wv_ref[0]).astype(BF16)
    tick(1)
    if number == 1:
        mate_ref = mates[0].got
    else:
        mate_ref = scratch[1]
        for index in range(number):

            @pl.when(step == 2 * index)
            def _():
                mate_ref[...] = mates[index].got[...]

    kl_ref[0, rows:] = dot(mate_ref[...], wk_ref[0]).astype(BF16)
    vl_ref[0, rows:] = dot(mate_ref[...], wv_ref[0]).astype(BF16)
    everything = slice(None)
    length = long_ref[kind, place // 2]
    other = (length - (1 - half) * rows) * (1 - kind * (1 - half))
    bias = scores_bias(length - half * rows, other, rows, ahead)
    attend_rows(
        bias,
        q_ref.at[0, 1],
        kl_ref.at[0],
        vl_ref.at[0],
        el_ref.at[0],
        o_ref.at[0, 1],
        inv_ref.at[0, 1],
        everything,
        everything,
    )


def attend(xs, causal, cross, weights, base, lengths, collective):
    _, rows, width = xs[0].shape
    number = len(causal)
    heads = width // 64
    place = lambda step: step // 2
    weight = lambda index: (
        weights,
        pl.BlockSpec((1, width, COLS), lambda step: (base + 4 * place(step) + index, 0, step % 2)),
    )
    both = lambda kind: (
        shaped((number, 2, rows, width), kind),
        pl.BlockSpec((1, 2, rows, COLS), lambda step: (place(step), 0, 0, step % 2)),
    )
    cols = lambda count: (
        shaped((number, count, width), BF16),
        pl.BlockSpec((1, count, COLS), lambda step: (place(step), 0, step % 2)),
    )
    powers = lambda count: (
        shaped((number, heads, rows, count), BF16),
        pl.BlockSpec((1, COLS // 64, rows, count), lambda step: (place(step), step % 2, 0, 0)),
    )
    flops = 2 * rows * width * width * 7 + 4 * rows * width * (SHORT + LONG)
    mates = [Swap(0, (rows, width)) for _ in range(number)]
    plan = {(0, 0): [(index, None) for index in range(number)]}
    for index in range(number):
        plan[2 * index, 1] = [(index, 0)]
    return call(
        functools.partial(attend_kernel, causal, cross, mates),
        2 * number,
        [(array, whole(array)) for array in xs]
        + [(array, pl.BlockSpec(memory_space=pltpu.SMEM)) for array in lengths]
        + [weight(0), weight(1), weight(2)],
        [both(BF16), both(F32), both(BF16), cols(rows), cols(rows), cols(LONG), cols(LONG)]
        + [powers(SHORT), powers(LONG)],
        [] if number == 1 else [pltpu.VMEM((2, rows, width), BF16), pltpu.VMEM((rows, width), BF16)],
        "attend",
        cost(flops * 2 * number, number * (22 << 20), number * heads * rows * (SHORT + LONG)),
        mates,
        plan,
        collective,
    )


def attend_back_rows(
    do_ref,
    o_ref,
    inv_ref,
    q_ref,
    k_ref,
    v_ref,
    e_ref,
    dq_ref,
    dk_ref,
    dv_ref,
    rows,
    keys,
    pair,
    scale,
):
    cols = pl.ds(pl.multiple_of(pair * 128, 128), 128)
    grad = do_ref[rows, cols].astype(F32) * inv_ref[rows, cols]
    product = grad * o_ref[rows, cols].astype(F32)
    grad_low = grad.astype(BF16)
    queries = q_ref[rows, cols]
    key_pair = k_ref[keys, cols]
    value_pair = v_ref[keys, cols]
    grad_turned = grad.T.astype(BF16)
    queries_turned = queries.astype(F32).T.astype(BF16)
    grad_q, grad_k, grad_v = [], [], []
    for which in range(2):
        inner = jnp.sum(one_head(which, product), axis=1, keepdims=True)
        grad_probs = dot(one_head(which, grad_low), value_pair, NT)
        powers = e_ref[pair * 2 + which, rows, :]
        grad_scores = (powers.astype(F32) * (grad_probs - inner)).astype(BF16)
        grad_q.append(dot(grad_scores, key_pair))
        head = slice(which * 64, which * 64 + 64)
        grad_v.append(dot(grad_turned[head], powers))
        grad_k.append(dot(queries_turned[head], grad_scores))
    dq_ref[rows, cols] = (join_heads(*grad_q) * scale).astype(BF16)
    dk_ref[keys, cols] = jnp.concatenate(grad_k, axis=0).T.astype(BF16)
    dv_ref[keys, cols] = jnp.concatenate(grad_v, axis=0).T.astype(BF16)


def attend_back_kernel(number, cross, own, swaps, total, after, tick, *refs):
    refs = list(refs)
    take = lambda count: [refs.pop(0) for _ in range(count)]
    if total:
        total.refs = take(len(total.terms))
    do_ref, o_ref, inv_ref, q_ref, ks_ref, vs_ref, kl_ref, vl_ref, es_ref, el_ref, resid_ref, *ins = take(
        11 + (2 if cross else number)
    )
    wq_ref, wk_ref, wv_ref = take(3)
    mates = take(number)
    dx_ref = take(1)[0]
    if cross:
        dy_ref, dmate_ref, dwq_ref, dwk_ref, dwv_ref = take(5)
    dqs, dks, dvs, dql, dkl, dvl, mate_sum, mate_low, resid_sem, *scratch = refs
    step = pl.program_id(0)
    first = step % 2 == 0
    if cross:
        xq_ref, xk_ref, mate_ref = ins[0], ins[1], mates[0]
        dy_ref = dy_ref.at[0]
    else:
        xq_ref = xk_ref = scratch[0]
        mate_ref = scratch[1]
        terms_ref = scratch[2]
        for place, flow in enumerate(own):
            kind, start = OWN_PARTS[place // 2]
            every = (slice(None),) * len(flow.order)
            flow.source = terms_ref.at[(kind, place % 2) + every + (slice(start, start + flow.block[0]),)]
        for index in range(number):
            swaps[index].source = mate_low.at[index]

            @pl.when(step == 2 * (number - 1 - index))
            def _():
                xq_ref[...] = ins[index][...]
                mate_ref[...] = mates[index][...]

        dy_ref = dx_ref.at[0]
    dx_ref = dx_ref.at[0]
    rows = xq_ref.shape[1]
    load = pltpu.make_async_copy(resid_ref.at[number - 1 - step // 2], dx_ref, resid_sem)

    @pl.when(first)
    def _():
        load.start()

    scale = 0.125
    everything = slice(None)
    tick(0)
    pairs = COLS // 128

    def long_pair(pair, carry):
        attend_back_rows(
            do_ref.at[0, 1],
            o_ref.at[0, 1],
            inv_ref.at[0, 1],
            q_ref.at[0, 1],
            kl_ref.at[0],
            vl_ref.at[0],
            el_ref.at[0],
            dql,
            dkl,
            dvl,
            everything,
            everything,
            pair,
            scale,
        )
        for index in range(pairs):
            tick(1 + index, pair == index)
        return carry

    def short_slot(slot, carry):
        here = pl.ds(pl.multiple_of(slot * SHORT, SHORT), SHORT)
        for pair in range(pairs):
            attend_back_rows(
                do_ref.at[0, 0],
                o_ref.at[0, 0],
                inv_ref.at[0, 0],
                q_ref.at[0, 0],
                ks_ref.at[0],
                vs_ref.at[0],
                es_ref.at[0],
                dqs,
                dks,
                dvs,
                here,
                here,
                pair,
                scale,
            )
        return carry

    lax.fori_loop(0, pairs, long_pair, 0)
    lax.fori_loop(0, rows // SHORT, short_slot, 0)
    tick(3)
    wq, wk, wv = wq_ref[0], wk_ref[0], wv_ref[0]
    front = slice(0, rows)
    other = slice(rows, 2 * rows)
    dwq = dot(xq_ref[0], dqs[...], TN) + dot(xq_ref[1], dql[...], TN)
    short, long, mate = xk_ref[0], xk_ref[1], mate_ref[...]
    dwk = dot(short, dks[...], TN) + dot(long, dkl[front], TN) + dot(mate, dkl[other], TN)
    dwv = dot(short, dvs[...], TN) + dot(long, dvl[front], TN) + dot(mate, dvl[other], TN)
    if cross:
        dwq_ref[...] = dwq.astype(BF16)
        dwk_ref[...] = dwk.astype(BF16)
        dwv_ref[...] = dwv.astype(BF16)
    else:
        flow = own[0]
        _, share, columns = flow.block
        for index, total_w in enumerate((dwq, dwk, dwv)):
            low = total_w.astype(BF16)
            for device in range(low.shape[0] // share):
                at = tuple((device >> bit) & 1 for bit in reversed(range(len(flow.order))))
                for color in range(2):
                    terms_ref[(1 - step // 2, color) + at + (step % 2 * 3 + index,)] = low[
                        device * share : (device + 1) * share, color * columns : (color + 1) * columns
                    ]

    tick(4)

    @pl.when(first)
    def _():
        load.wait()
        if cross:
            dy_ref[...] = jnp.zeros_like(dy_ref)
        mate_sum[...] = jnp.zeros_like(mate_sum)

    mate_sum[...] += dot(dkl[other], wk, NT) + dot(dvl[other], wv, NT)
    if cross:

        @pl.when(jnp.logical_not(first))
        def _():
            dmate_ref[...] = mate_sum[...].astype(BF16)

    else:
        for index in range(number):

            @pl.when(step == 2 * (number - 1 - index) + 1)
            def _():
                mate_low[index] = mate_sum[...].astype(BF16)

    tick(5)
    dx_ref[0] += dot(dqs[...], wq, NT)
    dx_ref[1] += dot(dql[...], wq, NT)
    dy_ref[0] += dot(dks[...], wk, NT) + dot(dvs[...], wv, NT)
    dy_ref[1] += dot(dkl[front], wk, NT) + dot(dvl[front], wv, NT)
    for slot in range(6, 6 + after):
        tick(slot)


def attend_back(grad, saved, mates, resid, xs, cross, weights, base, flows, plan, collective, last=None):
    _, rows, width = xs[0].shape
    number = 1 if cross else len(xs)
    place = lambda step: number - 1 - step // 2
    weight = lambda index: (
        weights,
        pl.BlockSpec((1, width, COLS), lambda step: (base + 4 * place(step) + index, 0, step % 2)),
    )
    both = pl.BlockSpec((1, 2, rows, COLS), lambda step: (place(step), 0, 0, step % 2))
    cols = lambda count: pl.BlockSpec((1, count, COLS), lambda step: (place(step), 0, step % 2))
    powers = lambda count: pl.BlockSpec((1, COLS // 64, rows, count), lambda step: (place(step), step % 2, 0, 0))
    deep = pl.BlockSpec((1, 2, rows, width), lambda step: (place(step), 0, 0, 0))
    flops = 2 * rows * width * width * 14 + 8 * rows * width * (SHORT + LONG)
    specs = [both] * 4 + [cols(rows)] * 2 + [cols(LONG)] * 2 + [powers(SHORT), powers(LONG)]
    o, inverse, *rest = saved
    own, swaps, total = last or ((), (), None)
    data = (shaped((number, 2, rows, width), F32), deep)
    outs = [data]
    scratch = (
        [pltpu.VMEM((rows, COLS), BF16)] * 4
        + [pltpu.VMEM((LONG, COLS), BF16)] * 2
        + [pltpu.VMEM((rows, width), F32), pltpu.VMEM((number, rows, width), BF16)]
        + [pltpu.SemaphoreType.DMA]
    )
    if cross:
        outs += [data, (shaped((rows, width), BF16), pl.BlockSpec((rows, width), lambda step: (0, 0)))]
        outs += [(shaped((width, width), BF16), pl.BlockSpec((width, COLS), lambda step: (0, step)))] * 3
    else:
        scratch += [pltpu.VMEM((2, rows, width), BF16), pltpu.VMEM((rows, width), BF16)]
        _, share, columns = own[0].block
        scratch += [pltpu.VMEM((number, 2) + own[0].shape(0)[:-3] + (6, share, columns), BF16)]
    after = 1 + max([spot for _, spot in plan] + [5]) - 6
    norms = total.terms if total else []
    return call(
        functools.partial(attend_back_kernel, number, cross, own, swaps, total, after),
        2 * number,
        [(array, whole(array)) for array in norms]
        + list(zip((grad, o, inverse, *rest), specs))
        + [(resid, pl.BlockSpec(memory_space=pl.ANY))]
        + [(array, whole(array)) for array in xs]
        + [weight(0), weight(1), weight(2)]
        + [(array, whole(array)) for array in mates],
        outs,
        scratch,
        "attend_back",
        cost(flops * 2 * number, number * (28 << 20)),
        flows,
        plan,
        collective,
    )


BLOCK = 512
WIDE = 1024
ANY = pl.BlockSpec(memory_space=pl.ANY)


def norm_parts(resid):
    average = jnp.mean(resid, axis=-1, keepdims=True)
    centered = resid - average
    variance = jnp.mean(centered * centered, axis=-1, keepdims=True)
    spread = lax.rsqrt(variance + EPSILON)
    return centered * spread, spread


def norm_back(normal, spread, gain, grad):
    scaled = grad * gain
    first = jnp.mean(scaled, axis=-1, keepdims=True)
    second = jnp.mean(scaled * normal, axis=-1, keepdims=True)
    return (scaled - first - normal * second) * spread


def add_norm_grads(ref, place, grad, normal):
    ref[place : place + 1, :] += jnp.sum(grad * normal, axis=0, keepdims=True)
    ref[8 + place : 9 + place, :] += jnp.sum(grad, axis=0, keepdims=True)


def logistic(value):
    return 1.0 / (1.0 + jnp.exp(-value))


def each_block(count, work, size=BLOCK):
    def step(index, carry):
        work(pl.ds(pl.multiple_of(index * size, size), size))
        return carry

    lax.fori_loop(0, count // size, step, 0)


def each_chunk(count, work):
    def step(index, carry):
        work(index)
        return carry

    lax.fori_loop(0, count, step, 0)


class Loads:
    def __init__(self, pairs, sems):
        self.copies = [
            pltpu.make_async_copy(source, target, sems.at[index])
            for index, (source, target) in enumerate(pairs)
        ]

    def start(self):
        for copy in self.copies:
            copy.start()

    def wait(self, *places):
        for place in places:
            self.copies[place].wait()


def chunk_loads(up_ref, down_ref, up_s, down_s, sems):
    def copies(chunk):
        part = pl.ds(pl.multiple_of(chunk * CHUNK, CHUNK), CHUNK)
        return (
            pltpu.make_async_copy(up_ref.at[:, part], up_s.at[chunk], sems.at[0, chunk]),
            pltpu.make_async_copy(down_ref.at[part], down_s.at[chunk], sems.at[1, chunk]),
        )

    return copies


def chunk_writes(dup_ref, ddown_ref, dup_s, ddown_s, sems):
    def copies(chunk):
        return (
            pltpu.make_async_copy(dup_s.at[chunk], dup_ref.at[chunk], sems.at[0, chunk]),
            pltpu.make_async_copy(ddown_s.at[chunk], ddown_ref.at[chunk], sems.at[1, chunk]),
        )

    def write(chunk, dup, ddown):
        dup_s[chunk] = dup.astype(BF16)
        ddown_s[chunk] = ddown.astype(BF16)
        for copy in copies(chunk):
            copy.start()

    def wait():
        for chunk in range(dup_s.shape[0]):
            for copy in copies(chunk):
                copy.wait()

    return write, wait


def feed_chunks(copies, low_s, total_s, up_s, down_s, u_s, a_s, out=None):
    count = low_s.shape[0]

    def chunk_work(chunk):
        for copy in copies(chunk):
            copy.wait()

        def block_work(rows):
            upward = dot(low_s[rows, :], up_s[chunk])
            u_s[chunk, rows, :] = upward
            active = (upward * logistic(upward)).astype(BF16)
            if a_s is not None:
                a_s[chunk, rows, :] = active
            total_s[rows, :] += dot(active, down_s[chunk])

        each_block(count, block_work, WIDE)
        if out is not None:
            out(chunk)

    each_chunk(up_s.shape[0], chunk_work)


def feed_back_chunks(tick, wait, low_s, hidden_s, total_s, up_s, down_s, u_s, a_s, du_s, write):
    count = low_s.shape[0]
    chunks = up_s.shape[0]

    def chunk_work(chunk):
        wait(chunk)
        store = a_s is None
        active_ref = du_s.at[1] if store else a_s.at[chunk]

        def block_work(rows):
            upward = u_s[chunk, rows, :]
            gate = logistic(upward)
            if store:
                active_ref[rows, :] = (upward * gate).astype(BF16)
            grad_active = dot(low_s[rows, :], down_s[chunk], NT)
            grad_up = (grad_active * gate * (1.0 + upward * (1.0 - gate))).astype(BF16)
            du_s[0, rows, :] = grad_up
            total_s[rows, :] += dot(grad_up, up_s[chunk], NT)

        each_block(count, block_work, WIDE)
        write(chunk, dot(hidden_s[...], du_s[0], TN), dot(active_ref[...], low_s[...], TN))
        for index in range(chunks):
            tick(2 + index, chunk == index)

    each_chunk(chunks, chunk_work)


def feed_kernel(
    tick,
    os_ref,
    x_ref,
    z_ref,
    wm_ref,
    wo_ref,
    up_ref,
    down_ref,
    gain_ref,
    shift_ref,
    u_ref,
    r1_ref,
    r2_ref,
    enc_ref,
    r3_ref,
    h3_ref,
    *scratch,
):
    up_s, down_s, u_s, low_s, sems, out_sems = scratch
    copies = chunk_loads(up_ref.at[0], down_ref.at[0], up_s, down_s, sems)
    chunks = up_s.shape[0]
    for chunk in range(chunks):
        for copy in copies(chunk):
            copy.start()
    count = low_s.shape[0]

    def first(rows):
        resid = x_ref[rows, :].astype(F32) + dot(os_ref[0, rows, :], wo_ref[0])
        r1_ref[rows, :] = resid
        normal, _ = norm_parts(resid)
        hidden = normal * gain_ref[0:1] + shift_ref[0:1]
        r2_ref[rows, :] = hidden
        low_s[rows, :] = hidden.astype(BF16)
        resid = z_ref[rows, :].astype(F32) + dot(os_ref[1, rows, :], wm_ref[0])
        r3_ref[rows, :] = resid
        normal, _ = norm_parts(resid)
        h3_ref[rows, :] = (normal * gain_ref[2:3] + shift_ref[2:3]).astype(BF16)

    each_block(count, first)
    keep = lambda chunk: pltpu.make_async_copy(u_s.at[chunk], u_ref.at[chunk], out_sems.at[chunk])
    feed_chunks(copies, low_s, r2_ref, up_s, down_s, u_s, None, lambda chunk: keep(chunk).start())

    def last(rows):
        normal, _ = norm_parts(r2_ref[rows, :])
        enc_ref[rows, :] = (normal * gain_ref[1:2] + shift_ref[1:2]).astype(BF16)

    each_block(count, last)
    for chunk in range(chunks):
        keep(chunk).wait()


def picked(array, index):
    return array, pl.BlockSpec((1,) + array.shape[1:], lambda step: (index, 0, 0))


def flat(array):
    return array.reshape((-1,) + array.shape[2:])


def full(array):
    return array, whole(array)


def new(kind, *shape):
    return shaped(shape, kind), pl.BlockSpec(shape, lambda step: (0,) * len(shape))


def weight_scratch(width, chunks):
    return [
        pltpu.VMEM((chunks, width, CHUNK), BF16),
        pltpu.VMEM((chunks, CHUNK, width), BF16),
    ]


def feed(o, x, z, attn, ups, downs, gains, shifts):
    shape = x.shape
    o, x, z = o.reshape((2, -1, shape[-1])), flat(x), flat(z)
    count, width = x.shape
    inner = ups.shape[2]
    chunks = inner // CHUNK
    results, _ = call(
        feed_kernel,
        1,
        [full(o), full(x), full(z), picked(attn, 7), picked(attn, 3)]
        + [(ups, ANY), (downs, ANY), full(gains), full(shifts)],
        [
            (shaped((chunks, count, CHUNK), F32), ANY),
            new(F32, count, width),
            new(F32, count, width),
            new(BF16, count, width),
            new(F32, count, width),
            new(BF16, count, width),
        ],
        weight_scratch(width, chunks)
        + [
            pltpu.VMEM((chunks, count, CHUNK), F32),
            pltpu.VMEM((count, width), BF16),
            pltpu.SemaphoreType.DMA((2, chunks)),
            pltpu.SemaphoreType.DMA((chunks,)),
        ],
        "feed",
        cost(2 * count * width * (2 * width + 2 * inner), 28 << 20, 2 * count * inner),
    )
    u, r1, r2, enc, r3, h3 = results
    return u, r1, r2, enc.reshape(shape), r3, h3.reshape(shape)


def turn_kernel(
    tick,
    o_ref,
    r3_ref,
    wo_ref,
    cot_ref,
    up_ref,
    down_ref,
    gain_ref,
    shift_ref,
    out_ref,
    dr_ref,
    do_ref,
    dup_ref,
    ddown_ref,
    dwo_ref,
    norm_ref,
    *scratch,
):
    up_s, down_s, u_s, a_s, low_s, hidden_s, du_s, cot_s, total_s, normal_s, spread_s, sems, cot_sem, *outs = scratch
    dup_s, ddown_s, out_sems = outs
    copies = chunk_loads(up_ref.at[1], down_ref.at[1], up_s, down_s, sems)
    chunks = up_s.shape[0]
    for chunk in range(chunks):
        for copy in copies(chunk):
            copy.start()
    load = pltpu.make_async_copy(cot_ref, cot_s, cot_sem)
    load.start()
    count = low_s.shape[0]
    norm_ref[...] = jnp.zeros_like(norm_ref)

    def first(rows):
        normal3, _ = norm_parts(r3_ref[rows, :])
        resid4 = normal3 * gain_ref[2:3] + shift_ref[2:3] + dot(o_ref[rows, :], wo_ref[0])
        normal4, spread4 = norm_parts(resid4)
        hidden = normal4 * gain_ref[3:4] + shift_ref[3:4]
        normal_s[rows, :] = normal4
        spread_s[rows, :] = spread4
        total_s[rows, :] = hidden
        hidden_s[rows, :] = hidden.astype(BF16)

    each_block(count, first)
    feed_chunks(copies, hidden_s, total_s, up_s, down_s, u_s, a_s)
    load.wait()

    def top(rows):
        normal5, spread5 = norm_parts(total_s[rows, :])
        out_ref[rows, :] = (normal5 * gain_ref[4:5] + shift_ref[4:5]).astype(BF16)
        grad = cot_s[rows, :].astype(F32)
        add_norm_grads(norm_ref, 4, grad, normal5)
        grad = norm_back(normal5, spread5, gain_ref[4:5], grad)
        total_s[rows, :] = grad
        low_s[rows, :] = grad.astype(BF16)

    each_block(count, top)

    write, finish_writes = chunk_writes(dup_ref, ddown_ref, dup_s, ddown_s, out_sems)

    feed_back_chunks(
        tick, lambda chunk: None, low_s, hidden_s, total_s, up_s, down_s, u_s, a_s, du_s, write
    )

    def bottom(rows):
        grad = total_s[rows, :]
        normal4 = normal_s[rows, :]
        add_norm_grads(norm_ref, 3, grad, normal4)
        grad = norm_back(normal4, spread_s[rows, :], gain_ref[3:4], grad)
        dr_ref[rows, :] = grad
        low = grad.astype(BF16)
        low_s[rows, :] = low
        do_ref[rows, :] = dot(low, wo_ref[0], NT).astype(BF16)

    each_block(count, bottom)
    dwo_ref[...] = dot(o_ref[...], low_s[...], TN).astype(BF16)
    finish_writes()


def turn(o, r3, cot, attn, ups, downs, gains, shifts):
    rows = cot.shape[1]
    o, cot = flat(flat(o)), flat(cot)
    count, width = r3.shape
    inner = ups.shape[2]
    chunks = inner // CHUNK
    wide = pltpu.VMEM((count, width), BF16)
    results, _ = call(
        turn_kernel,
        1,
        [full(o), full(r3), picked(attn, 11), (cot, ANY), (ups, ANY), (downs, ANY), full(gains), full(shifts)],
        [
            new(BF16, count, width),
            new(F32, count, width),
            new(BF16, count, width),
            (shaped((chunks, width, CHUNK), BF16), ANY),
            (shaped((chunks, CHUNK, width), BF16), ANY),
            new(BF16, width, width),
            new(F32, 16, width),
        ],
        weight_scratch(width, chunks)
        + [
            pltpu.VMEM((chunks, count, CHUNK), F32),
            pltpu.VMEM((chunks, count, CHUNK), BF16),
            wide,
            wide,
            pltpu.VMEM((1, count, CHUNK), BF16),
            wide,
            pltpu.VMEM((count, width), F32),
            pltpu.VMEM((count, width), F32),
            pltpu.VMEM((count, 1), F32),
            pltpu.SemaphoreType.DMA((2, chunks)),
            pltpu.SemaphoreType.DMA,
        ]
        + weight_scratch(width, chunks)
        + [pltpu.SemaphoreType.DMA((2, chunks))],
        "turn",
        cost(6 * count * width * (width + 2 * inner), 20 << 20, 4 * count * inner),
    )
    out, dr, do, dup, ddown, dwo, norms = results
    pair = lambda array: array.reshape((2, rows) + array.shape[1:])
    return pair(out), pair(dr)[None], pair(do)[None], dup, ddown.reshape(inner, width), dwo, norms


def feed_back_kernel(
    mate,
    tick,
    gradm_ref,
    r3_ref,
    wm_ref,
    wo_ref,
    grad_ref,
    r2_ref,
    r1_ref,
    os_ref,
    u_ref,
    up_ref,
    down_ref,
    gain_ref,
    shift_ref,
    dr_ref,
    do_ref,
    dup_ref,
    ddown_ref,
    dwo_ref,
    dwm_ref,
    norm_ref,
    *scratch,
):
    (
        up_s,
        down_s,
        u_s,
        low_s,
        hidden_s,
        du_s,
        total_s,
        normal_s,
        spread_s,
        grad_s,
        r2_s,
        r1_s,
        os_s,
        sems,
        u_sems,
        in_sems,
        dup_s,
        ddown_s,
        out_sems,
    ) = scratch
    copies = chunk_loads(up_ref.at[0], down_ref.at[0], up_s, down_s, sems)
    chunks = up_s.shape[0]
    keep = lambda chunk: pltpu.make_async_copy(u_ref.at[chunk], u_s.at[chunk], u_sems.at[chunk])
    late = Loads([(os_ref, os_s), (grad_ref, grad_s), (r2_ref, r2_s), (r1_ref, r1_s)], in_sems)
    late.start()
    for chunk in range(chunks):
        keep(chunk).start()
        for copy in copies(chunk):
            copy.start()
    tick(0)
    count = low_s.shape[0]
    half = count // 2
    norm_ref[...] = jnp.zeros_like(norm_ref)

    def middle(rows):
        grad = gradm_ref[rows, :]
        normal, spread = norm_parts(r3_ref[rows, :])
        add_norm_grads(norm_ref, 2, grad, normal)
        grad = norm_back(normal, spread, gain_ref[2:3], grad)
        dr_ref[1, rows, :] = grad
        low = grad.astype(BF16)
        low_s[rows, :] = low
        do_ref[1, rows, :] = dot(low, wm_ref[0], NT).astype(BF16)

    each_block(count, middle)
    late.wait(0)
    dwm_ref[...] = dot(os_s[1], low_s[...], TN).astype(BF16)
    tick(1)

    def first(rows, grad):
        normal2, spread2 = norm_parts(r2_s[rows, :])
        add_norm_grads(norm_ref, 1, grad, normal2)
        grad = norm_back(normal2, spread2, gain_ref[1:2], grad)
        total_s[rows, :] = grad
        low_s[rows, :] = grad.astype(BF16)
        normal1, spread1 = norm_parts(r1_s[rows, :])
        normal_s[rows, :] = normal1
        spread_s[rows, :] = spread1
        hidden_s[rows, :] = (normal1 * gain_ref[0:1] + shift_ref[0:1]).astype(BF16)

    late.wait(1, 2, 3)
    each_block(half, lambda rows: first(rows, grad_s[rows, :]))

    def long(index, carry):
        start = pl.multiple_of(index * BLOCK, BLOCK)
        rows = pl.ds(pl.multiple_of(start + half, BLOCK), BLOCK)
        first(rows, grad_s[rows, :] + mate.got[pl.ds(start, BLOCK), :].astype(F32))
        return carry

    lax.fori_loop(0, half // BLOCK, long, 0)

    write, finish_writes = chunk_writes(dup_ref, ddown_ref, dup_s, ddown_s, out_sems)

    def wait(chunk):
        keep(chunk).wait()
        for copy in copies(chunk):
            copy.wait()

    feed_back_chunks(tick, wait, low_s, hidden_s, total_s, up_s, down_s, u_s, None, du_s, write)

    def bottom(rows):
        grad = total_s[rows, :]
        normal1 = normal_s[rows, :]
        add_norm_grads(norm_ref, 0, grad, normal1)
        grad = norm_back(normal1, spread_s[rows, :], gain_ref[0:1], grad)
        dr_ref[0, rows, :] = grad
        low = grad.astype(BF16)
        low_s[rows, :] = low
        do_ref[0, rows, :] = dot(low, wo_ref[0], NT).astype(BF16)

    each_block(count, bottom)
    dwo_ref[...] = dot(os_s[0], low_s[...], TN).astype(BF16)
    finish_writes()
    tick(2 + chunks)


def feed_back(gradm, r3, grad, r2, r1, u, o, attn, ups, downs, gains, shifts, mate, flows, plan, collective):
    gradm, grad = flat(flat(gradm)), flat(flat(grad))
    o = o.reshape((2,) + grad.shape)
    count, width = r1.shape
    inner = ups.shape[2]
    chunks = inner // CHUNK
    wide = pltpu.VMEM((count, width), BF16)
    deep = pltpu.VMEM((count, width), F32)
    results, sums = call(
        functools.partial(feed_back_kernel, mate),
        1,
        [full(gradm), full(r3), picked(attn, 7), picked(attn, 3)]
        + [(array, ANY) for array in (grad, r2, r1, o, u, ups, downs)]
        + [full(gains), full(shifts)],
        [
            new(F32, 2, count, width),
            new(BF16, 2, count, width),
            (shaped((chunks, width, CHUNK), BF16), ANY),
            (shaped((chunks, CHUNK, width), BF16), ANY),
            new(BF16, width, width),
            new(BF16, width, width),
            new(F32, 16, width),
        ],
        weight_scratch(width, chunks)
        + [
            pltpu.VMEM((chunks, count, CHUNK), F32),
            wide,
            wide,
            pltpu.VMEM((2, count, CHUNK), BF16),
            deep,
            deep,
            pltpu.VMEM((count, 1), F32),
            deep,
            deep,
            deep,
            pltpu.VMEM((2, count, width), BF16),
            pltpu.SemaphoreType.DMA((2, chunks)),
            pltpu.SemaphoreType.DMA((chunks,)),
            pltpu.SemaphoreType.DMA((4,)),
        ]
        + weight_scratch(width, chunks)
        + [pltpu.SemaphoreType.DMA((2, chunks))],
        "feed_back",
        cost(4 * count * width * (2 * width + 2 * inner), 36 << 20, 2 * count * inner),
        flows,
        plan,
        collective,
    )
    dr, do, dup, ddown, dwo, dwm, norms = results
    halves = lambda array: array.reshape((2, 2, count // 2, width))
    return (halves(dr), halves(do), dup, ddown.reshape(inner, width), dwo, dwm, norms), sums


def finish_kernel(counts, part_ref, src_mate_ref, tgt_mate_ref, norm_ref, *refs):
    sums, outs = refs[: -7], refs[-7:]
    gs_ref, gt_ref, attn_ref, up_ref, down_ref, gain_ref, shift_ref = outs
    long = pl.program_id(0) >= pl.num_programs(0) // 2
    for index, mate_ref, out_ref in ((0, src_mate_ref, gs_ref), (1, tgt_mate_ref, gt_ref)):

        @pl.when(long)
        def _():
            out_ref[...] = part_ref[index] + mate_ref[...].astype(F32)[None]

        @pl.when(jnp.logical_not(long))
        def _():
            out_ref[...] = part_ref[index]

    @pl.when(pl.program_id(0) == 0)
    def _():
        for ref, (kind, index, cols) in zip(sums, counts):
            share = ref.shape[-2]
            if kind == "attn":
                for number, place in enumerate(index):
                    attn_ref[place, :, cols[number]] = ref[number]
                continue
            tiles = up_ref.shape[2] // CHUNK
            index, place = index
            for number in range(ref.shape[0]):
                tile = tiles - 1 if kind == "both" else number
                if place is not None and number == tiles - 1:
                    attn_ref[place, :, :] = ref[number]
                elif kind == "up" or (kind == "both" and number == 0):
                    up_ref[index, :, tile * CHUNK : (tile + 1) * CHUNK] = ref[number]
                else:
                    down_ref[index, tile * share : (tile + 1) * share, :] = ref[number]
        share = gain_ref.shape[1]
        here = lax.axis_index("dp") * lax.axis_size("head") + lax.axis_index("head")
        width = norm_ref.shape[1]
        turned = pltpu.roll(norm_ref[...], (width - here * share) % width, axis=1)
        gain_ref[...] = turned[:5, :share]
        shift_ref[...] = turned[8:13, :share]


def finish(data, source_mate, target_mate, norms, named, share, inner, devices):
    _, _, rows, width = data.shape
    pieces = 1
    part = rows // pieces
    row = pl.BlockSpec((1, part, width), lambda step: (step // pieces, step % pieces, 0))
    mate = pl.BlockSpec((part, width), lambda step: (step % pieces, 0))
    sums = [array for array, *_ in named]
    counts = [tuple(rest) for _, *rest in named]
    outs = [
        (shaped((2, rows, width), F32), row),
        (shaped((2, rows, width), F32), row),
    ]
    for shape in ((12, share, width), (2, share, inner), (2, inner // devices, width), (5, share), (5, share)):
        outs.append((shaped(shape, F32), pl.BlockSpec(shape, lambda step, size=len(shape): (0,) * size)))
    return pl.pallas_call(
        functools.partial(finish_kernel, counts),
        grid=(2 * pieces,),
        out_shape=[shape for shape, _ in outs],
        in_specs=[pl.BlockSpec((2, 1, part, width), lambda step: (0, step // pieces, step % pieces, 0)), mate, mate, whole(norms)] + [whole(array) for array in sums],
        out_specs=[spec for _, spec in outs],
        compiler_params=params(),
        cost_estimate=cost(0, 11 << 20),
        name="finish",
    )(data, source_mate, target_mate, norms, *sums)


CROSS_FFN = [(0, 2), (1, 2)]
FEED_FFN = [(0, 3), (0, 6)]
FEED_CROSS = [(0, 3), (0, 6)]
LAST_FFN = [(0, 3), (1, 5), (2, 5), (3, 3), (3, 9)]
LAST_CROSS = [(0, 4), (2, 0), (3, 3)]
LAST_FFN1 = [(1, 4)]
LAST_NORMS = [(0, 2), (2, 0), (3, 1), (3, 7), (3, 8), (3, 9)]
LAST_OWN = [
    [(1, 4), (2, 2), (2, 5), (3, 3), (3, 6), (3, 8)],
    [(2, 4), (3, 2), (3, 4), (3, 7), (3, 8), (3, 9)],
    [(3, 4), (3, 6), (3, 7), (3, 8), (3, 9), (3, 10)],
]
OWN_PARTS = [(1, 0), (0, 0), (0, 3)]


def place_stages(plan, numbers, stages, start, spots):
    plan.setdefault(start, []).extend((number, None) for number in numbers)
    for index, stage in enumerate(stages):
        plan.setdefault(spots[min(index, len(spots) - 1)], []).extend((number, stage) for number in numbers)


def body(
    source,
    target,
    cotangent,
    short_lengths,
    long_lengths,
    attn,
    ups,
    downs,
    gains,
    shifts,
):
    _, rows, width = source.shape
    inner = ups.shape[2]
    devices = lax.axis_size("dp") * lax.axis_size("head")
    bits = devices.bit_length() - 1
    assert 2 * rows == LONG and rows % SHORT == 0 and devices == 1 << bits
    share = width // devices
    parts = (2,) * bits
    lengths = (short_lengths, long_lengths)
    orders = (
        tuple(range(bits)),
        (0, 2, 1) + tuple(range(3, bits)),
        (0,) + tuple(range(3, bits)) + (1, 2),
    )
    tiles = inner // width

    def square(array):
        return array.reshape(parts + (1, share, width)), None, 0, 1

    def ffn_flows(last, dup, ddown, extra=((), ())):
        up = dup.reshape((tiles,) + parts + (1, share, width))
        down = ddown.reshape(parts + (tiles, share, width))
        most = tiles - 1
        pieces = (
            [(up, index, 0, 1) for index in range(most)] + [square(array) for array in extra[0]],
            [(down, None, 0, most)] + [square(array) for array in extra[1]],
            [(up, most, 0, 1), (down, None, most, 1)],
        )
        return [Flow(order, 0, last, piece) for order, piece in zip(orders, pieces)]

    def attn_flows(last, *groups):
        pieces = [[square(array) for array in group] for group in groups]
        return [Flow(order, 0, last, piece) for order, piece in zip(orders, pieces)]

    def later(first, last, partial):
        return [
            Flow(order, first, last, [(part, None, 0, part.shape[-3])])
            for order, part in zip(orders, partial)
        ]

    self_saved, mates = attend((source, target), (False, True), False, attn, 0, lengths, 0)
    u, r1, r2, enc, r3, h3 = feed(self_saved[0], source, target, attn, ups, downs, gains, shifts)
    cross_saved, enc_mates = attend((h3, enc), (False,), True, attn, 8, lengths, 1)
    decoded, dr4, do_cross, dup1, ddown1, dw11, norms_a = turn(
        cross_saved[0], r3, cotangent, attn, ups, downs, gains, shifts
    )

    plan = {}
    place_stages(plan, (0, 1, 2), range(2), (0, 0), CROSS_FFN)
    (dh3, denc, denc_mate, dw8, dw9, dw10), ffn1 = attend_back(
        do_cross,
        cross_saved,
        enc_mates,
        dr4,
        (h3, enc),
        True,
        attn,
        8,
        ffn_flows(2, dup1, ddown1),
        plan,
        2,
    )

    plan = {}
    mate = Swap(0, (rows, width), denc_mate, kept=False)
    place_stages(plan, (5,), [0], (0, 0), [(0, 1)])
    place_stages(plan, (0, 1, 2), range(2, 4), (0, 0), FEED_FFN)
    place_stages(plan, (3, 4), range(2), (0, 0), FEED_CROSS)
    (dr, do, dup0, ddown0, dw3, dw7, norms_b), sums = feed_back(
        dh3,
        r3,
        denc,
        r2,
        r1,
        u,
        self_saved[0],
        attn,
        ups,
        downs,
        gains,
        shifts,
        mate,
        later(2, 4, ffn1) + attn_flows(2, [dw8, dw11], [dw9, dw10]) + [mate],
        plan,
        3,
    )
    ffn1, cross = sums[:3], sums[3:]

    plan = {}
    stages = range(bits)
    own = [
        Flow(order, 0, bits, [], (count, share, COLS // 2)) for count in (6, 3, 3) for order in orders[:2]
    ]
    swaps = [Swap(0, (rows, width)) for _ in range(2)]
    total = Total(bits, [norms_a, norms_b])
    for index in reversed(range(3)):
        spots = LAST_OWN[index]
        place_stages(plan, (6 + 2 * index, 7 + 2 * index), stages, spots[0], spots[1:])
    place_stages(plan, (0, 1, 2), stages, (0, 0), LAST_FFN)
    place_stages(plan, (3, 4), range(2, bits), (0, 0), LAST_CROSS)
    place_stages(plan, (14, 15, 16), range(4, bits), (0, 0), LAST_FFN1)
    place_stages(plan, (5,), stages, LAST_NORMS[0], LAST_NORMS[1:])
    place_stages(plan, (13,), [0], (1, 5), [(3, 9)])
    place_stages(plan, (12,), [0], (3, 5), [(3, 9)])
    (data,), sums = attend_back(
        do,
        self_saved,
        mates,
        dr,
        (source, target),
        False,
        attn,
        0,
        ffn_flows(bits, dup0, ddown0, ([dw3], [dw7]))
        + later(2, bits, cross)
        + [total]
        + own
        + swaps
        + later(4, bits, ffn1),
        plan,
        4,
        (own, swaps, total),
    )
    ffn0, cross = sums[:3], sums[3:5]
    norms, *own_sums, source_back, target_back = sums[5:-3]
    ffn1 = sums[-3:]

    everything = slice(None)
    named = [(array, "attn", places, (everything,) * 2) for array, places in zip(cross, ((8, 11), (9, 10)))]
    for index, sums in enumerate((ffn0, ffn1)):
        squares = (3, 7, None) if index == 0 else (None,) * 3
        named += [
            (array, kind, (index, place), None) for array, kind, place in zip(sums, ("up", "down", "both"), squares)
        ]
    for number, array in enumerate(own_sums):
        kind, first = OWN_PARTS[number // 2]
        places, cols = [], []
        for index in range(first, first + array.shape[0]):
            start = index // 3 * COLS + number % 2 * (COLS // 2)
            places.append(4 * kind + index % 3)
            cols.append(slice(start, start + COLS // 2))
        named.append((array, "attn", tuple(places), tuple(cols)))
    grad_source, grad_target, grad_attn, grad_up, grad_down, grad_gains, grad_shifts = finish(
        data, source_back, target_back, norms, named, share, inner, devices
    )
    return decoded, grad_source, grad_target, grad_attn, grad_up, grad_down, grad_gains, grad_shifts


def solution(mesh):
    rows = P(None, AXES, None)
    return jax.shard_map(
        body,
        mesh=mesh,
        in_specs=(rows, rows, rows, P(None, "dp"), P(None, "dp"), P(), P(), P(), P(), P()),
        out_specs=(rows, rows, rows, rows, rows, rows, P(None, AXES), P(None, AXES)),
        check_vma=False,
    )
```
